32 devices in a mesh: grp: 2 (over y), tm: 8 (over z, x), unit: 2 (over core).
Axes of the slice: x: 2, y: 2, z: 4, core: 2. Of those that a mesh axis runs over, the one named last changes fastest.
Arguments:
- panel_data: bfloat16 [1024, 64], P(('grp', 'tm', 'unit')), parts along dimension 0, may hold values from -6 to 6
- cell_mask: int32 [8, 64], P('grp'), parts along dimension 0, may hold values 0 or 1
- loadings: bfloat16 [512, 128], replicated, may hold values from -1 to 1
- noise_prec: float32 [512], replicated, may hold values from 0.5 to 4
- transition: float32 [128, 128], replicated, may hold values from -1 to 1, as said below
- proc_var: float32 [128], replicated, may hold values from 0.00625 to 2
- prior_mean: float32 [128], replicated, may hold values from -6 to 6
Outputs:
- smoothed_mean: float32 [128, 128], P(('grp', 'tm')), parts along dimension 0
- smoothed_var: float32 [128, 128], P(('grp', 'tm')), parts along dimension 0
The draws below stay inside these ranges and needn't reach their ends.
There are 2 independent parts, one for each index of `grp`. The reference program is written for one: setup_inputs(seed, part) draws one part's arguments, and reference() takes and returns one part's arrays. A program takes and returns all parts, laid end to end along the dimension named above; an argument that names none is the same for every part. Nothing has to cross between parts.
Inputs may be any that keep to these rules, and one draw needn't show every extreme that they name: transition is lower triangular with diagonal entries in (0, 1).
All inputs are finite; a program needn't handle non-finite values.
Results may differ from the reference program's by a relative error of at most 0.003.
Values may be sent and summed in bfloat16 or wider, within the bound.
No kernel may reach another device: no remote copies, remote signals or barrier semaphores. Data moves between devices by JAX's collectives and lax.ppermute only.
A program may use at most 128 MiB of HBM per device.

```python
import math
import jax
import jax.numpy as jnp
from jax import lax

K = 128
BLOCK = 128
TIME = 64
UNITS = 512
NB = 4


def decay_rates(key):
    lowest = math.log(1.0 / TIME)
    highest = math.log(1.0 / 20.0)
    spread = jax.random.uniform(jax.random.fold_in(key, 7), (K,), jnp.float32)
    return jnp.exp(lowest + (highest - lowest) * spread)


def draw_transition(key, part):
    factor = jnp.exp(-decay_rates(key))
    noise = jnp.clip(jax.random.normal(jax.random.fold_in(key, 8), (K, K), jnp.float32), -4.0, 4.0)
    below = jnp.tril(jnp.ones((K, K), jnp.float32), -1)
    return (jnp.diag(factor) + below * noise * (0.1 / math.sqrt(K))).astype(jnp.float32)


def draw_proc_var(key, part):
    factor = jnp.exp(-decay_rates(key))
    spread = jax.random.uniform(jax.random.fold_in(key, 9), (K,), jnp.float32, 0.5, 2.0)
    return ((1.0 - factor * factor) * spread).astype(jnp.float32)


def draw_loadings(key, part):
    spread = jax.random.uniform(jax.random.fold_in(key, 11), (K,), jnp.float32)
    column_scale = jnp.exp(math.log(0.01) + (0.0 - math.log(0.01)) * spread)
    noise = jnp.clip(jax.random.normal(jax.random.fold_in(key, 12), (UNITS, K), jnp.float32), -5.0, 5.0)
    return (noise * column_scale[None, :] / math.sqrt(UNITS)).astype(jnp.bfloat16)


def touch_ends(entries, rng, smallest, top_value):
    place = [jax.random.randint(jax.random.fold_in(rng, axis), (), 0, length) for axis, length in enumerate(entries.shape)]
    widest = entries.shape.index(max(entries.shape))
    next_to = place[:widest] + [(place[widest] + 1) % entries.shape[widest]] + place[widest + 1:]
    return entries.at[tuple(place)].set(smallest).at[tuple(next_to)].set(top_value)


def level_of(key, extent, shards, smallest, high):
    level = 1.0
    for dim, parts in shards:
        draws = jax.random.uniform(jax.random.fold_in(jax.random.fold_in(key, 6), dim), (parts,), jnp.float32, smallest / len(shards), high / len(shards))
        level = level * jnp.repeat(jnp.exp(draws), extent[dim] // parts).reshape((-1,) + (1,) * (len(extent) - 1 - dim))
    return level


def gaussian(key, extent, scale, most, pieces=(), kind=jnp.bfloat16):
    drawn = scale * jax.random.normal(key, extent, jnp.float32)
    if pieces:
        drawn = drawn * level_of(key, extent, pieces, -0.22, 0.18)
    return jnp.clip(drawn, -most, most).astype(kind)


def setup_inputs(seed: int = 0, part: int = 0) -> dict:
    keys = jax.random.split(jax.random.key(seed), 8)
    own_keys = jax.random.split(jax.random.fold_in(keys[7], part), 8)
    return {
        "panel_data": gaussian(own_keys[0], (UNITS, TIME), 1.0, 6.0, ((0, 16),)),
        "cell_mask": touch_ends((jax.random.randint(own_keys[1], (NB, TIME), 0, 4) < 3).astype(jnp.int32), jax.random.fold_in(own_keys[1], 1), 0, 1),
        "loadings": draw_loadings(jax.random.fold_in(keys[7], 71), part),
        "noise_prec": jnp.clip(jnp.exp(jax.random.uniform(keys[3], (UNITS,), jnp.float32, math.log(0.5), math.log(4.0))), 0.5, 4.0),
        "transition": draw_transition(jax.random.fold_in(keys[7], 71), part),
        "proc_var": draw_proc_var(jax.random.fold_in(keys[7], 71), part),
        "prior_mean": gaussian(keys[6], (K,), 1.0, 6.0, (), jnp.float32),
    }


HIGHEST = lax.Precision.HIGHEST

def product(left, right):
    return jnp.matmul(left, right, precision=HIGHEST)

def chol_apply(factor, rhs):
    middle = lax.linalg.triangular_solve(factor, rhs, left_side=True, lower=True)
    return lax.linalg.triangular_solve(factor, middle, left_side=True, lower=True, transpose_a=True)

def reference(panel_data, cell_mask, loadings, noise_prec, transition, proc_var, prior_mean):
    identity_mat = jnp.eye(K, dtype=jnp.float32)
    weighted = (noise_prec[:, None] * loadings.astype(jnp.float32)).astype(jnp.bfloat16)
    observed = jnp.repeat(cell_mask.astype(jnp.bfloat16), BLOCK, axis=0)
    masked = observed * panel_data
    info_vec = jnp.dot(masked.T.astype(jnp.float32), weighted.astype(jnp.float32), preferred_element_type=jnp.float32)
    blocks_w = weighted.reshape(UNITS // BLOCK, BLOCK, K).astype(jnp.float32)
    blocks_l = loadings.reshape(UNITS // BLOCK, BLOCK, K).astype(jnp.float32)
    gram = jnp.einsum('bnk,bnl->bkl', blocks_w, blocks_l, precision=HIGHEST)
    info_mat = jnp.einsum('bt,bkl->tkl', cell_mask.astype(jnp.float32), gram, precision=HIGHEST)
    noise_cov = jnp.diag(proc_var)

    def update(pred_mean, pred_cov, info_one, vec_one):
        pred_prec = chol_apply(jnp.linalg.cholesky(pred_cov), identity_mat)
        post_cov = chol_apply(jnp.linalg.cholesky(pred_prec + info_one), identity_mat)
        post_mean = product(post_cov, product(pred_prec, pred_mean) + vec_one)
        return (post_mean, post_cov)
    start_mean, start_cov = update(prior_mean, identity_mat, info_mat[0], info_vec[0])

    def forward(carry, inputs):
        mean_prev, cov_prev = carry
        info_one, vec_one = inputs
        pred_mean = product(transition, mean_prev)
        pred_cov = product(product(transition, cov_prev), transition.T) + noise_cov
        new_mean, new_cov = update(pred_mean, pred_cov, info_one, vec_one)
        return ((new_mean, new_cov), (new_mean, new_cov, pred_mean, pred_cov))
    ends, outputs = lax.scan(forward, (start_mean, start_cov), (info_mat[1:], info_vec[1:]))
    means = jnp.concatenate([start_mean[None], outputs[0]], axis=0)
    covs = jnp.concatenate([start_cov[None], outputs[1]], axis=0)

    def backward(carry, inputs):
        next_mean, next_cov = carry
        mean_now, cov_now, pred_mean, pred_cov = inputs
        gain = chol_apply(jnp.linalg.cholesky(pred_cov), product(transition, cov_now)).T
        new_mean = mean_now + product(gain, next_mean - pred_mean)
        new_cov = cov_now + product(product(gain, next_cov - pred_cov), gain.T)
        return ((new_mean, new_cov), (new_mean, jnp.diagonal(new_cov)))
    finals, smoothed = lax.scan(backward, (means[-1], covs[-1]), (means[:-1], covs[:-1], outputs[2], outputs[3]), reverse=True)
    smoothed_mean = jnp.concatenate([smoothed[0], means[-1][None]], axis=0)
    smoothed_var = jnp.concatenate([smoothed[1], jnp.diagonal(covs[-1])[None]], axis=0)
    return (smoothed_mean, smoothed_var)
```

```python
import functools

import jax
import jax.numpy as jnp
from jax import lax
from jax.experimental import pallas as pl
from jax.experimental.pallas import tpu as pltpu
from jax.sharding import PartitionSpec as P

f32 = jnp.float32
bf16 = jnp.bfloat16
WIDTH = 128
HIGHEST = lax.Precision.HIGHEST
VMEM_LIMIT = 30 << 20
RESIDUAL_MAX = 1e-2
JOIN_BOUNDS = ((1.0, 3.3), (1.0, 3.0), (1.0, 3.3), (1.0, 4.8), (1.0, 7.2), (1.0, 10.5))
COV_BOUNDS = ((0.72, 1.32), (0.51, 1.75), (0.31, 2.50), (0.19, 3.75), (0.13, 4.50), (0.09, 5.00))


def schedule(bounds, goal=2.5e-3):
    low, high = bounds
    alpha, radius, factors = 2.0 / (low + high), (high - low) / (high + low), []
    while radius > goal:
        square = radius * radius
        factors.append(2.0 / (2.0 - square))
        radius = square / (2.0 - square)
    return alpha, factors


def bounds_at(table, level):
    return table[min(level, len(table) - 1)]


def mm(left, right):
    return lax.dot_general(left, right, (((1,), (0,)), ((), ())), preferred_element_type=f32)


def mm_nt(left, right):
    return lax.dot_general(left, right, (((1,), (1,)), ((), ())), preferred_element_type=f32)


def split(value):
    high = value.astype(bf16)
    return high, (value - high.astype(f32)).astype(bf16)


def lanes(*parts):
    return jnp.concatenate(parts, axis=1)


def rows(*parts):
    return jnp.concatenate(parts, axis=0)


def mm3(left, right):
    lh, ll = split(left)
    rh, rl = split(right)
    return mm(lanes(lh, ll), rows(rh, rh)) + mm(lh, rl)


def mm3_nt(left, right):
    lh, ll = split(left)
    rh, rl = split(right)
    return mm_nt(lanes(lh, ll), lanes(rh, rh)) + mm_nt(lh, rl)


def identity():
    shape = (WIDTH, WIDTH)
    return (lax.broadcasted_iota(jnp.int32, shape, 0) == lax.broadcasted_iota(jnp.int32, shape, 1)).astype(f32)


def squares(value):
    return jnp.sum((value * value).reshape(WIDTH // 8, 8, WIDTH), axis=0)


def fast_inverses(mats, eye, bounds, twice=False):
    alpha, factors = schedule(bounds)
    halves = [split(mat) for mat in mats]
    rest = [eye - alpha * mat for mat in mats]
    guess = [(alpha * factors[0]) * (eye + r) for r in rest]
    rest_b = [r.astype(bf16) for r in rest]
    rest = [(1.0 - factors[0]) * eye + factors[0] * mm(r, r) for r in rest_b]
    for number, factor in enumerate(factors[1:]):
        rest_b = [r.astype(bf16) for r in rest]
        guess_b = [g.astype(bf16) for g in guess]
        if number == len(factors) - 2:
            out = [mm(r, g) for r, g in zip(rest_b, guess_b)]
            guess = [factor * (g + o) for g, o in zip(guess, out)]
        else:
            out = [mm(r, lanes(g, r)) for r, g in zip(rest_b, guess_b)]
            guess = [factor * (g + o[:, :WIDTH]) for g, o in zip(guess, out)]
            rest = [(1.0 - factor) * eye + factor * o[:, WIDTH:] for o in out]
    guess_b = [g.astype(bf16) for g in guess]
    resid = [eye - mm(lanes(h, l), rows(g, g)) for (h, l), g in zip(halves, guess_b)]
    guess = [g.astype(f32) + mm(g, e.astype(bf16)) for g, e in zip(guess_b, resid)]
    if twice:
        resid = [eye - mm3(mat, g) for mat, g in zip(mats, guess)]
        guess = [g + mm(g.astype(bf16), e.astype(bf16)) for g, e in zip(guess, resid)]
    return guess, [squares(e) for e in resid]


def safe_inverse(mat, eye):
    size = jnp.max(jnp.sum(jnp.abs(mat), axis=0, keepdims=True), axis=1, keepdims=True)
    product = functools.partial(jnp.dot, precision=HIGHEST, preferred_element_type=f32)

    def unfinished(state):
        step, size, _ = state
        return jnp.logical_and(step < 64, jnp.logical_not(size <= 1e-7))

    def improve(state):
        step, _, guess = state
        resid = eye - product(mat, guess)
        return step + 1, jnp.sum(squares(resid)), guess + product(guess, resid)

    return lax.while_loop(unfinished, improve, (0, f32(jnp.inf), eye / size))[2]


def diagonal(mat, eye):
    return jnp.sum(mat * eye, axis=0, keepdims=True)


def scaled(mat, eye):
    row = 1.0 / diagonal(mat, eye)
    return mat * row, row


def pack(value):
    return lanes(*split(value))


def unpack(value):
    return value[:, :WIDTH].astype(f32) + value[:, WIDTH:].astype(f32)


def path_steps(half, steps, first):
    found = []
    for level in reversed(range(half.bit_length() - 1)):
        stride = 1 << level
        if 2 * stride > steps:
            found.append((level, (first // (2 * stride)) * (2 * stride) + stride - 1))
        else:
            found += [(level, first + (2 * k + 1) * stride - 1) for k in range(steps // (2 * stride))]
    return found


def up_kernel(steps, index_ref, mask_ref, load_ref, prec_ref, trans_ref, var_ref,
              uz_ref, yv_ref, gt_ref, cond_ref, shift_ref, weight_ref, end_ref, message_ref,
              a_ref, c_ref, j_ref, p_ref, gram_ref, base_ref, acc_ref):
    unit, place, n_unit = index_ref[0], index_ref[1], index_ref[2]
    half = uz_ref.shape[0]
    n_levels = half.bit_length() - 1
    n_blocks = load_ref.shape[0] // WIDTH
    eye = identity()
    for block in range(n_blocks):
        load = load_ref[block * WIDTH:(block + 1) * WIDTH, :]
        weighted = (jnp.transpose(load.astype(f32)) * prec_ref[block:block + 1, :]).astype(bf16)
        weight_ref[block] = weighted
        gram = mm(weighted, load)
        gram_ref[block] = 0.5 * (gram + jnp.transpose(gram))
    base_ref[0] = trans_ref[...]
    base_ref[1] = eye * var_ref[...]

    def info(step):
        out = jnp.zeros((WIDTH, WIDTH), f32)
        for block in range(n_blocks):
            out = out + mask_ref[block, step].astype(f32) * gram_ref[block]
        return out

    end_ref[...] = info(n_unit * half - 1)

    def leaves(node):
        step = unit * half + 2 * node
        start = jnp.where(step == 0, 1.0, 0.0).astype(f32)
        trans, noise = base_ref[0], base_ref[1]
        before = info(jnp.maximum(step - 1, 0)) * (1.0 - start)
        first = (trans * (1.0 - start), noise + start * (eye - noise), before)
        return first, (trans, noise, info(step))

    def children(level, node):
        if level == 0:
            return leaves(node)
        at = (2 * node + 1) * (1 << level) - 1
        near = (1 << level) // 2
        return tuple((a_ref[k], c_ref[k], j_ref[k]) for k in (at - near, at + near))

    def join(level, nodes, fast):
        pairs = [children(level, node) for node in nodes]
        mats = [eye + mm3(one[1], two[2]) for one, two in pairs]
        if fast:
            inverses, errors = fast_inverses(mats, eye, bounds_at(JOIN_BOUNDS, level))
            worst = errors[0]
            for error in errors[1:]:
                worst = jnp.maximum(worst, error)
            acc_ref[...] = jnp.maximum(acc_ref[...], worst)
        else:
            inverses = [safe_inverse(mat, eye) for mat in mats]
        us = [mm3(two[0], p) for (one, two), p in zip(pairs, inverses)]
        vs = [mm3(p, one[0]) for (one, two), p in zip(pairs, inverses)]
        azs = [mm3(u, lanes(one[0], one[1])) for u, (one, two) in zip(us, pairs)]
        ys = [mm3(two[2], v) for v, (one, two) in zip(vs, pairs)]
        cs = [two[1] + mm3_nt(az[:, WIDTH:], two[0]) for az, (one, two) in zip(azs, pairs)]
        js = [one[2] + mm3(jnp.transpose(one[0]), y) for y, (one, two) in zip(ys, pairs)]
        for node, p, u, v, az, y, c, j in zip(nodes, inverses, us, vs, azs, ys, cs, js):
            at = (2 * node + 1) * (1 << level) - 1
            uh, ul = split(u)
            zh, zl = split(az[:, WIDTH:])
            uz_ref[at] = rows(lanes(uh, zh), lanes(ul, zl))
            yv_ref[at] = rows(pack(y), pack(v))
            p_ref[at] = p
            a_ref[at] = az[:, :WIDTH]
            c_ref[at] = 0.5 * (c + jnp.transpose(c))
            j_ref[at] = 0.5 * (j + jnp.transpose(j))

    path = path_steps(half, steps, place * steps)

    def condition(entries, fast):
        level = entries[0][1]
        mats, scales = zip(*[scaled(c_ref[at], eye) for _, _, at in entries])
        if fast:
            inverses, errors = fast_inverses(mats, eye, bounds_at(COV_BOUNDS, level), level > 1)
            worst = errors[0]
            for error in errors[1:]:
                worst = jnp.maximum(worst, error)
            acc_ref[...] = jnp.maximum(acc_ref[...], worst)
        else:
            inverses = [safe_inverse(mat, eye) for mat in mats]
        for (slot, level, at), inverse, scale in zip(entries, inverses, scales):
            uz = uz_ref[at]
            z = uz[:WIDTH, WIDTH:].astype(f32) + uz[WIDTH:, WIDTH:].astype(f32)
            v = unpack(yv_ref[at, WIDTH:, :])
            back = mm3(jnp.transpose(inverse) * scale, z)
            forth = jnp.transpose(back)
            if level == 0:
                start = jnp.where(unit * half + at == 0, 1.0, 0.0).astype(f32)
                first = base_ref[1] + start * (eye - base_ref[1])
            else:
                first = c_ref[at - (1 << level) // 2]
            p = p_ref[at]
            kept = mm3(p, first)
            gain = v - mm3(forth, a_ref[at])
            gt_ref[slot] = pack(rows(jnp.transpose(gain), back))
            cond = kept - mm3(forth, z)
            cond_ref[slot] = 0.5 * (cond + jnp.transpose(cond))
            shift_ref[slot] = pack(rows(jnp.transpose(p), jnp.transpose(kept), -back))

    def sweep(fast):
        for level in range(n_levels):
            count = half >> (level + 1)
            group = min(count, 4) if fast else 1

            def some(block, carry):
                join(level, [block * group + k for k in range(group)], fast)
                return carry

            lax.fori_loop(0, count // group, some, 0)
        entries = [(slot, level, at) for slot, (level, at) in enumerate(path)]
        for level in reversed(range(n_levels)):
            some = [entry for entry in entries if entry[1] == level]
            if fast:
                condition(some, True)
            else:
                for entry in some:
                    condition([entry], False)
        top = half // 2 - 1
        message_ref[0] = a_ref[top]
        message_ref[1] = c_ref[top]
        message_ref[2] = j_ref[top]

    acc_ref[...] = jnp.zeros((8, WIDTH), f32)
    sweep(True)
    worst = jnp.sum(acc_ref[...])

    @pl.when(jnp.logical_not(worst <= RESIDUAL_MAX))
    def _():
        sweep(False)


SMEM = pl.BlockSpec(memory_space=pltpu.SMEM)
VMEM = pl.BlockSpec(memory_space=pltpu.VMEM)


def up_sweep(index, cell_mask, loadings, prec_rows, transition, var_row, half, steps):
    n_blocks = loadings.shape[0] // WIDTH
    mat = (WIDTH, WIDTH)
    wide = (2 * WIDTH, 2 * WIDTH)
    n_path = len(path_steps(half, steps, 0))
    return pl.pallas_call(
        functools.partial(up_kernel, steps),
        out_shape=(
            jax.ShapeDtypeStruct((half,) + wide, bf16),
            jax.ShapeDtypeStruct((half,) + wide, bf16),
            jax.ShapeDtypeStruct((n_path,) + wide, bf16),
            jax.ShapeDtypeStruct((n_path,) + mat, f32),
            jax.ShapeDtypeStruct((n_path, 3 * WIDTH, 2 * WIDTH), bf16),
            jax.ShapeDtypeStruct((n_blocks,) + mat, bf16),
            jax.ShapeDtypeStruct(mat, f32),
            jax.ShapeDtypeStruct((3,) + mat, f32),
        ),
        in_specs=[SMEM, SMEM] + [VMEM] * 4,
        out_specs=(VMEM,) * 8,
        scratch_shapes=[
            pltpu.VMEM((half,) + mat, f32),
            pltpu.VMEM((half,) + mat, f32),
            pltpu.VMEM((half,) + mat, f32),
            pltpu.VMEM((half,) + mat, f32),
            pltpu.VMEM((n_blocks,) + mat, f32),
            pltpu.VMEM((2,) + mat, f32),
            pltpu.VMEM((8, WIDTH), f32),
        ],
        compiler_params=pltpu.CompilerParams(vmem_limit_bytes=VMEM_LIMIT),
        cost_estimate=pl.CostEstimate(flops=half * 600 * WIDTH**3, transcendentals=0, bytes_accessed=32 << 20),
        name="up_sweep",
    )(index, cell_mask, loadings, prec_rows, transition, var_row)


def vector_kernel(index_ref, mask_ref, weight_ref, prior_ref, uz_ref, yv_ref, *refs):
    *pair_refs, leaf_ref, b_ref, e_ref, message_ref, all_ref, panel_ref = refs
    unit, place = index_ref[0], index_ref[3]
    half = uz_ref.shape[0]
    total = panel_ref.shape[1]
    n_blocks = weight_ref.shape[0]
    n_time = len(pair_refs)
    rows_own = pair_refs[0].shape[0] // 2
    for shift, pair_ref in enumerate(pair_refs):
        source = lax.rem(place + (n_time - shift), n_time)
        for k, own in enumerate((unit, 1 - unit)):
            at = pl.multiple_of((2 * source + own) * rows_own, rows_own)
            panel_ref[pl.ds(at, rows_own), :] = pair_ref[k * rows_own:(k + 1) * rows_own, :]
    turned = jnp.zeros((WIDTH, total), f32)
    for block in range(n_blocks):
        mask = mask_ref[block:block + 1, :].astype(bf16)
        turned = turned + mm(weight_ref[block], mask * panel_ref[block * WIDTH:(block + 1) * WIDTH, :])
    late = pltpu.roll(jnp.transpose(turned), 1, 0)
    end = late[0:1, :]
    all_ref[...] = late
    all_ref[0:1, :] = jnp.zeros((1, WIDTH), f32)
    leaf_ref[...] = all_ref[pl.ds(pl.multiple_of(unit * half, half), half), :]
    prior = jnp.where(unit == 0, 1.0, 0.0) * prior_ref[...]
    zero = jnp.zeros((1, WIDTH), f32)
    for level in range(half.bit_length() - 1):
        stride = 1 << level
        for node in range(half >> (level + 1)):
            at = (2 * node + 1) * stride - 1
            if level == 0:
                b1, b2 = (prior if node == 0 else zero), zero
                e1, e2 = leaf_ref[at:at + 1, :], leaf_ref[at + 1:at + 2, :]
            else:
                one, two = at - stride // 2, at + stride // 2
                b1, b2 = b_ref[one:one + 1, :], b_ref[two:two + 1, :]
                e1, e2 = e_ref[one:one + 1, :], e_ref[two:two + 1, :]
            high, low = split(lanes(b1, e2))
            out = mm_nt(rows(high, low), uz_ref[at])
            b_ref[at:at + 1, :] = b2 + out[0:1, :WIDTH] + out[1:2, :WIDTH] + out[0:1, WIDTH:]
            high, low = split(lanes(-b1, e2))
            out = mm(rows(high, low), yv_ref[at])
            e_ref[at:at + 1, :] = e1 + out[0:1, :WIDTH] + out[1:2, :WIDTH] + out[0:1, WIDTH:]
    top = half // 2 - 1
    message_ref[...] = rows(b_ref[top:top + 1, :], e_ref[top:top + 1, :], end, jnp.zeros((5, WIDTH), f32))


def vector_sweep(index, pairs, cell_mask, weighted, prior_row, uz, yv):
    total = pairs[0].shape[1]
    half = uz.shape[0]
    row = jax.ShapeDtypeStruct((half, WIDTH), f32)
    return pl.pallas_call(
        vector_kernel,
        out_shape=(row, row, row, jax.ShapeDtypeStruct((8, WIDTH), f32)),
        in_specs=[SMEM] + [VMEM] * (5 + len(pairs)),
        out_specs=(VMEM,) * 4,
        scratch_shapes=[
            pltpu.VMEM((total, WIDTH), f32),
            pltpu.VMEM((len(pairs) * pairs[0].shape[0], total), bf16),
        ],
        compiler_params=pltpu.CompilerParams(vmem_limit_bytes=VMEM_LIMIT),
        name="vector_sweep",
    )(index, cell_mask, weighted, prior_row, uz, yv, *pairs)


def down_kernel(steps, index_ref, own_ref, other_ref, end_ref, vown_ref, vother_ref, prior_ref, leaf_ref, b_ref, e_ref,
                gt_ref, cond_ref, shift_ref, out_ref, acc_ref, top_ref):
    unit, place = index_ref[0], index_ref[1]
    half = leaf_ref.shape[0]
    n_levels = half.bit_length() - 1
    eye = identity()
    flag = jnp.where(unit == 0, 1.0, 0.0).astype(f32)

    def pick(zero, one):
        return flag * zero + (1.0 - flag) * one

    cov0 = pick(own_ref[1], other_ref[1])
    trans1, cov1, info1 = [pick(other_ref[k], own_ref[k]) for k in range(3)]
    b0 = pick(vown_ref[0:1, :], vother_ref[0:1, :])
    b1, e1 = [pick(vother_ref[k:k + 1, :], vown_ref[k:k + 1, :]) for k in range(2)]
    e_end = vown_ref[2:3, :]
    end = end_ref[...]

    def roots(fast):
        mat = eye + mm3(cov0, info1)
        if fast:
            (p,), (error,) = fast_inverses([mat], eye, bounds_at(JOIN_BOUNDS, n_levels))
        else:
            p = safe_inverse(mat, eye)
        kept = mm3(p, cov0)
        z = mm3(trans1, kept)
        cov = cov1 + mm3_nt(z, trans1)
        cov = 0.5 * (cov + jnp.transpose(cov))
        mat, scale = scaled(cov, eye)
        last = eye + mm3(cov, end)
        if fast:
            (inverse,), (error2,) = fast_inverses([mat], eye, bounds_at(COV_BOUNDS, n_levels), True)
            (p_end,), (error3,) = fast_inverses([last], eye, bounds_at(JOIN_BOUNDS, 0))
            acc_ref[...] = jnp.maximum(error, jnp.maximum(error2, error3))
        else:
            inverse = safe_inverse(mat, eye)
            p_end = safe_inverse(last, eye)
        top_ref[0], top_ref[1], top_ref[2], top_ref[3] = p, kept, z, cov
        top_ref[4], top_ref[5] = jnp.transpose(inverse) * scale, p_end

    roots(True)
    worst = jnp.sum(acc_ref[...])

    @pl.when(jnp.logical_not(worst <= RESIDUAL_MAX))
    def _():
        roots(False)

    p, kept, z, cov, inverse, p_end = [top_ref[k] for k in range(6)]
    back = mm3(inverse, z)
    forth = jnp.transpose(back)
    mean_mid = mm3_nt(b0 + mm3(e1, cov0), p)
    b_end = mm3_nt(mean_mid, trans1) + b1
    mean_top = mm3_nt(b_end + mm3(e_end, cov), p_end)
    mean_mid = mean_mid + mm3(mean_top - b_end, back)
    cov_top = mm3(p_end, cov)
    cov_top = 0.5 * (cov_top + jnp.transpose(cov_top))
    cov_cross = mm3(cov_top, back)
    cov_mid = kept - mm3(forth, z) + mm3(forth, cov_cross)
    keep = 1.0 - flag
    joint = rows(
        lanes(keep * cov_mid, keep * jnp.transpose(cov_cross)),
        lanes(keep * cov_cross, pick(cov_mid, cov_top)),
    )
    means = lanes(keep * mean_mid, pick(mean_mid, mean_top))
    prior = flag * prior_ref[...]
    first = place * steps
    path = path_steps(half, steps, first)

    def shift(slot):
        level, at = path[slot]
        row_of = lambda ref, k: ref[pl.ds(k, 1), :]
        if level == 0:
            one, two = jnp.where(at == 0, 1.0, 0.0) * prior, row_of(leaf_ref, at + 1)
        else:
            near = (1 << level) // 2
            one, two = row_of(b_ref, at - near), row_of(e_ref, at + near)
        high, low = split(lanes(one, two, row_of(b_ref, at)))
        out = mm(rows(high, low), shift_ref[slot])
        return out[0:1, :WIDTH] + out[1:2, :WIDTH] + out[0:1, WIDTH:]

    shifts = [shift(slot) for slot in range(len(path))]

    def node(slot, joint, means, leaf):
        packed = gt_ref[slot]
        gh, gl = packed[:, :WIDTH], packed[:, WIDTH:]
        jh, jl = split(joint)
        cross = mm(lanes(jh, jl), rows(gh, gh)) + mm(jh, gl)
        high, low = split(means)
        out = mm(rows(high, low), packed)
        mean = shifts[slot] + out[0:1, :WIDTH] + out[1:2, :WIDTH] + out[0:1, WIDTH:]
        gain = unpack(packed)
        if leaf:
            own = diagonal(cond_ref[slot], eye) + jnp.sum(gain * cross, axis=0, keepdims=True)
        else:
            own = cond_ref[slot] + mm3(jnp.transpose(gain), cross)
        return mean, own, cross

    def left_pair(joint, means, mean, own, cross):
        c = cross[:WIDTH]
        return rows(lanes(joint[:WIDTH, :WIDTH], c), lanes(jnp.transpose(c), own)), lanes(means[:, :WIDTH], mean)

    def right_pair(joint, means, mean, own, cross):
        c = cross[WIDTH:]
        return rows(lanes(own, jnp.transpose(c)), lanes(c, joint[WIDTH:, WIDTH:])), lanes(mean, means[:, WIDTH:])

    slot = 0
    while path[slot][0] >= steps.bit_length() - 1:
        result = node(slot, joint, means, False)
        go_right = jnp.where(first > path[slot][1], 1.0, 0.0).astype(f32)
        lj, lm = left_pair(joint, means, *result)
        rj, rm = right_pair(joint, means, *result)
        joint = go_right * rj + (1.0 - go_right) * lj
        means = go_right * rm + (1.0 - go_right) * lm
        slot += 1

    out_ref[steps - 1:steps, :] = means[:, WIDTH:]
    out_ref[2 * steps - 1:2 * steps, :] = diagonal(joint[WIDTH:, WIDTH:], eye)
    todo = [(0, steps, joint, means)]
    while todo:
        later = []
        for low, count, joint, means in todo:
            stride = count // 2
            at = low + stride - 1
            result = node(slot, joint, means, stride == 1)
            slot += 1
            out_ref[at:at + 1, :] = result[0]
            if stride == 1:
                out_ref[steps + at:steps + at + 1, :] = result[1]
                continue
            out_ref[steps + at:steps + at + 1, :] = diagonal(result[1], eye)
            later.append((low, stride) + left_pair(joint, means, *result))
            later.append((low + stride, stride) + right_pair(joint, means, *result))
        todo = later


def down_sweep(index, own, other, end, vown, vother, prior_row, leaves, bs, es, gains, conds, shifts, steps):
    return pl.pallas_call(
        functools.partial(down_kernel, steps),
        out_shape=jax.ShapeDtypeStruct((2 * steps, WIDTH), f32),
        in_specs=[SMEM] + [VMEM] * 12,
        out_specs=VMEM,
        scratch_shapes=[pltpu.VMEM((8, WIDTH), f32), pltpu.VMEM((6, WIDTH, WIDTH), f32)],
        compiler_params=pltpu.CompilerParams(vmem_limit_bytes=VMEM_LIMIT),
        name="down_sweep",
    )(index, own, other, end, vown, vother, prior_row, leaves, bs, es, gains, conds, shifts)


def redundant(panel_data, cell_mask, loadings, noise_prec, transition, proc_var, prior_mean):
    n_time = lax.axis_size("tm")
    n_unit = lax.axis_size("unit")
    place, unit = lax.axis_index("tm"), lax.axis_index("unit")
    total = panel_data.shape[1]
    half = total // n_unit
    steps = total // n_time
    per_half = half // steps
    index = jnp.stack([unit, place % per_half, n_unit, place]).astype(jnp.int32)
    swap = [(0, 1), (1, 0)]
    pair = jnp.concatenate([panel_data, lax.ppermute(panel_data, "unit", swap)])
    transition, pair = lax.optimization_barrier((transition, pair))
    pairs = [pair] + [
        lax.ppermute(pair, "tm", [(k, (k + shift) % n_time) for k in range(n_time)]) for shift in range(1, n_time)
    ]
    prior_row = prior_mean.reshape(1, WIDTH)
    uz, yv, gains, conds, shifts, weighted, end, message = up_sweep(
        index, cell_mask, loadings, noise_prec.reshape(-1, WIDTH), transition, proc_var.reshape(1, WIDTH), half, steps
    )
    other = lax.ppermute(message, "unit", swap)
    leaves, bs, es, vmessage = vector_sweep(index, pairs, cell_mask, weighted, prior_row, uz, yv)
    vother = lax.ppermute(vmessage, "unit", swap)
    mine = down_sweep(
        index, message, other, end, vmessage, vother, prior_row, leaves, bs, es, gains, conds, shifts, steps
    )
    theirs = lax.ppermute(mine, "unit", swap)
    out = jnp.where(unit == place // per_half, mine, theirs)
    return out[:steps], out[steps:]


BLOCK = 128


def carried_in(value, axis, join, neutral, backward):
    count, mine = (lax.axis_size(axis), lax.axis_index(axis))
    pieces = jax.tree.map(lambda part: lax.all_gather(part, axis), value)
    if backward:
        pieces = jax.tree.map(lambda part: part[::-1], pieces)
        mine = count - 1 - mine
    running = jax.tree.map(
        lambda part, zero: jnp.full_like(part, 0) + jnp.asarray(zero, part.dtype), value, neutral
    )

    def step(position, running):
        longer = join(running, jax.tree.map(lambda part: part[position], pieces))
        return jax.tree.map(lambda new, old: jnp.where(position < mine, new, old), longer, running)

    return lax.fori_loop(0, count - 1, step, running)


def product(left, right):
    return jnp.matmul(left, right, precision=HIGHEST)


def mat_vec(matrix, vector):
    return jnp.einsum("...kl,...l->...k", matrix, vector, precision=HIGHEST)


def flipped(matrix):
    return jnp.swapaxes(matrix, -1, -2)


def chol_apply(factor, rhs):
    middle = lax.linalg.triangular_solve(factor, rhs, left_side=True, lower=True)
    return lax.linalg.triangular_solve(factor, middle, left_side=True, lower=True, transpose_a=True)


def filter_join(earlier, later):
    trans_one, shift_one, cov_one, info_one, vec_one, live_one = earlier
    trans_two, shift_two, cov_two, info_two, vec_two, live_two = later
    identity_mat = jnp.eye(trans_one.shape[-1], dtype=jnp.float32)
    live_mat = live_one[..., None, None]
    factor_one = jnp.linalg.cholesky(cov_one + (1.0 - live_mat) * identity_mat)
    inner_mat = identity_mat + product(product(flipped(factor_one), info_two), factor_one)
    inner_factor = jnp.linalg.cholesky(inner_mat)
    solved = lax.linalg.triangular_solve(
        inner_factor, flipped(factor_one), left_side=True, lower=True
    )
    spread_mat = product(trans_two, flipped(solved))
    pushed = product(info_two, trans_one)
    reduced = product(solved, pushed)
    residue = vec_two - mat_vec(info_two, shift_one)
    solved_residue = mat_vec(solved, residue)
    trans_new = product(trans_two, trans_one) - product(spread_mat, reduced)
    shift_new = mat_vec(trans_two, shift_one) + mat_vec(spread_mat, solved_residue) + shift_two
    cov_new = product(spread_mat, flipped(spread_mat)) + cov_two
    info_new = product(flipped(trans_one), pushed) - product(flipped(reduced), reduced) + info_one
    vec_new = (
        mat_vec(flipped(trans_one), residue) - mat_vec(flipped(reduced), solved_residue) + vec_one
    )
    alive_mat = live_mat > 0.5
    alive_vec = live_one[..., None] > 0.5
    return (
        jnp.where(alive_mat, trans_new, trans_two),
        jnp.where(alive_vec, shift_new, shift_two),
        jnp.where(alive_mat, cov_new, cov_two),
        jnp.where(alive_mat, info_new, info_two),
        jnp.where(alive_vec, vec_new, vec_two),
        jnp.maximum(live_one, live_two),
    )


def smooth_join(lower_elem, higher_elem):
    gain_low, offset_low, cov_low = lower_elem
    gain_high, offset_high, cov_high = higher_elem
    return (
        product(gain_low, gain_high),
        mat_vec(gain_low, offset_high) + offset_low,
        product(product(gain_low, cov_high), flipped(gain_low)) + cov_low,
    )


def smooth_scan_join(earlier, later):
    return smooth_join(later, earlier)


def take_last(stacked):
    return stacked[-1]


def take_first(stacked):
    return stacked[0]


def per_device(panel_data, cell_mask, loadings, noise_prec, transition, proc_var, prior_mean):
    n_time = lax.axis_size("tm")
    n_unit = lax.axis_size("unit")
    time_index = lax.axis_index("tm")
    unit_index = lax.axis_index("unit")
    rows_own, total_time = panel_data.shape
    steps = total_time // n_time
    width = transition.shape[0]
    identity_mat = jnp.eye(width, dtype=jnp.float32)
    my_columns = lax.dynamic_slice_in_dim(cell_mask, time_index * steps, steps, 1)
    half_load = lax.dynamic_index_in_dim(
        loadings.reshape(n_time, n_unit, rows_own, width), unit_index, 1, keepdims=False
    ).reshape(n_time * rows_own, width)
    half_prec = lax.dynamic_index_in_dim(
        noise_prec.reshape(n_time, n_unit, rows_own), unit_index, 1, keepdims=False
    ).reshape(n_time * rows_own)
    half_ids = (
        (jnp.arange(n_time, dtype=jnp.int32)[:, None] * n_unit + unit_index) * rows_own
        + jnp.arange(rows_own, dtype=jnp.int32)[None, :]
    ).reshape(-1)
    half_weighted = (half_prec[:, None] * half_load.astype(jnp.float32)).astype(jnp.bfloat16)
    half_mask = jnp.take(my_columns, half_ids // BLOCK, axis=0).astype(jnp.bfloat16)
    regrouped = lax.all_to_all(panel_data, "tm", split_axis=1, concat_axis=0, tiled=True)
    vec_half = jnp.dot((half_mask * regrouped).T, half_weighted, preferred_element_type=jnp.float32)
    group_rows = min(rows_own, BLOCK)
    n_groups = n_time * rows_own // group_rows
    group_gram = jnp.einsum(
        "gnk,gnl->gkl",
        half_weighted.reshape(n_groups, group_rows, width),
        half_load.reshape(n_groups, group_rows, width),
        preferred_element_type=jnp.float32,
    )
    group_block = half_ids.reshape(n_groups, group_rows)[:, 0] // BLOCK
    group_mask = jnp.take(my_columns, group_block, axis=0).astype(jnp.float32)
    info_half = jnp.einsum("gt,gkl->tkl", group_mask, group_gram, precision=HIGHEST)
    info_mat, info_vec = lax.psum((info_half, vec_half), "unit")
    global_step = time_index * steps + jnp.arange(steps, dtype=jnp.int32)
    first_step = (global_step == 0).astype(jnp.float32)
    keep_step = 1.0 - first_step
    last_keep = 1.0 - (global_step == total_time - 1).astype(jnp.float32)
    inv_var = 1.0 / proc_var
    prior_prec = first_step[:, None, None] * identity_mat + keep_step[:, None, None] * jnp.diag(
        inv_var
    )
    eyes = jnp.broadcast_to(identity_mat, info_mat.shape)
    post_cov = chol_apply(jnp.linalg.cholesky(prior_prec + info_mat), eyes)
    shift_vec = jnp.einsum(
        "skl,sl->sk",
        post_cov,
        info_vec + first_step[:, None] * prior_mean[None, :],
        precision=HIGHEST,
    )
    scaled_trans = inv_var[:, None] * transition
    trans_part = keep_step[:, None, None] * jnp.einsum(
        "skl,lm->skm", post_cov, scaled_trans, precision=HIGHEST
    )
    middle = jnp.diag(inv_var)[None] - inv_var[None, :, None] * post_cov * inv_var[None, None, :]
    pressed = jnp.einsum("slm,mn->sln", middle, transition, precision=HIGHEST)
    info_part = keep_step[:, None, None] * jnp.einsum(
        "lk,sln->skn", transition, pressed, precision=HIGHEST
    )
    vec_part = keep_step[:, None] * jnp.einsum(
        "lk,sl->sk", transition, inv_var[None, :] * shift_vec, precision=HIGHEST
    )
    elements = (
        trans_part,
        shift_vec,
        post_cov,
        info_part,
        vec_part,
        jnp.ones((steps,), jnp.float32),
    )
    zero_vec = jnp.zeros((width,), jnp.float32)
    zero_mat = jnp.zeros((width, width), jnp.float32)
    filter_identity = (identity_mat, zero_vec, zero_mat, zero_mat, zero_vec, jnp.float32(0.0))
    local_joined = lax.associative_scan(filter_join, elements)
    filter_total = jax.tree.map(take_last, local_joined)
    before = carried_in(filter_total, "tm", filter_join, filter_identity, False)
    filtered = jax.vmap(filter_join, in_axes=(None, 0))(before, local_joined)
    filt_mean = filtered[1]
    filt_cov = filtered[2]
    moved_cov = jnp.einsum("kl,slm->skm", transition, filt_cov, precision=HIGHEST)
    pred_next = (
        jnp.einsum("skm,nm->skn", moved_cov, transition, precision=HIGHEST)
        + jnp.diag(proc_var)[None]
    )
    gain = (
        jnp.transpose(chol_apply(jnp.linalg.cholesky(pred_next), moved_cov), (0, 2, 1))
        * last_keep[:, None, None]
    )
    moved_mean = jnp.einsum("kl,sl->sk", transition, filt_mean, precision=HIGHEST)
    offset = filt_mean - jnp.einsum("skl,sl->sk", gain, moved_mean, precision=HIGHEST)
    resid_cov = filt_cov - jnp.einsum("skl,slm->skm", gain, moved_cov, precision=HIGHEST)
    smooth_identity = (identity_mat, zero_vec, zero_mat)
    local_suffix = lax.associative_scan(smooth_scan_join, (gain, offset, resid_cov), reverse=True)
    smooth_total = jax.tree.map(take_first, local_suffix)
    after = carried_in(smooth_total, "tm", smooth_scan_join, smooth_identity, True)
    smoothed = jax.vmap(smooth_join, in_axes=(0, None))(local_suffix, after)
    smoothed_mean = smoothed[1]
    smoothed_var = jnp.diagonal(smoothed[2], axis1=1, axis2=2)
    return (smoothed_mean, smoothed_var)


def per_device_any(*arrays):
    fits = arrays[0].shape[1] <= 64 * lax.axis_size("unit") and lax.axis_size("unit") == 2
    return redundant(*arrays) if fits else per_device(*arrays)


def solution(mesh):
    return jax.shard_map(
        per_device_any,
        mesh=mesh,
        in_specs=(P(("grp", "tm", "unit"), None), P("grp", None), P(), P(), P(), P(), P()),
        out_specs=(P(("grp", "tm"), None), P(("grp", "tm"), None)),
        check_vma=False,
    )
```

```python
import functools

import jax
import jax.numpy as jnp
from jax import lax
from jax.experimental import pallas as pl
from jax.experimental.pallas import tpu as pltpu
from jax.sharding import PartitionSpec as P

f32 = jnp.float32
bf16 = jnp.bfloat16
WIDTH = 128
HIGHEST = lax.Precision.HIGHEST
VMEM_LIMIT = 30 << 20
RESIDUAL_MAX = 1e-2
GROUP = 8
JOIN_BOUNDS = ((1.0, 3.3), (1.0, 3.0), (1.0, 3.3), (1.0, 4.8), (1.0, 7.2), (1.0, 10.5))
COV_BOUNDS = ((0.72, 1.32), (0.51, 1.75), (0.31, 2.50), (0.19, 3.75), (0.13, 4.50), (0.09, 5.00))


def schedule(bounds, goal=2.5e-3):
    low, high = bounds
    alpha, radius, factors = 2.0 / (low + high), (high - low) / (high + low), []
    while radius > goal:
        square = radius * radius
        factors.append(2.0 / (2.0 - square))
        radius = square / (2.0 - square)
    return alpha, factors


def bounds_at(table, level):
    return table[min(level, len(table) - 1)]


def mm(left, right):
    return lax.dot_general(left, right, (((1,), (0,)), ((), ())), preferred_element_type=f32)


def mm_nt(left, right):
    return lax.dot_general(left, right, (((1,), (1,)), ((), ())), preferred_element_type=f32)


def split(value):
    high = value.astype(bf16)
    return high, (value - high.astype(f32)).astype(bf16)


def lanes(*parts):
    return jnp.concatenate(parts, axis=1)


def rows(*parts):
    return jnp.concatenate(parts, axis=0)


def mm3(left, right):
    lh, ll = split(left)
    rh, rl = split(right)
    return mm(lanes(lh, ll), rows(rh, rh)) + mm(lh, rl)


def mm3_nt(left, right):
    lh, ll = split(left)
    rh, rl = split(right)
    return mm_nt(lanes(lh, ll), lanes(rh, rh)) + mm_nt(lh, rl)


def identity():
    shape = (WIDTH, WIDTH)
    return (lax.broadcasted_iota(jnp.int32, shape, 0) == lax.broadcasted_iota(jnp.int32, shape, 1)).astype(f32)


def squares(value):
    return jnp.sum((value * value).reshape(WIDTH // 8, 8, WIDTH), axis=0)


def fast_inverses(items, eye):
    mats = [mat for mat, _, _ in items]
    plans = [schedule(bounds) for _, bounds, _ in items]
    n = range(len(items))
    halves = [split(mat) for mat in mats]
    rest = [eye - plan[0] * mat for plan, mat in zip(plans, mats)]
    guess = [(plan[0] * plan[1][0]) * (eye + r) for plan, r in zip(plans, rest)]
    for step in range(max(len(factors) for _, factors in plans)):
        rest_b = [r.astype(bf16) for r in rest]
        guess_b = [g.astype(bf16) for g in guess]
        for k in n:
            factors = plans[k][1]
            more = step + 1 < len(factors)
            if step >= len(factors):
                continue
            factor = factors[step]
            if step == 0:
                if more:
                    rest[k] = (1.0 - factor) * eye + factor * mm(rest_b[k], rest_b[k])
            elif more:
                out = mm(rest_b[k], lanes(guess_b[k], rest_b[k]))
                guess[k] = factor * (guess[k] + out[:, :WIDTH])
                rest[k] = (1.0 - factor) * eye + factor * out[:, WIDTH:]
            else:
                guess[k] = factor * (guess[k] + mm(rest_b[k], guess_b[k]))
    guess_b = [g.astype(bf16) for g in guess]
    resid = [eye - mm(lanes(h, l), rows(g, g)) for (h, l), g in zip(halves, guess_b)]
    guess = [g.astype(f32) + mm(g, e.astype(bf16)) for g, e in zip(guess_b, resid)]
    again = [k for k in n if items[k][2]]
    fine = {k: eye - mm3(mats[k], guess[k]) for k in again}
    for k in again:
        resid[k] = fine[k]
        guess[k] = guess[k] + mm(guess[k].astype(bf16), fine[k].astype(bf16))
    worst = squares(resid[0])
    for e in resid[1:]:
        worst = jnp.maximum(worst, squares(e))
    return guess, worst


def safe_inverse(mat, eye):
    size = jnp.max(jnp.sum(jnp.abs(mat), axis=0, keepdims=True), axis=1, keepdims=True)
    product = functools.partial(jnp.dot, precision=HIGHEST, preferred_element_type=f32)

    def unfinished(state):
        step, size, _ = state
        return jnp.logical_and(step < 64, jnp.logical_not(size <= 1e-7))

    def improve(state):
        step, _, guess = state
        resid = eye - product(mat, guess)
        return step + 1, jnp.sum(squares(resid)), guess + product(guess, resid)

    return lax.while_loop(unfinished, improve, (0, f32(jnp.inf), eye / size))[2]


def diagonal(mat, eye):
    return jnp.sum(mat * eye, axis=0, keepdims=True)


def scaled(mat, eye):
    row = 1.0 / diagonal(mat, eye)
    return mat * row, row


def pack(value):
    return lanes(*split(value))


def unpack(value):
    return value[:, :WIDTH].astype(f32) + value[:, WIDTH:].astype(f32)


def path_steps(half, steps, first):
    found = []
    for level in reversed(range(half.bit_length() - 1)):
        stride = 1 << level
        if 2 * stride > steps:
            found.append((level, (first // (2 * stride)) * (2 * stride) + stride - 1))
        else:
            found += [(level, first + (2 * k + 1) * stride - 1) for k in range(steps // (2 * stride))]
    return found


def join_item(level, pair, eye):
    (_, c1, _), (_, _, j2) = pair
    return eye + mm3(c1, j2), bounds_at(JOIN_BOUNDS, level), False


def joined(level, pairs, inverses, eye, turned=None):
    if level < 2:
        less = [(eye - p).astype(bf16) for p in inverses]
        us = [two[0] - mm(two[0].astype(bf16), d) for (one, two), d in zip(pairs, less)]
        vs = [one[0] - mm(d, one[0].astype(bf16)) for (one, two), d in zip(pairs, less)]
    else:
        us = [mm3(two[0], p) for (one, two), p in zip(pairs, inverses)]
        vs = [mm3(p, one[0]) for (one, two), p in zip(pairs, inverses)]
    if turned is None:
        turned = [jnp.transpose(one[0]) for one, two in pairs]
    ts = [mm3(two[0], v) for v, (one, two) in zip(vs, pairs)]
    zs = [mm3(u, one[1]) for u, (one, two) in zip(us, pairs)]
    ys = [mm3(two[2], v) for v, (one, two) in zip(vs, pairs)]
    cs = [two[1] + mm3_nt(z, two[0]) for z, (one, two) in zip(zs, pairs)]
    js = [one[2] + mm3(t, y) for t, y, (one, two) in zip(turned, ys, pairs)]
    return list(zip(us, vs, ts, zs, ys, cs, js))


def condition_item(level, entry, eye):
    mat, scale = scaled(entry["c"], eye)
    return (mat, bounds_at(COV_BOUNDS, level), level > 2), scale


def conditioned(entries, scales, inverses):
    zs, vs = [e["z"] for e in entries], [e["v"] for e in entries]
    backs = [mm3(jnp.transpose(inverse) * scale, z) for inverse, scale, z in zip(inverses, scales, zs)]
    kepts = [mm3(e["p"], e["c1"]) for e in entries]
    forths = [jnp.transpose(back) for back in backs]
    gains = [v - mm3(forth, e["a"]) for v, forth, e in zip(vs, forths, entries)]
    conds = [kept - mm3(forth, z) for kept, forth, z in zip(kepts, forths, zs)]
    return [
        (
            pack(rows(jnp.transpose(gain), back)),
            cond,
            pack(rows(jnp.transpose(e["p"]), jnp.transpose(kept), -back)),
        )
        for e, gain, back, cond, kept in zip(entries, gains, backs, conds, kepts)
    ]


def level_entry(refs, level, node, c1):
    uz_ref, yv_ref, a_ref, c_ref, _, p_ref = refs
    uz = uz_ref[node]
    return dict(
        z=uz[:WIDTH, WIDTH:].astype(f32) + uz[WIDTH:, WIDTH:].astype(f32),
        v=unpack(yv_ref[node, WIDTH:, :]),
        a=a_ref[node],
        c=c_ref[node],
        p=p_ref[node],
        c1=c1,
    )


LEVEL_ARRAYS = 6


def first_kernel(half, index_ref, mask_hbm, load_hbm, prec_hbm, trans_hbm, var_hbm, prior_hbm,
                 weight_ref, end_ref, mask_out, const_ref, uz_ref, yv_ref, a_ref, c_ref, j_ref, p_ref,
                 gram_ref, acc_ref, mask_ref, mask_vmem, load_ref, prec_ref, base_ref, row_ref, sems):
    unit, n_unit = index_ref[0], index_ref[2]
    copies = [
        pltpu.make_async_copy(source, target, sems.at[k])
        for k, (source, target) in enumerate((
            (load_hbm, load_ref), (prec_hbm, prec_ref), (trans_hbm, base_ref.at[0]), (var_hbm, row_ref.at[0]),
            (prior_hbm, row_ref.at[1]), (mask_hbm, mask_ref), (mask_hbm, mask_vmem),
        ))
    ]
    for copy in copies:
        copy.start()
    for copy in copies:
        copy.wait()
    eye = identity()
    n_blocks = load_ref.shape[0] // WIDTH
    for block in range(n_blocks):
        load = load_ref[block * WIDTH:(block + 1) * WIDTH, :]
        weighted = (jnp.transpose(load.astype(f32)) * prec_ref[block:block + 1, :]).astype(bf16)
        weight_ref[block] = weighted
        gram = mm(weighted, load)
        gram_ref[block] = 0.5 * (gram + jnp.transpose(gram))
    base_ref[1] = eye * row_ref[0]
    base_ref[2] = jnp.transpose(base_ref[0])
    const_ref[0] = jnp.broadcast_to(row_ref[1], (WIDTH, WIDTH))
    const_ref[1] = base_ref[1]
    mask_out[...] = mask_vmem[...].astype(f32).astype(bf16)

    def info(step):
        out = mask_ref[0, step].astype(f32) * gram_ref[0]
        for block in range(1, n_blocks):
            out = out + mask_ref[block, step].astype(f32) * gram_ref[block]
        return out

    end_ref[...] = info(n_unit * half - 1)

    def leaves(node):
        step = unit * half + 2 * node
        start = jnp.where(step == 0, 1.0, 0.0).astype(f32)
        trans, noise = base_ref[0], base_ref[1]
        before = info(jnp.maximum(step - 1, 0)) * (1.0 - start)
        first = (trans * (1.0 - start), noise + start * (eye - noise), before)
        return first, (trans, noise, info(step))

    outs = (uz_ref, yv_ref, a_ref, c_ref, j_ref, p_ref)

    def sweep(fast):
        count = half // 2
        group = min(count, GROUP) if fast else 1

        def some(block, carry):
            nodes = [block * group + k for k in range(group)]
            pairs = [leaves(node) for node in nodes]
            items = [join_item(0, pair, eye) for pair in pairs]
            inverses = invert(items, eye, fast, acc_ref)
            store_joined(outs, nodes, inverses, joined(0, pairs, inverses, eye, [base_ref[2]] * group))
            return carry

        lax.fori_loop(0, count // group, some, 0)

    checked(sweep, acc_ref)


def invert(items, eye, fast, acc_ref):
    if not fast:
        return [safe_inverse(mat, eye) for mat, _, _ in items]
    inverses, worst = fast_inverses(items, eye)
    acc_ref[...] = jnp.maximum(acc_ref[...], worst)
    return inverses


def checked(sweep, acc_ref):
    acc_ref[...] = jnp.zeros((8, WIDTH), f32)
    sweep(True)
    worst = jnp.sum(acc_ref[...])

    @pl.when(jnp.logical_not(worst <= RESIDUAL_MAX))
    def _():
        sweep(False)


def store_joined(outs, nodes, inverses, results):
    uz_ref, yv_ref, a_ref, c_ref, j_ref, p_ref = outs
    for node, p, (u, v, t, z, y, c, j) in zip(nodes, inverses, results):
        uh, ul = split(u)
        zh, zl = split(z)
        uz_ref[node] = rows(lanes(uh, zh), lanes(ul, zl))
        yv_ref[node] = rows(pack(y), pack(v))
        p_ref[node] = p
        a_ref[node] = t
        c_ref[node] = c
        j_ref[node] = j


def entries_of(level, half, steps, first, unit, refs, below):
    found = []
    for at_level, at in path_steps(half, steps, first):
        if at_level != level:
            continue
        node = at // (2 << level)
        if level == 0:
            eye = identity()
            start = jnp.where(unit * half + at == 0, 1.0, 0.0).astype(f32)
            c1 = below + start * (eye - below)
        else:
            c1 = below[2 * node]
        found.append(level_entry(refs, level, node, c1))
    return found


def up_kernel(joins, half, steps, index_ref, const_ref, *refs):
    unit, place = index_ref[0], index_ref[1]
    low = joins[0]
    held = {}
    refs = list(refs)
    if low > 1:
        below_ref = refs.pop(0)
    held[low - 1], refs = refs[:LEVEL_ARRAYS], refs[LEVEL_ARRAYS:]
    outs = {}
    for level in joins:
        held[level], refs = refs[:LEVEL_ARRAYS], refs[LEVEL_ARRAYS:]
        outs[level], refs = refs[:3], refs[3:]
    acc_ref, = refs
    eye = identity()

    def children(level, node):
        _, _, a_ref, c_ref, j_ref, _ = held[level - 1]
        return tuple((a_ref[k], c_ref[k], j_ref[k]) for k in (2 * node, 2 * node + 1))

    def condition_inputs(level):
        if level == 0:
            below = const_ref[1]
        elif level == low - 1:
            below = below_ref
        else:
            below = held[level - 1][3]
        return entries_of(level, half, steps, place * steps, unit, held[level], below)

    def store(level, results):
        for slot, result in enumerate(results):
            for ref, value in zip(outs[level], result):
                ref[slot] = value

    def sweep(fast):
        for level in joins:
            count = half >> (level + 1)
            under = level - 1
            if fast and count <= GROUP:
                nodes = list(range(count))
                entries = condition_inputs(under)
                pairs = [children(level, node) for node in nodes]
                items = [join_item(level, pair, eye) for pair in pairs]
                extra = [condition_item(under, entry, eye) for entry in entries]
                inverses = invert(items + [item for item, _ in extra], eye, True, acc_ref)
                store_joined(held[level], nodes, inverses[:count], joined(level, pairs, inverses[:count], eye))
                store(level, conditioned(entries, [scale for _, scale in extra], inverses[count:]))
                continue
            group = min(count, GROUP) if fast else 1

            def some(block, carry):
                nodes = [block * group + k for k in range(group)]
                pairs = [children(level, node) for node in nodes]
                inverses = invert([join_item(level, pair, eye) for pair in pairs], eye, fast, acc_ref)
                store_joined(held[level], nodes, inverses, joined(level, pairs, inverses, eye))
                return carry

            lax.fori_loop(0, count // group, some, 0)
            entries = condition_inputs(under)
            extra = [condition_item(under, entry, eye) for entry in entries]
            inverses = invert([item for item, _ in extra], eye, fast, acc_ref)
            store(level, conditioned(entries, [scale for _, scale in extra], inverses))

    checked(sweep, acc_ref)


SMEM = pl.BlockSpec(memory_space=pltpu.SMEM)
VMEM = pl.BlockSpec(memory_space=pltpu.VMEM)


ANY = pl.BlockSpec(memory_space=pl.ANY)


def level_shapes(half, level):
    count = half >> (level + 1)
    mat = (count, WIDTH, WIDTH)
    wide = (count, 2 * WIDTH, 2 * WIDTH)
    return [jax.ShapeDtypeStruct(wide, bf16)] * 2 + [jax.ShapeDtypeStruct(mat, f32)] * 4


def path_shapes(half, steps, level):
    count = len([k for k, _ in path_steps(half, steps, 0) if k == level])
    return [
        jax.ShapeDtypeStruct((count, 2 * WIDTH, 2 * WIDTH), bf16),
        jax.ShapeDtypeStruct((count, WIDTH, WIDTH), f32),
        jax.ShapeDtypeStruct((count, 3 * WIDTH, 2 * WIDTH), bf16),
    ]


def estimate(matrices):
    return pl.CostEstimate(flops=matrices * 600 * WIDTH**3, transcendentals=0, bytes_accessed=1 << 20)


def first_sweep(half, index, cell_mask, loadings, prec_rows, transition, var_row, prior_row):
    mat = (WIDTH, WIDTH)
    n_blocks = loadings.shape[0] // WIDTH
    outs = [
        jax.ShapeDtypeStruct((n_blocks,) + mat, bf16),
        jax.ShapeDtypeStruct(mat, f32),
        jax.ShapeDtypeStruct(cell_mask.shape, bf16),
        jax.ShapeDtypeStruct((2,) + mat, f32),
    ] + level_shapes(half, 0)
    inputs = [
        pltpu.with_memory_space_constraint(array, pltpu.HBM)
        for array in (cell_mask, loadings, prec_rows, transition, var_row, prior_row)
    ]
    return pl.pallas_call(
        functools.partial(first_kernel, half),
        out_shape=outs,
        in_specs=[SMEM] + [ANY] * 6,
        out_specs=[VMEM] * len(outs),
        scratch_shapes=[
            pltpu.VMEM((n_blocks,) + mat, f32),
            pltpu.VMEM((8, WIDTH), f32),
            pltpu.SMEM(cell_mask.shape, jnp.int32),
            pltpu.VMEM(cell_mask.shape, jnp.int32),
            pltpu.VMEM(loadings.shape, bf16),
            pltpu.VMEM(prec_rows.shape, f32),
            pltpu.VMEM((3,) + mat, f32),
            pltpu.VMEM((2, 1, WIDTH), f32),
            pltpu.SemaphoreType.DMA((7,)),
        ],
        compiler_params=pltpu.CompilerParams(vmem_limit_bytes=VMEM_LIMIT),
        cost_estimate=estimate(half // 2),
        name="first_sweep",
    )(index, *inputs)


def up_sweep(joins, half, steps, index, consts, held):
    low = joins[0]
    operands = ([held[low - 2][3]] if low > 1 else []) + list(held[low - 1])
    outs = []
    for level in joins:
        outs += level_shapes(half, level) + path_shapes(half, steps, level - 1)
    results = pl.pallas_call(
        functools.partial(up_kernel, joins, half, steps),
        out_shape=outs,
        in_specs=[SMEM] + [VMEM] * (1 + len(operands)),
        out_specs=[VMEM] * len(outs),
        scratch_shapes=[pltpu.VMEM((8, WIDTH), f32)],
        compiler_params=pltpu.CompilerParams(vmem_limit_bytes=VMEM_LIMIT),
        cost_estimate=estimate(sum(half >> level for level in joins)),
        name="up_sweep_%d" % low,
    )(index, consts, *operands)
    results = list(results)
    step = LEVEL_ARRAYS + 3
    parts = [results[k * step:(k + 1) * step] for k in range(len(joins))]
    return [part[:LEVEL_ARRAYS] for part in parts], [part[LEVEL_ARRAYS:] for part in parts]


def vector_kernel(half, rows_own, index_ref, mask_ref, weight_ref, const_ref, *refs):
    n_levels = half.bit_length() - 1
    gain_refs, refs = refs[:2 * n_levels], refs[2 * n_levels:]
    *pair_refs, leaf_ref, b_ref, e_ref, message_ref, all_ref, panel_ref = refs
    unit, place = index_ref[0], index_ref[3]
    total = panel_ref.shape[1]
    n_blocks = weight_ref.shape[0]
    panel_in, = pair_refs
    n_time = panel_in.shape[0] // (2 * rows_own)
    for k in range(panel_in.shape[0] // rows_own):
        core, chip, hop = unit, place, n_time // 2
        for bit in range(n_time.bit_length() - 1):
            if (k >> bit) % 2:
                chip = jnp.bitwise_xor(chip, hop)
            hop = hop // 2
        if k >= n_time:
            core = 1 - unit
        at = pl.multiple_of((2 * chip + core) * rows_own, rows_own)
        panel_ref[pl.ds(at, rows_own), :] = panel_in[k * rows_own:(k + 1) * rows_own, :]
    turned = jnp.zeros((WIDTH, total), f32)
    for block in range(n_blocks):
        mask = mask_ref[block:block + 1, :]
        turned = turned + mm(weight_ref[block], mask * panel_ref[block * WIDTH:(block + 1) * WIDTH, :])
    late = pltpu.roll(jnp.transpose(turned), 1, 0)
    end = late[0:1, :]
    all_ref[...] = late
    all_ref[0:1, :] = jnp.zeros((1, WIDTH), f32)
    leaf_ref[...] = all_ref[pl.ds(pl.multiple_of(unit * half, half), half), :]
    prior = jnp.where(unit == 0, 1.0, 0.0) * const_ref[0, 0:1, :]
    zero = jnp.zeros((1, WIDTH), f32)
    for level in range(half.bit_length() - 1):
        stride = 1 << level
        uz_ref, yv_ref = gain_refs[2 * level:2 * level + 2]
        for node in range(half >> (level + 1)):
            at = (2 * node + 1) * stride - 1
            if level == 0:
                b1, b2 = (prior if node == 0 else zero), zero
                e1, e2 = leaf_ref[at:at + 1, :], leaf_ref[at + 1:at + 2, :]
            else:
                one, two = at - stride // 2, at + stride // 2
                b1, b2 = b_ref[one:one + 1, :], b_ref[two:two + 1, :]
                e1, e2 = e_ref[one:one + 1, :], e_ref[two:two + 1, :]
            high, low = split(lanes(b1, e2))
            out = mm_nt(rows(high, low), uz_ref[node])
            b_ref[at:at + 1, :] = b2 + out[0:1, :WIDTH] + out[1:2, :WIDTH] + out[0:1, WIDTH:]
            high, low = split(lanes(-b1, e2))
            out = mm(rows(high, low), yv_ref[node])
            e_ref[at:at + 1, :] = e1 + out[0:1, :WIDTH] + out[1:2, :WIDTH] + out[0:1, WIDTH:]
    top = half // 2 - 1
    message_ref[...] = rows(b_ref[top:top + 1, :], e_ref[top:top + 1, :], end, jnp.zeros((5, WIDTH), f32))


def vector_sweep(half, rows_own, index, mask, weighted, consts, gains, pairs):
    total = pairs[0].shape[1]
    row = jax.ShapeDtypeStruct((half, WIDTH), f32)
    return pl.pallas_call(
        functools.partial(vector_kernel, half, rows_own),
        out_shape=(row, row, row, jax.ShapeDtypeStruct((8, WIDTH), f32)),
        in_specs=[SMEM] + [VMEM] * (3 + len(gains) + len(pairs)),
        out_specs=(VMEM,) * 4,
        scratch_shapes=[
            pltpu.VMEM((total, WIDTH), f32),
            pltpu.VMEM((len(pairs) * pairs[0].shape[0], total), bf16),
        ],
        compiler_params=pltpu.CompilerParams(vmem_limit_bytes=VMEM_LIMIT),
        name="vector_sweep",
    )(index, mask, weighted, consts, *gains, *pairs)


def down_kernel(steps, index_ref, own_ref, other_ref, end_ref, vown_ref, vother_ref, const_ref, leaf_ref, b_ref, e_ref, below_ref,
                *refs):
    refs = list(refs)
    top_refs, refs = refs[:LEVEL_ARRAYS], refs[LEVEL_ARRAYS:]
    out_ref, acc_ref, top_ref, gt_ref, cond_ref, shift_ref = refs[-6:]
    path_refs = refs[:-6]
    unit, place = index_ref[0], index_ref[1]
    half = leaf_ref.shape[0]
    n_levels = half.bit_length() - 1
    eye = identity()
    flag = jnp.where(unit == 0, 1.0, 0.0).astype(f32)

    def pick(zero, one):
        return flag * zero + (1.0 - flag) * one

    cov0 = pick(own_ref[1], other_ref[1])
    trans1, cov1, info1 = [pick(other_ref[k], own_ref[k]) for k in range(3)]
    b0 = pick(vown_ref[0:1, :], vother_ref[0:1, :])
    b1, e1 = [pick(vother_ref[k:k + 1, :], vown_ref[k:k + 1, :]) for k in range(2)]
    e_end = vown_ref[2:3, :]
    end = end_ref[...]

    first = place * steps

    def roots(fast):
        under = n_levels - 1
        entries = entries_of(under, half, steps, first, unit, top_refs, below_ref)
        extra = [condition_item(under, entry, eye) for entry in entries]
        item = (eye + mm3(cov0, info1), bounds_at(JOIN_BOUNDS, n_levels), False)
        p, *inverses = invert([item] + [item for item, _ in extra], eye, fast, acc_ref)
        kept = mm3(p, cov0)
        z = mm3(trans1, kept)
        cov = cov1 + mm3_nt(z, trans1)
        cov = 0.5 * (cov + jnp.transpose(cov))
        mat, scale = scaled(cov, eye)
        results = conditioned(entries, [scale for _, scale in extra], inverses)
        for slot, result in enumerate(results):
            for ref, value in zip((gt_ref, cond_ref, shift_ref), result):
                ref[slot] = value
        last = (eye + mm3(cov, end), bounds_at(JOIN_BOUNDS, 0), False)
        inverse, p_end = invert([(mat, bounds_at(COV_BOUNDS, n_levels), True), last], eye, fast, acc_ref)
        top_ref[0], top_ref[1], top_ref[2], top_ref[3] = p, kept, z, cov
        top_ref[4], top_ref[5] = jnp.transpose(inverse) * scale, p_end

    checked(roots, acc_ref)
    p, kept, z, cov, inverse, p_end = [top_ref[k] for k in range(6)]
    back = mm3(inverse, z)
    forth = jnp.transpose(back)
    mean_mid = mm3_nt(b0 + mm3(e1, cov0), p)
    b_end = mm3_nt(mean_mid, trans1) + b1
    mean_top = mm3_nt(b_end + mm3(e_end, cov), p_end)
    mean_mid = mean_mid + mm3(mean_top - b_end, back)
    cov_top = mm3(p_end, cov)
    cov_top = 0.5 * (cov_top + jnp.transpose(cov_top))
    cov_cross = mm3(cov_top, back)
    cov_mid = kept - mm3(forth, z) + mm3(forth, cov_cross)
    keep = 1.0 - flag
    joint = rows(
        lanes(keep * cov_mid, keep * jnp.transpose(cov_cross)),
        lanes(keep * cov_cross, pick(cov_mid, cov_top)),
    )
    means = lanes(keep * mean_mid, pick(mean_mid, mean_top))
    prior = flag * const_ref[0, 0:1, :]
    path = path_steps(half, steps, first)
    levels = [(gt_ref, cond_ref, shift_ref)] + [path_refs[k:k + 3] for k in range(0, len(path_refs), 3)]
    places, seen = [], {}
    for level, _ in path:
        seen[level] = seen.get(level, -1) + 1
        places.append((levels[n_levels - 1 - level], seen[level]))

    def shift(slot):
        level, at = path[slot]
        row_of = lambda ref, k: ref[pl.ds(k, 1), :]
        if level == 0:
            one, two = jnp.where(at == 0, 1.0, 0.0) * prior, row_of(leaf_ref, at + 1)
        else:
            near = (1 << level) // 2
            one, two = row_of(b_ref, at - near), row_of(e_ref, at + near)
        high, low = split(lanes(one, two, row_of(b_ref, at)))
        arrays, own = places[slot]
        out = mm(rows(high, low), arrays[2][own])
        return out[0:1, :WIDTH] + out[1:2, :WIDTH] + out[0:1, WIDTH:]

    shifts = [shift(slot) for slot in range(len(path))]

    def node(slot, joint, means, leaf):
        (gt_ref, cond_ref, _), at = places[slot]
        packed = gt_ref[at]
        gh, gl = packed[:, :WIDTH], packed[:, WIDTH:]
        jh, jl = split(joint)
        cross = mm(lanes(jh, jl), rows(gh, gh)) + mm(jh, gl)
        high, low = split(means)
        out = mm(rows(high, low), packed)
        mean = shifts[slot] + out[0:1, :WIDTH] + out[1:2, :WIDTH] + out[0:1, WIDTH:]
        gain = unpack(packed)
        if leaf:
            own = diagonal(cond_ref[at], eye) + jnp.sum(gain * cross, axis=0, keepdims=True)
        else:
            own = cond_ref[at] + mm3(jnp.transpose(gain), cross)
        return mean, own, cross

    def left_pair(joint, means, mean, own, cross):
        c = cross[:WIDTH]
        return rows(lanes(joint[:WIDTH, :WIDTH], c), lanes(jnp.transpose(c), own)), lanes(means[:, :WIDTH], mean)

    def right_pair(joint, means, mean, own, cross):
        c = cross[WIDTH:]
        return rows(lanes(own, jnp.transpose(c)), lanes(c, joint[WIDTH:, WIDTH:])), lanes(mean, means[:, WIDTH:])

    slot = 0
    while path[slot][0] >= steps.bit_length() - 1:
        result = node(slot, joint, means, False)
        go_right = jnp.where(first > path[slot][1], 1.0, 0.0).astype(f32)
        lj, lm = left_pair(joint, means, *result)
        rj, rm = right_pair(joint, means, *result)
        joint = go_right * rj + (1.0 - go_right) * lj
        means = go_right * rm + (1.0 - go_right) * lm
        slot += 1

    out_ref[steps - 1:steps, :] = means[:, WIDTH:]
    out_ref[2 * steps - 1:2 * steps, :] = diagonal(joint[WIDTH:, WIDTH:], eye)
    todo = [(0, steps, joint, means)]
    while todo:
        later = []
        for low, count, joint, means in todo:
            stride = count // 2
            at = low + stride - 1
            result = node(slot, joint, means, stride == 1)
            slot += 1
            out_ref[at:at + 1, :] = result[0]
            if stride == 1:
                out_ref[steps + at:steps + at + 1, :] = result[1]
                continue
            out_ref[steps + at:steps + at + 1, :] = diagonal(result[1], eye)
            later.append((low, stride) + left_pair(joint, means, *result))
            later.append((low + stride, stride) + right_pair(joint, means, *result))
        todo = later


def down_sweep(steps, half, *operands):
    return pl.pallas_call(
        functools.partial(down_kernel, steps),
        out_shape=jax.ShapeDtypeStruct((2 * steps, WIDTH), f32),
        in_specs=[SMEM] + [VMEM] * (len(operands) - 1),
        out_specs=VMEM,
        scratch_shapes=[pltpu.VMEM((8, WIDTH), f32), pltpu.VMEM((6, WIDTH, WIDTH), f32)]
        + [pltpu.VMEM(shape.shape, shape.dtype) for shape in path_shapes(half, steps, half.bit_length() - 2)],
        compiler_params=pltpu.CompilerParams(vmem_limit_bytes=VMEM_LIMIT),
        name="down_sweep",
    )(*operands)


def redundant(panel_data, cell_mask, loadings, noise_prec, transition, proc_var, prior_mean):
    n_time = lax.axis_size("tm")
    n_unit = lax.axis_size("unit")
    place, unit = lax.axis_index("tm"), lax.axis_index("unit")
    total = panel_data.shape[1]
    half = total // n_unit
    steps = total // n_time
    per_half = half // steps
    index = jnp.stack([unit, place % per_half, n_unit, place]).astype(jnp.int32)
    swap = [(0, 1), (1, 0)]

    def swapped(value, other):
        return lax.ppermute(value, "tm", [(k, k ^ other) for k in range(n_time)])

    n_levels = half.bit_length() - 1
    hops = [1 << k for k in reversed(range(n_time.bit_length() - 1))]
    weighted, end, mask, consts, *level0 = first_sweep(
        half, index, cell_mask, loadings, noise_prec.reshape(-1, WIDTH), transition,
        proc_var.reshape(1, WIDTH), prior_mean.reshape(1, WIDTH),
    )
    held, paths = [level0], []
    panel = panel_data
    cuts = [[1], [2], list(range(3, n_levels))]
    panel = jnp.concatenate([panel, swapped(panel, hops[0])])
    for k, joins in enumerate(cuts):
        panel, latest = lax.optimization_barrier((panel, held[-1]))
        held[-1] = latest
        if k + 1 < len(hops):
            panel = jnp.concatenate([panel, swapped(panel, hops[k + 1])])
        else:
            panel = jnp.concatenate([panel, lax.ppermute(panel, "unit", swap)])
        new, path = up_sweep(joins, half, steps, index, consts, held)
        held += new
        paths += path
    message = jnp.concatenate(held[-1][2:5])
    other = lax.ppermute(message, "unit", swap)
    gains = [array for level in held for array in level[:2]]
    leaves, bs, es, vmessage = vector_sweep(half, panel_data.shape[0], index, mask, weighted, consts, gains, [panel])
    vother = lax.ppermute(vmessage, "unit", swap)
    mine = down_sweep(
        steps, half, index, message, other, end, vmessage, vother, consts, leaves, bs, es, held[-2][3], *held[-1],
        *[array for path in reversed(paths) for array in path],
    )
    theirs = lax.ppermute(mine, "unit", swap)
    out = jnp.where(unit == place // per_half, mine, theirs)
    return out[:steps], out[steps:]


BLOCK = 128


def carried_in(value, axis, join, neutral, backward):
    count, mine = (lax.axis_size(axis), lax.axis_index(axis))
    pieces = jax.tree.map(lambda part: lax.all_gather(part, axis), value)
    if backward:
        pieces = jax.tree.map(lambda part: part[::-1], pieces)
        mine = count - 1 - mine
    running = jax.tree.map(
        lambda part, zero: jnp.full_like(part, 0) + jnp.asarray(zero, part.dtype), value, neutral
    )

    def step(position, running):
        longer = join(running, jax.tree.map(lambda part: part[position], pieces))
        return jax.tree.map(lambda new, old: jnp.where(position < mine, new, old), longer, running)

    return lax.fori_loop(0, count - 1, step, running)


def product(left, right):
    return jnp.matmul(left, right, precision=HIGHEST)


def mat_vec(matrix, vector):
    return jnp.einsum("...kl,...l->...k", matrix, vector, precision=HIGHEST)


def flipped(matrix):
    return jnp.swapaxes(matrix, -1, -2)


def chol_apply(factor, rhs):
    middle = lax.linalg.triangular_solve(factor, rhs, left_side=True, lower=True)
    return lax.linalg.triangular_solve(factor, middle, left_side=True, lower=True, transpose_a=True)


def filter_join(earlier, later):
    trans_one, shift_one, cov_one, info_one, vec_one, live_one = earlier
    trans_two, shift_two, cov_two, info_two, vec_two, live_two = later
    identity_mat = jnp.eye(trans_one.shape[-1], dtype=jnp.float32)
    live_mat = live_one[..., None, None]
    factor_one = jnp.linalg.cholesky(cov_one + (1.0 - live_mat) * identity_mat)
    inner_mat = identity_mat + product(product(flipped(factor_one), info_two), factor_one)
    inner_factor = jnp.linalg.cholesky(inner_mat)
    solved = lax.linalg.triangular_solve(
        inner_factor, flipped(factor_one), left_side=True, lower=True
    )
    spread_mat = product(trans_two, flipped(solved))
    pushed = product(info_two, trans_one)
    reduced = product(solved, pushed)
    residue = vec_two - mat_vec(info_two, shift_one)
    solved_residue = mat_vec(solved, residue)
    trans_new = product(trans_two, trans_one) - product(spread_mat, reduced)
    shift_new = mat_vec(trans_two, shift_one) + mat_vec(spread_mat, solved_residue) + shift_two
    cov_new = product(spread_mat, flipped(spread_mat)) + cov_two
    info_new = product(flipped(trans_one), pushed) - product(flipped(reduced), reduced) + info_one
    vec_new = (
        mat_vec(flipped(trans_one), residue) - mat_vec(flipped(reduced), solved_residue) + vec_one
    )
    alive_mat = live_mat > 0.5
    alive_vec = live_one[..., None] > 0.5
    return (
        jnp.where(alive_mat, trans_new, trans_two),
        jnp.where(alive_vec, shift_new, shift_two),
        jnp.where(alive_mat, cov_new, cov_two),
        jnp.where(alive_mat, info_new, info_two),
        jnp.where(alive_vec, vec_new, vec_two),
        jnp.maximum(live_one, live_two),
    )


def smooth_join(lower_elem, higher_elem):
    gain_low, offset_low, cov_low = lower_elem
    gain_high, offset_high, cov_high = higher_elem
    return (
        product(gain_low, gain_high),
        mat_vec(gain_low, offset_high) + offset_low,
        product(product(gain_low, cov_high), flipped(gain_low)) + cov_low,
    )


def smooth_scan_join(earlier, later):
    return smooth_join(later, earlier)


def take_last(stacked):
    return stacked[-1]


def take_first(stacked):
    return stacked[0]


def per_device(panel_data, cell_mask, loadings, noise_prec, transition, proc_var, prior_mean):
    n_time = lax.axis_size("tm")
    n_unit = lax.axis_size("unit")
    time_index = lax.axis_index("tm")
    unit_index = lax.axis_index("unit")
    rows_own, total_time = panel_data.shape
    steps = total_time // n_time
    width = transition.shape[0]
    identity_mat = jnp.eye(width, dtype=jnp.float32)
    my_columns = lax.dynamic_slice_in_dim(cell_mask, time_index * steps, steps, 1)
    half_load = lax.dynamic_index_in_dim(
        loadings.reshape(n_time, n_unit, rows_own, width), unit_index, 1, keepdims=False
    ).reshape(n_time * rows_own, width)
    half_prec = lax.dynamic_index_in_dim(
        noise_prec.reshape(n_time, n_unit, rows_own), unit_index, 1, keepdims=False
    ).reshape(n_time * rows_own)
    half_ids = (
        (jnp.arange(n_time, dtype=jnp.int32)[:, None] * n_unit + unit_index) * rows_own
        + jnp.arange(rows_own, dtype=jnp.int32)[None, :]
    ).reshape(-1)
    half_weighted = (half_prec[:, None] * half_load.astype(jnp.float32)).astype(jnp.bfloat16)
    half_mask = jnp.take(my_columns, half_ids // BLOCK, axis=0).astype(jnp.bfloat16)
    regrouped = lax.all_to_all(panel_data, "tm", split_axis=1, concat_axis=0, tiled=True)
    vec_half = jnp.dot((half_mask * regrouped).T, half_weighted, preferred_element_type=jnp.float32)
    group_rows = min(rows_own, BLOCK)
    n_groups = n_time * rows_own // group_rows
    group_gram = jnp.einsum(
        "gnk,gnl->gkl",
        half_weighted.reshape(n_groups, group_rows, width),
        half_load.reshape(n_groups, group_rows, width),
        preferred_element_type=jnp.float32,
    )
    group_block = half_ids.reshape(n_groups, group_rows)[:, 0] // BLOCK
    group_mask = jnp.take(my_columns, group_block, axis=0).astype(jnp.float32)
    info_half = jnp.einsum("gt,gkl->tkl", group_mask, group_gram, precision=HIGHEST)
    info_mat, info_vec = lax.psum((info_half, vec_half), "unit")
    global_step = time_index * steps + jnp.arange(steps, dtype=jnp.int32)
    first_step = (global_step == 0).astype(jnp.float32)
    keep_step = 1.0 - first_step
    last_keep = 1.0 - (global_step == total_time - 1).astype(jnp.float32)
    inv_var = 1.0 / proc_var
    prior_prec = first_step[:, None, None] * identity_mat + keep_step[:, None, None] * jnp.diag(
        inv_var
    )
    eyes = jnp.broadcast_to(identity_mat, info_mat.shape)
    post_cov = chol_apply(jnp.linalg.cholesky(prior_prec + info_mat), eyes)
    shift_vec = jnp.einsum(
        "skl,sl->sk",
        post_cov,
        info_vec + first_step[:, None] * prior_mean[None, :],
        precision=HIGHEST,
    )
    scaled_trans = inv_var[:, None] * transition
    trans_part = keep_step[:, None, None] * jnp.einsum(
        "skl,lm->skm", post_cov, scaled_trans, precision=HIGHEST
    )
    middle = jnp.diag(inv_var)[None] - inv_var[None, :, None] * post_cov * inv_var[None, None, :]
    pressed = jnp.einsum("slm,mn->sln", middle, transition, precision=HIGHEST)
    info_part = keep_step[:, None, None] * jnp.einsum(
        "lk,sln->skn", transition, pressed, precision=HIGHEST
    )
    vec_part = keep_step[:, None] * jnp.einsum(
        "lk,sl->sk", transition, inv_var[None, :] * shift_vec, precision=HIGHEST
    )
    elements = (
        trans_part,
        shift_vec,
        post_cov,
        info_part,
        vec_part,
        jnp.ones((steps,), jnp.float32),
    )
    zero_vec = jnp.zeros((width,), jnp.float32)
    zero_mat = jnp.zeros((width, width), jnp.float32)
    filter_identity = (identity_mat, zero_vec, zero_mat, zero_mat, zero_vec, jnp.float32(0.0))
    local_joined = lax.associative_scan(filter_join, elements)
    filter_total = jax.tree.map(take_last, local_joined)
    before = carried_in(filter_total, "tm", filter_join, filter_identity, False)
    filtered = jax.vmap(filter_join, in_axes=(None, 0))(before, local_joined)
    filt_mean = filtered[1]
    filt_cov = filtered[2]
    moved_cov = jnp.einsum("kl,slm->skm", transition, filt_cov, precision=HIGHEST)
    pred_next = (
        jnp.einsum("skm,nm->skn", moved_cov, transition, precision=HIGHEST)
        + jnp.diag(proc_var)[None]
    )
    gain = (
        jnp.transpose(chol_apply(jnp.linalg.cholesky(pred_next), moved_cov), (0, 2, 1))
        * last_keep[:, None, None]
    )
    moved_mean = jnp.einsum("kl,sl->sk", transition, filt_mean, precision=HIGHEST)
    offset = filt_mean - jnp.einsum("skl,sl->sk", gain, moved_mean, precision=HIGHEST)
    resid_cov = filt_cov - jnp.einsum("skl,slm->skm", gain, moved_cov, precision=HIGHEST)
    smooth_identity = (identity_mat, zero_vec, zero_mat)
    local_suffix = lax.associative_scan(smooth_scan_join, (gain, offset, resid_cov), reverse=True)
    smooth_total = jax.tree.map(take_first, local_suffix)
    after = carried_in(smooth_total, "tm", smooth_scan_join, smooth_identity, True)
    smoothed = jax.vmap(smooth_join, in_axes=(0, None))(local_suffix, after)
    smoothed_mean = smoothed[1]
    smoothed_var = jnp.diagonal(smoothed[2], axis1=1, axis2=2)
    return (smoothed_mean, smoothed_var)


def per_device_any(*arrays):
    fits = arrays[0].shape[1] <= 64 * lax.axis_size("unit") and lax.axis_size("unit") == 2
    return redundant(*arrays) if fits else per_device(*arrays)


def solution(mesh):
    return jax.shard_map(
        per_device_any,
        mesh=mesh,
        in_specs=(P(("grp", "tm", "unit"), None), P("grp", None), P(), P(), P(), P(), P()),
        out_specs=(P(("grp", "tm"), None), P(("grp", "tm"), None)),
        check_vma=False,
    )
```

```python
import functools

import jax
import jax.numpy as jnp
from jax import lax
from jax.experimental import pallas as pl
from jax.experimental.pallas import tpu as pltpu
from jax.sharding import PartitionSpec as P

f32 = jnp.float32
bf16 = jnp.bfloat16
WIDTH = 128
HIGHEST = lax.Precision.HIGHEST
VMEM_LIMIT = 30 << 20
RESIDUAL_MAX = 1e-2
GROUP = 16
JOIN_BOUNDS = ((1.0, 3.3), (1.0, 3.0), (1.0, 3.3), (1.0, 4.8), (1.0, 7.2), (1.0, 10.5))
COV_BOUNDS = ((0.72, 1.32), (0.51, 1.75), (0.31, 2.50), (0.19, 3.75), (0.13, 4.50), (0.09, 5.00))


def schedule(bounds, goal=2.5e-3):
    low, high = bounds
    alpha, radius, factors = 2.0 / (low + high), (high - low) / (high + low), []
    while radius > goal:
        square = radius * radius
        factors.append(2.0 / (2.0 - square))
        radius = square / (2.0 - square)
    return alpha, factors


def bounds_at(table, level):
    return table[min(level, len(table) - 1)]


def mm(left, right):
    return lax.dot_general(left, right, (((1,), (0,)), ((), ())), preferred_element_type=f32)


def mm_nt(left, right):
    return lax.dot_general(left, right, (((1,), (1,)), ((), ())), preferred_element_type=f32)


def split(value):
    high = value.astype(bf16)
    return high, (value - high.astype(f32)).astype(bf16)


def lanes(*parts):
    return jnp.concatenate(parts, axis=1)


def rows(*parts):
    return jnp.concatenate(parts, axis=0)


def mm3(left, right):
    lh, ll = split(left)
    rh, rl = split(right)
    return mm(lanes(lh, ll), rows(rh, rh)) + mm(lh, rl)


def mm3_nt(left, right):
    lh, ll = split(left)
    rh, rl = split(right)
    return mm_nt(lanes(lh, ll), lanes(rh, rh)) + mm_nt(lh, rl)


def identity():
    shape = (WIDTH, WIDTH)
    return (lax.broadcasted_iota(jnp.int32, shape, 0) == lax.broadcasted_iota(jnp.int32, shape, 1)).astype(f32)


def squares(value):
    return jnp.sum((value * value).reshape(WIDTH // 8, 8, WIDTH), axis=0)


def fast_inverses(items, eye, beside=iter(())):
    mats = [mat for mat, _, _ in items]
    plans = [schedule(bounds) for _, bounds, _ in items]
    n = range(len(items))
    halves = [split(mat) for mat in mats]
    rest = [eye - plan[0] * mat for plan, mat in zip(plans, mats)]
    guess = [(plan[0] * plan[1][0]) * (eye + r) for plan, r in zip(plans, rest)]
    for step in range(max(len(factors) for _, factors in plans)):
        rest_b = [r.astype(bf16) for r in rest]
        guess_b = [g.astype(bf16) for g in guess]
        for k in n:
            factors = plans[k][1]
            more = step + 1 < len(factors)
            if step >= len(factors):
                continue
            factor = factors[step]
            if step == 0:
                if more:
                    rest[k] = (1.0 - factor) * eye + factor * mm(rest_b[k], rest_b[k])
            elif more:
                out = mm(rest_b[k], lanes(guess_b[k], rest_b[k]))
                guess[k] = factor * (guess[k] + out[:, :WIDTH])
                rest[k] = (1.0 - factor) * eye + factor * out[:, WIDTH:]
            else:
                guess[k] = factor * (guess[k] + mm(rest_b[k], guess_b[k]))
        next(beside, None)
    guess_b = [g.astype(bf16) for g in guess]
    resid = [eye - mm(lanes(h, l), rows(g, g)) for (h, l), g in zip(halves, guess_b)]
    guess = [g.astype(f32) + mm(g, e.astype(bf16)) for g, e in zip(guess_b, resid)]
    next(beside, None)
    sides = [(g, e.astype(bf16)) for g, e in zip(guess_b, resid)]
    again = [k for k in n if items[k][2]]
    fine = {k: eye - mm3(mats[k], guess[k]) for k in again}
    for k in again:
        resid[k] = fine[k]
        guess[k] = guess[k] + mm(guess[k].astype(bf16), fine[k].astype(bf16))
    worst = squares(resid[0])
    for e in resid[1:]:
        worst = jnp.maximum(worst, squares(e))
    return guess, sides, worst


def safe_inverse(mat, eye):
    size = jnp.max(jnp.sum(jnp.abs(mat), axis=0, keepdims=True), axis=1, keepdims=True)
    product = functools.partial(jnp.dot, precision=HIGHEST, preferred_element_type=f32)

    def unfinished(state):
        step, size, _ = state
        return jnp.logical_and(step < 64, jnp.logical_not(size <= 1e-7))

    def improve(state):
        step, _, guess = state
        resid = eye - product(mat, guess)
        return step + 1, jnp.sum(squares(resid)), guess + product(guess, resid)

    return lax.while_loop(unfinished, improve, (0, f32(jnp.inf), eye / size))[2]


def diagonal(mat, eye):
    return jnp.sum(mat * eye, axis=0, keepdims=True)


def scaled(mat, eye):
    row = 1.0 / diagonal(mat, eye)
    return mat * row, row


def pack(value):
    return lanes(*split(value))


def unpack(value):
    return value[:, :WIDTH].astype(f32) + value[:, WIDTH:].astype(f32)


def path_steps(half, steps, first):
    found = []
    for level in reversed(range(half.bit_length() - 1)):
        stride = 1 << level
        if 2 * stride > steps:
            found.append((level, (first // (2 * stride)) * (2 * stride) + stride - 1))
        else:
            found += [(level, first + (2 * k + 1) * stride - 1) for k in range(steps // (2 * stride))]
    return found


def join_item(level, pair, eye):
    (_, c1, _), (_, _, j2) = pair
    return eye + mm3(c1, j2), bounds_at(JOIN_BOUNDS, level), False


def in_turns(*works):
    works = list(works)
    while works:
        for work in tuple(works):
            if next(work, works) is works:
                works.remove(work)


def joining(level, pairs, inverses, eye, results):
    turned = [jnp.transpose(one[0]) for one, two in pairs]
    if level < 2:
        less = [(eye - p).astype(bf16) for p in inverses]
        us = [two[0] - mm(two[0].astype(bf16), d) for (one, two), d in zip(pairs, less)]
        vs = [one[0] - mm(d, one[0].astype(bf16)) for (one, two), d in zip(pairs, less)]
    else:
        us = [mm3(two[0], p) for (one, two), p in zip(pairs, inverses)]
        vs = [mm3(p, one[0]) for (one, two), p in zip(pairs, inverses)]
    yield
    zs = [mm3(u, one[1]) for u, (one, two) in zip(us, pairs)]
    ys = [mm3(two[2], v) for v, (one, two) in zip(vs, pairs)]
    yield
    ts = [mm3(two[0], v) for v, (one, two) in zip(vs, pairs)]
    cs = [two[1] + mm3_nt(z, two[0]) for z, (one, two) in zip(zs, pairs)]
    yield
    js = [one[2] + mm3(t, y) for t, y, (one, two) in zip(turned, ys, pairs)]
    results += list(zip(us, vs, ts, zs, ys, cs, js))


def condition_item(level, entry, eye):
    mat, scale = scaled(entry["c"], eye)
    return (mat, bounds_at(COV_BOUNDS, level), level > 2), scale


def conditioning(entries, scales, inverses, results):
    zs, vs = [e["z"] for e in entries], [e["v"] for e in entries]
    kepts = [mm3(e["p"], e["c1"]) for e in entries]
    backs = [mm3(jnp.transpose(inverse) * scale, z) for inverse, scale, z in zip(inverses, scales, zs)]
    yield
    forths = [jnp.transpose(back) for back in backs]
    gains = [v - mm3(forth, e["a"]) for v, forth, e in zip(vs, forths, entries)]
    yield
    conds = [kept - mm3(forth, z) for kept, forth, z in zip(kepts, forths, zs)]
    yield
    results += [
        (
            pack(rows(jnp.transpose(gain), back)),
            cond,
            pack(rows(jnp.transpose(e["p"]), jnp.transpose(kept), -back)),
        )
        for e, gain, back, cond, kept in zip(entries, gains, backs, conds, kepts)
    ]


def level_entry(refs, level, node, c1):
    uz_ref, yv_ref, a_ref, c_ref, _, p_ref = refs
    uz = uz_ref[node]
    return dict(
        z=uz[:WIDTH, WIDTH:].astype(f32) + uz[WIDTH:, WIDTH:].astype(f32),
        v=unpack(yv_ref[node, WIDTH:, :]),
        a=a_ref[node],
        c=c_ref[node],
        p=p_ref[node],
        c1=c1,
    )


LEVEL_ARRAYS = 6


def first_kernel(half, index_ref, mask_hbm, load_hbm, prec_hbm, trans_hbm, var_hbm, prior_hbm,
                 weight_ref, end_ref, mask_out, const_ref, uz_ref, yv_ref, a_ref, c_ref, j_ref, p_ref,
                 gram_ref, acc_ref, mask_ref, mask_vmem, load_ref, prec_ref, base_ref, row_ref, sems):
    unit, n_unit = index_ref[0], index_ref[2]
    copies = [
        pltpu.make_async_copy(source, target, sems.at[k])
        for k, (source, target) in enumerate((
            (load_hbm, load_ref), (prec_hbm, prec_ref), (trans_hbm, base_ref.at[0]), (var_hbm, row_ref.at[0]),
            (prior_hbm, row_ref.at[1]), (mask_hbm, mask_ref), (mask_hbm, mask_vmem),
        ))
    ]
    for copy in copies:
        copy.start()
    for copy in copies:
        copy.wait()
    eye = identity()
    n_blocks = load_ref.shape[0] // WIDTH
    for block in range(n_blocks):
        load = load_ref[block * WIDTH:(block + 1) * WIDTH, :]
        weighted = (jnp.transpose(load.astype(f32)) * prec_ref[block:block + 1, :]).astype(bf16)
        weight_ref[block] = weighted
        gram = mm(weighted, load)
        gram_ref[block] = 0.5 * (gram + jnp.transpose(gram))
    base_ref[1] = eye * row_ref[0]
    base_ref[2] = jnp.transpose(base_ref[0])
    base_ref[3] = jnp.transpose(jnp.broadcast_to(row_ref[0], (WIDTH, WIDTH)))
    const_ref[0] = jnp.broadcast_to(row_ref[1], (WIDTH, WIDTH))
    const_ref[1] = base_ref[1]
    mask_out[...] = mask_vmem[...].astype(f32).astype(bf16)

    def info(step):
        out = mask_ref[0, step].astype(f32) * gram_ref[0]
        for block in range(1, n_blocks):
            out = out + mask_ref[block, step].astype(f32) * gram_ref[block]
        return out

    end_ref[...] = info(n_unit * half - 1)

    outs = (uz_ref, yv_ref, a_ref, c_ref, j_ref, p_ref)

    def leaf_joins(nodes, fast):
        trans, noise, turned, column, row = base_ref[0], base_ref[1], base_ref[2], base_ref[3], row_ref[0]
        step = [unit * half + 2 * node for node in nodes]
        start = jnp.where(step[0] == 0, 1.0, 0.0).astype(f32)
        before = [info(jnp.maximum(at - 1, 0)) for at in step]
        before[0] = before[0] * (1.0 - start)
        after = [info(at) for at in step]
        left = [trans * (1.0 - start)] + [trans] * (len(nodes) - 1)
        rows_of = [row + start * (1.0 - row)] + [row] * (len(nodes) - 1)
        mats = [eye + column * j for j in after]
        mats[0] = eye + (column + start * (1.0 - column)) * after[0]
        inverses = invert([(mat, bounds_at(JOIN_BOUNDS, 0), False) for mat in mats], eye, fast, acc_ref)
        less = [(eye - p).astype(bf16) for p in inverses]
        trans_b, turned_b = trans.astype(bf16), turned.astype(bf16)
        us = [trans - mm(trans_b, d) for d in less]
        vs = [one - mm(d, one.astype(bf16)) for one, d in zip(left, less)]
        zs = [u * r for u, r in zip(us, rows_of)]
        ts = [mm3(trans, v) for v in vs]
        ys = [mm3(j, v) for j, v in zip(after, vs)]
        cs = [noise + mm3_nt(z, trans) for z in zs]
        js = [j + mm3(turned, y) for j, y in zip(before, ys)]
        for node, p, u, v, t, z, y, c, j in zip(nodes, inverses, us, vs, ts, zs, ys, cs, js):
            zh, zl = split(z)
            uz_ref[node, :, WIDTH:] = rows(zh, zl)
            yv_ref[node, WIDTH:, :] = pack(v)
            p_ref[node] = p
            a_ref[node] = t
            c_ref[node] = c
            j_ref[node] = j
        uh, ul = split(us[0])
        uz_ref[nodes[0], :, :WIDTH] = rows(uh, ul)
        yv_ref[nodes[0], :WIDTH, :] = pack(ys[0])

    def sweep(fast):
        count = half // 2
        group = min(count, GROUP) if fast else 1

        def some(block, carry):
            leaf_joins([block * group + k for k in range(group)], fast)
            return carry

        lax.fori_loop(0, count // group, some, 0)

    checked(sweep, acc_ref)


def invert(items, eye, fast, acc_ref, apart=False, beside=iter(())):
    if not fast:
        inverses = [safe_inverse(mat, eye) for mat, _, _ in items]
        return (inverses, [(p, None, None) for p in inverses]) if apart else inverses
    inverses, sides, worst = fast_inverses(items, eye, beside)
    acc_ref[...] = jnp.maximum(acc_ref[...], worst)
    return (inverses, [(g, e, mat) for (g, e), (mat, _, _) in zip(sides, items)]) if apart else inverses


def times_inverse(left, side):
    guess, resid, _ = side
    if resid is None:
        return mm3(left, guess)
    out = mm(lanes(*split(left)), rows(guess, guess))
    return out + mm(out.astype(bf16), resid)


def inverse_times(side, right, eye):
    guess, resid, mat = side
    if resid is None:
        return mm3(guess, right)
    resid = eye - mm(lanes(guess, guess), rows(*split(mat)))
    out = mm(lanes(guess, guess), rows(*split(right)))
    return out + mm(resid.astype(bf16), out.astype(bf16))


def checked(sweep, acc_ref, **beside):
    acc_ref[...] = jnp.zeros((8, WIDTH), f32)
    sweep(True, **beside)
    worst = jnp.sum(acc_ref[...])

    @pl.when(jnp.logical_not(worst <= RESIDUAL_MAX))
    def _():
        sweep(False)


def store_joined(outs, nodes, inverses, results):
    uz_ref, yv_ref, a_ref, c_ref, j_ref, p_ref = outs
    for node, p, (u, v, t, z, y, c, j) in zip(nodes, inverses, results):
        uh, ul = split(u)
        zh, zl = split(z)
        uz_ref[node] = rows(lanes(uh, zh), lanes(ul, zl))
        yv_ref[node] = rows(pack(y), pack(v))
        p_ref[node] = p
        a_ref[node] = t
        c_ref[node] = c
        j_ref[node] = j


def entries_of(level, half, steps, first, unit, refs, below):
    found = []
    for at_level, at in path_steps(half, steps, first):
        if at_level != level:
            continue
        node = at // (2 << level)
        if level == 0:
            eye = identity()
            start = jnp.where(unit * half + at == 0, 1.0, 0.0).astype(f32)
            c1 = below + start * (eye - below)
        else:
            c1 = below[2 * node]
        found.append(level_entry(refs, level, node, c1))
    return found


def panel_vectors(half, rows_own, unit, place, panel_in, mask_ref, weight_ref, panel_ref, all_ref, leaf_ref):
    total = panel_ref.shape[1]
    n_blocks = weight_ref.shape[0]
    n_time = panel_in.shape[0] // (2 * rows_own)
    for k in range(2 * n_time):
        core, chip, hop = (1 - unit if k % 2 else unit), place, n_time // 2
        for bit in range(1, n_time.bit_length()):
            if (k >> bit) % 2:
                chip = jnp.bitwise_xor(chip, hop)
            hop = hop // 2
        at = pl.multiple_of((2 * chip + core) * rows_own, rows_own)
        panel_ref[pl.ds(at, rows_own), :] = panel_in[k * rows_own:(k + 1) * rows_own, :]
    turned = jnp.zeros((WIDTH, total), f32)
    for block in range(n_blocks):
        mask = mask_ref[block:block + 1, :]
        turned = turned + mm(weight_ref[block], mask * panel_ref[block * WIDTH:(block + 1) * WIDTH, :])
    late = pltpu.roll(jnp.transpose(turned), 1, 0)
    all_ref[...] = late
    all_ref[0:1, :] = jnp.zeros((1, WIDTH), f32)
    leaf = all_ref[pl.ds(pl.multiple_of(unit * half, half), half), :]
    leaf_ref[...] = leaf
    return late[0:1, :], leaf


def vector_level(level, half, prior, gain_refs, leaf, bs, es):
    uz_ref, yv_ref = gain_refs
    stride = 1 << level
    zero = jnp.zeros((1, WIDTH), f32)
    for node in range(half >> (level + 1)):
        if node and node % 4 == 0:
            yield
        at = (2 * node + 1) * stride - 1
        if level == 0:
            b1, b2 = (prior if node == 0 else zero), zero
            e1, e2 = leaf[at:at + 1, :], leaf[at + 1:at + 2, :]
            if node > 0:
                high, low = split(e2)
                both = rows(high, low)
                out = mm_nt(both, uz_ref[node, :, WIDTH:])
                bs[at] = out[0:1, :WIDTH] + out[1:2, :WIDTH] + out[0:1, WIDTH:]
                out = mm(both, yv_ref[node, WIDTH:, :])
                es[at] = e1 + out[0:1, :WIDTH] + out[1:2, :WIDTH] + out[0:1, WIDTH:]
                continue
        else:
            one, two = at - stride // 2, at + stride // 2
            b1, b2, e1, e2 = bs[one], bs[two], es[one], es[two]
        high, low = split(lanes(b1, e2))
        out = mm_nt(rows(high, low), uz_ref[node])
        bs[at] = b2 + out[0:1, :WIDTH] + out[1:2, :WIDTH] + out[0:1, WIDTH:]
        high, low = split(lanes(-b1, e2))
        out = mm(rows(high, low), yv_ref[node])
        es[at] = e1 + out[0:1, :WIDTH] + out[1:2, :WIDTH] + out[0:1, WIDTH:]


def up_kernel(joins, half, steps, rows_own, index_ref, const_ref, *refs):
    unit, place = index_ref[0], index_ref[1]
    n_levels = half.bit_length() - 1
    low = joins[0]
    held = {}
    refs = list(refs)
    if rows_own:
        panel_in, mask_ref, weight_ref = refs[:3]
        refs = refs[3:]
        gain_refs, refs = refs[:2 * (low - 1)], refs[2 * (low - 1):]
        panel_ref, all_ref = refs[-2:]
        leaf_ref, b_ref, e_ref, vmessage_ref = refs[-7:-3]
        refs = refs[:-7] + refs[-3:-2]
    if low > 1:
        below_ref = refs.pop(0)
    held[low - 1], refs = refs[:LEVEL_ARRAYS], refs[LEVEL_ARRAYS:]
    outs = {}
    for level in joins:
        held[level], refs = refs[:LEVEL_ARRAYS], refs[LEVEL_ARRAYS:]
        outs[level], refs = refs[:3], refs[3:]
    acc_ref, = refs
    eye = identity()

    def children(level, node):
        _, _, a_ref, c_ref, j_ref, _ = held[level - 1]
        return tuple((a_ref[k], c_ref[k], j_ref[k]) for k in (2 * node, 2 * node + 1))

    def condition_inputs(level):
        if level == 0:
            below = const_ref[1]
        elif level == low - 1:
            below = below_ref
        else:
            below = held[level - 1][3]
        return entries_of(level, half, steps, place * steps, unit, held[level], below)

    def store(level, results):
        for slot, result in enumerate(results):
            for ref, value in zip(outs[level], result):
                ref[slot] = value

    def sweep(fast, beside=iter(())):
        for level in joins:
            count = half >> (level + 1)
            under = level - 1
            if fast and count <= GROUP:
                nodes = list(range(count))
                entries = condition_inputs(under)
                pairs = [children(level, node) for node in nodes]
                items = [join_item(level, pair, eye) for pair in pairs]
                extra = [condition_item(under, entry, eye) for entry in entries]
                inverses = invert(items + [item for item, _ in extra], eye, True, acc_ref, beside=beside)
                results, seen = [], []
                in_turns(
                    joining(level, pairs, inverses[:count], eye, results),
                    conditioning(entries, [scale for _, scale in extra], inverses[count:], seen),
                    beside,
                )
                store_joined(held[level], nodes, inverses[:count], results)
                store(level, seen)
                continue
            group = min(count, GROUP) if fast else 1

            def some(block, carry):
                nodes = [block * group + k for k in range(group)]
                pairs = [children(level, node) for node in nodes]
                inverses = invert([join_item(level, pair, eye) for pair in pairs], eye, fast, acc_ref)
                results = []
                in_turns(joining(level, pairs, inverses, eye, results))
                store_joined(held[level], nodes, inverses, results)
                return carry

            lax.fori_loop(0, count // group, some, 0)
            entries = condition_inputs(under)
            extra = [condition_item(under, entry, eye) for entry in entries]
            inverses = invert([item for item, _ in extra], eye, fast, acc_ref)
            seen = []
            in_turns(conditioning(entries, [scale for _, scale in extra], inverses, seen))
            store(level, seen)

    if not rows_own:
        checked(sweep, acc_ref)
        return
    prior = jnp.where(unit == 0, 1.0, 0.0) * const_ref[0, 0:1, :]
    gains = [gain_refs[2 * level:2 * level + 2] for level in range(low - 1)] + [held[low - 1][:2]]
    bs, es, found = {}, {}, []

    def means():
        found.extend(panel_vectors(
            half, rows_own, unit, index_ref[3], panel_in, mask_ref, weight_ref, panel_ref, all_ref, leaf_ref
        ))
        yield
        for level in range(low):
            yield from vector_level(level, half, prior, gains[level], found[1], bs, es)
            yield

    pieces = means()
    checked(sweep, acc_ref, beside=pieces)
    for _ in pieces:
        pass
    end, leaf = found
    for level in range(low, n_levels):
        in_turns(vector_level(level, half, prior, held[level][:2], leaf, bs, es))
    for at in bs:
        b_ref[at:at + 1, :] = bs[at]
        e_ref[at:at + 1, :] = es[at]
    top = half // 2 - 1
    vmessage_ref[...] = rows(bs[top], es[top], end, jnp.zeros((5, WIDTH), f32))


SMEM = pl.BlockSpec(memory_space=pltpu.SMEM)
VMEM = pl.BlockSpec(memory_space=pltpu.VMEM)


ANY = pl.BlockSpec(memory_space=pl.ANY)


def level_shapes(half, level):
    count = half >> (level + 1)
    mat = (count, WIDTH, WIDTH)
    wide = (count, 2 * WIDTH, 2 * WIDTH)
    return [jax.ShapeDtypeStruct(wide, bf16)] * 2 + [jax.ShapeDtypeStruct(mat, f32)] * 4


def path_shapes(half, steps, level):
    count = len([k for k, _ in path_steps(half, steps, 0) if k == level])
    return [
        jax.ShapeDtypeStruct((count, 2 * WIDTH, 2 * WIDTH), bf16),
        jax.ShapeDtypeStruct((count, WIDTH, WIDTH), f32),
        jax.ShapeDtypeStruct((count, 3 * WIDTH, 2 * WIDTH), bf16),
    ]


def estimate(matrices):
    return pl.CostEstimate(flops=matrices * 600 * WIDTH**3, transcendentals=0, bytes_accessed=1 << 20)


def first_sweep(half, index, cell_mask, loadings, prec_rows, transition, var_row, prior_row):
    mat = (WIDTH, WIDTH)
    n_blocks = loadings.shape[0] // WIDTH
    outs = [
        jax.ShapeDtypeStruct((n_blocks,) + mat, bf16),
        jax.ShapeDtypeStruct(mat, f32),
        jax.ShapeDtypeStruct(cell_mask.shape, bf16),
        jax.ShapeDtypeStruct((2,) + mat, f32),
    ] + level_shapes(half, 0)
    inputs = [
        pltpu.with_memory_space_constraint(array, pltpu.HBM)
        for array in (cell_mask, loadings, prec_rows, transition, var_row, prior_row)
    ]
    return pl.pallas_call(
        functools.partial(first_kernel, half),
        out_shape=outs,
        in_specs=[SMEM] + [ANY] * 6,
        out_specs=[VMEM] * len(outs),
        scratch_shapes=[
            pltpu.VMEM((n_blocks,) + mat, f32),
            pltpu.VMEM((8, WIDTH), f32),
            pltpu.SMEM(cell_mask.shape, jnp.int32),
            pltpu.VMEM(cell_mask.shape, jnp.int32),
            pltpu.VMEM(loadings.shape, bf16),
            pltpu.VMEM(prec_rows.shape, f32),
            pltpu.VMEM((4,) + mat, f32),
            pltpu.VMEM((2, 1, WIDTH), f32),
            pltpu.SemaphoreType.DMA((7,)),
        ],
        compiler_params=pltpu.CompilerParams(vmem_limit_bytes=VMEM_LIMIT),
        cost_estimate=estimate(half // 2),
        name="first_sweep",
    )(index, *inputs)


def up_sweep(joins, half, steps, index, consts, held, rows_own=0, vectors=()):
    low = joins[0]
    operands = ([held[low - 2][3]] if low > 1 else []) + list(held[low - 1])
    outs = []
    for level in joins:
        outs += level_shapes(half, level) + path_shapes(half, steps, level - 1)
    scratch = [pltpu.VMEM((8, WIDTH), f32)]
    if rows_own:
        panel = vectors[0]
        operands = list(vectors) + [array for level in held[:-1] for array in level[:2]] + operands
        row = jax.ShapeDtypeStruct((half, WIDTH), f32)
        outs += [row, row, row, jax.ShapeDtypeStruct((8, WIDTH), f32)]
        scratch += [pltpu.VMEM((panel.shape[1], WIDTH), f32)]
        scratch = scratch[:1] + [pltpu.VMEM(panel.shape, bf16)] + scratch[1:]
    results = pl.pallas_call(
        functools.partial(up_kernel, joins, half, steps, rows_own),
        out_shape=outs,
        in_specs=[SMEM] + [VMEM] * (1 + len(operands)),
        out_specs=[VMEM] * len(outs),
        scratch_shapes=scratch,
        compiler_params=pltpu.CompilerParams(vmem_limit_bytes=VMEM_LIMIT),
        cost_estimate=estimate(sum(half >> level for level in joins)),
        name="up_sweep_%d" % low,
    )(index, consts, *operands)
    results = list(results)
    step = LEVEL_ARRAYS + 3
    parts = [results[k * step:(k + 1) * step] for k in range(len(joins))]
    return [part[:LEVEL_ARRAYS] for part in parts], [part[LEVEL_ARRAYS:] for part in parts], results[len(joins) * step:]


def down_kernel(steps, index_ref, own_ref, other_ref, end_ref, vown_ref, vother_ref, const_ref, leaf_ref, b_ref, e_ref, below_ref,
                *refs):
    refs = list(refs)
    top_refs, refs = refs[:LEVEL_ARRAYS], refs[LEVEL_ARRAYS:]
    out_ref, acc_ref, top_ref, gt_ref, cond_ref, shift_ref = refs[-6:]
    path_refs = refs[:-6]
    unit, place = index_ref[0], index_ref[1]
    half = leaf_ref.shape[0]
    n_levels = half.bit_length() - 1
    eye = identity()
    flag = jnp.where(unit == 0, 1.0, 0.0).astype(f32)

    def pick(zero, one):
        return flag * zero + (1.0 - flag) * one

    cov0 = pick(own_ref[1], other_ref[1])
    trans1, cov1, info1 = [pick(other_ref[k], own_ref[k]) for k in range(3)]
    b0 = pick(vown_ref[0:1, :], vother_ref[0:1, :])
    b1, e1 = [pick(vother_ref[k:k + 1, :], vown_ref[k:k + 1, :]) for k in range(2)]
    e_end = vown_ref[2:3, :]
    end = end_ref[...]

    first = place * steps

    def roots(fast, beside=iter(())):
        under = n_levels - 1
        entries = entries_of(under, half, steps, first, unit, top_refs, below_ref)
        extra = [condition_item(under, entry, eye) for entry in entries]
        item = (eye + mm3(cov0, info1), bounds_at(JOIN_BOUNDS, n_levels), False)
        ready = mm3_nt(cov0, trans1)
        ready_end, cov1_end = mm3(ready, end), mm3(cov1, end)
        (p, *inverses), sides = invert([item] + [item for item, _ in extra], eye, fast, acc_ref, True, beside)
        u = times_inverse(trans1, sides[0])
        last = eye + cov1_end + mm3(u, ready_end)
        cov = cov1 + mm3(u, ready)
        z = mm3(u, cov0)
        kept = mm3(p, cov0)
        results = []
        in_turns(conditioning(entries, [scale for _, scale in extra], inverses, results), beside)
        for slot, result in enumerate(results):
            for ref, value in zip((gt_ref, cond_ref, shift_ref), result):
                ref[slot] = value
        info_z = mm3(jnp.transpose(z), end)
        _, (side,) = invert([(last, bounds_at(JOIN_BOUNDS, 0), False)], eye, fast, acc_ref, True)
        top_ref[0], top_ref[1] = inverse_times(side, cov, eye), inverse_times(side, z, eye)
        top_ref[2] = kept - mm3(info_z, top_ref[1])
        top_ref[3] = p

    prior = flag * const_ref[0, 0:1, :]
    path = path_steps(half, steps, first)
    levels = [(gt_ref, cond_ref, shift_ref)] + [path_refs[k:k + 3] for k in range(0, len(path_refs), 3)]
    places, seen = [], {}
    for level, _ in path:
        seen[level] = seen.get(level, -1) + 1
        places.append((levels[n_levels - 1 - level], seen[level]))

    def shift(slot):
        level, at = path[slot]
        row_of = lambda ref, k: ref[pl.ds(k, 1), :]
        if level == 0:
            one, two = jnp.where(at == 0, 1.0, 0.0) * prior, row_of(leaf_ref, at + 1)
        else:
            near = (1 << level) // 2
            one, two = row_of(b_ref, at - near), row_of(e_ref, at + near)
        high, low = split(lanes(one, two, row_of(b_ref, at)))
        arrays, own = places[slot]
        out = mm(rows(high, low), arrays[2][own])
        return out[0:1, :WIDTH] + out[1:2, :WIDTH] + out[0:1, WIDTH:]

    shifts = {}

    def shifting():
        for slot, (level, _) in enumerate(path):
            if level < n_levels - 1:
                shifts[slot] = shift(slot)
                yield

    pieces = shifting()
    checked(roots, acc_ref, beside=pieces)
    for _ in pieces:
        pass
    shifts[0] = shift(0)
    cov_top, cov_cross, cov_mid, p = [top_ref[k] for k in range(4)]
    mean_mid = mm3_nt(b0 + mm3(e1, cov0), p)
    b_end = mm3_nt(mean_mid, trans1) + b1
    news = e_end - mm3(b_end, end)
    mean_top = b_end + mm3_nt(news, cov_top)
    mean_mid = mean_mid + mm3(news, cov_cross)
    keep = 1.0 - flag
    joint = rows(
        lanes(keep * cov_mid, keep * jnp.transpose(cov_cross)),
        lanes(keep * cov_cross, pick(cov_mid, cov_top)),
    )
    means = lanes(keep * mean_mid, pick(mean_mid, mean_top))

    def nodes(slots, joints, means, leaf):
        packs = [places[slot][0][0][places[slot][1]] for slot in slots]
        conds = [places[slot][0][1][places[slot][1]] for slot in slots]
        halves = [split(joint) for joint in joints]
        crosses = [
            mm(lanes(jh, jl), rows(g[:, :WIDTH], g[:, :WIDTH])) + mm(jh, g[:, WIDTH:])
            for (jh, jl), g in zip(halves, packs)
        ]
        outs = [mm(rows(*split(mean)), g) for mean, g in zip(means, packs)]
        found = [
            shifts[slot] + out[0:1, :WIDTH] + out[1:2, :WIDTH] + out[0:1, WIDTH:] for slot, out in zip(slots, outs)
        ]
        gains = [unpack(g) for g in packs]
        if leaf:
            owns = [
                diagonal(cond, eye) + jnp.sum(gain * cross, axis=0, keepdims=True)
                for cond, gain, cross in zip(conds, gains, crosses)
            ]
        else:
            owns = [cond + mm3(jnp.transpose(gain), cross) for cond, gain, cross in zip(conds, gains, crosses)]
        return list(zip(found, owns, crosses))

    def left_pair(joint, means, mean, own, cross):
        c = cross[:WIDTH]
        return rows(lanes(joint[:WIDTH, :WIDTH], c), lanes(jnp.transpose(c), own)), lanes(means[:, :WIDTH], mean)

    def right_pair(joint, means, mean, own, cross):
        c = cross[WIDTH:]
        return rows(lanes(own, jnp.transpose(c)), lanes(c, joint[WIDTH:, WIDTH:])), lanes(mean, means[:, WIDTH:])

    slot = 0
    while path[slot][0] >= steps.bit_length() - 1:
        result, = nodes([slot], [joint], [means], False)
        go_right = jnp.where(first > path[slot][1], 1.0, 0.0).astype(f32)
        lj, lm = left_pair(joint, means, *result)
        rj, rm = right_pair(joint, means, *result)
        joint = go_right * rj + (1.0 - go_right) * lj
        means = go_right * rm + (1.0 - go_right) * lm
        slot += 1

    out_ref[steps - 1:steps, :] = means[:, WIDTH:]
    out_ref[2 * steps - 1:2 * steps, :] = diagonal(joint[WIDTH:, WIDTH:], eye)
    todo = [(0, joint, means)]
    count = steps
    while todo:
        stride, later = count // 2, []
        leaf = stride == 1
        results = nodes(
            range(slot, slot + len(todo)), [joint for _, joint, _ in todo], [means for _, _, means in todo], leaf
        )
        slot += len(todo)
        for (low, joint, means), result in zip(todo, results):
            at = low + stride - 1
            out_ref[at:at + 1, :] = result[0]
            out_ref[steps + at:steps + at + 1, :] = result[1] if leaf else diagonal(result[1], eye)
            if not leaf:
                later.append((low,) + left_pair(joint, means, *result))
                later.append((low + stride,) + right_pair(joint, means, *result))
        todo, count = later, stride


def down_sweep(steps, half, *operands):
    return pl.pallas_call(
        functools.partial(down_kernel, steps),
        out_shape=jax.ShapeDtypeStruct((2 * steps, WIDTH), f32),
        in_specs=[SMEM] + [VMEM] * (len(operands) - 1),
        out_specs=VMEM,
        scratch_shapes=[pltpu.VMEM((8, WIDTH), f32), pltpu.VMEM((6, WIDTH, WIDTH), f32)]
        + [pltpu.VMEM(shape.shape, shape.dtype) for shape in path_shapes(half, steps, half.bit_length() - 2)],
        compiler_params=pltpu.CompilerParams(vmem_limit_bytes=VMEM_LIMIT),
        name="down_sweep",
    )(*operands)


def redundant(panel_data, cell_mask, loadings, noise_prec, transition, proc_var, prior_mean):
    n_time = lax.axis_size("tm")
    n_unit = lax.axis_size("unit")
    place, unit = lax.axis_index("tm"), lax.axis_index("unit")
    total = panel_data.shape[1]
    half = total // n_unit
    steps = total // n_time
    per_half = half // steps
    index = jnp.stack([unit, place % per_half, n_unit, place]).astype(jnp.int32)
    swap = [(0, 1), (1, 0)]

    def swapped(value, other):
        return lax.ppermute(value, "tm", [(k, k ^ other) for k in range(n_time)])

    n_levels = half.bit_length() - 1
    hops = [1 << k for k in reversed(range(n_time.bit_length() - 1))]
    weighted, end, mask, consts, *level0 = first_sweep(
        half, index, cell_mask, loadings, noise_prec.reshape(-1, WIDTH), transition,
        proc_var.reshape(1, WIDTH), prior_mean.reshape(1, WIDTH),
    )
    held, paths = [level0], []
    panel = jnp.concatenate([panel_data, lax.ppermute(panel_data, "unit", swap)])
    cuts = [[1], [2], [3], list(range(4, n_levels))]
    for k, joins in enumerate(cuts):
        panel, held[-1] = lax.optimization_barrier((panel, held[-1]))
        last = k + 1 == len(cuts)
        extra = (panel_data.shape[0], (panel, mask, weighted)) if last else ()
        new, path, rest = up_sweep(joins, half, steps, index, consts, held, *extra)
        if not last:
            panel = jnp.concatenate([panel, swapped(panel, hops[k])])
        held += new
        paths += path
    leaves, bs, es, vmessage = rest
    message = jnp.concatenate(held[-1][2:5])
    other = lax.ppermute(message, "unit", swap)
    vother = lax.ppermute(vmessage, "unit", swap)
    mine = down_sweep(
        steps, half, index, message, other, end, vmessage, vother, consts, leaves, bs, es, held[-2][3], *held[-1],
        *[array for path in reversed(paths) for array in path],
    )
    theirs = lax.ppermute(mine, "unit", swap)
    out = jnp.where(unit == place // per_half, mine, theirs)
    return out[:steps], out[steps:]


BLOCK = 128


def carried_in(value, axis, join, neutral, backward):
    count, mine = (lax.axis_size(axis), lax.axis_index(axis))
    pieces = jax.tree.map(lambda part: lax.all_gather(part, axis), value)
    if backward:
        pieces = jax.tree.map(lambda part: part[::-1], pieces)
        mine = count - 1 - mine
    running = jax.tree.map(
        lambda part, zero: jnp.full_like(part, 0) + jnp.asarray(zero, part.dtype), value, neutral
    )

    def step(position, running):
        longer = join(running, jax.tree.map(lambda part: part[position], pieces))
        return jax.tree.map(lambda new, old: jnp.where(position < mine, new, old), longer, running)

    return lax.fori_loop(0, count - 1, step, running)


def product(left, right):
    return jnp.matmul(left, right, precision=HIGHEST)


def mat_vec(matrix, vector):
    return jnp.einsum("...kl,...l->...k", matrix, vector, precision=HIGHEST)


def flipped(matrix):
    return jnp.swapaxes(matrix, -1, -2)


def chol_apply(factor, rhs):
    middle = lax.linalg.triangular_solve(factor, rhs, left_side=True, lower=True)
    return lax.linalg.triangular_solve(factor, middle, left_side=True, lower=True, transpose_a=True)


def filter_join(earlier, later):
    trans_one, shift_one, cov_one, info_one, vec_one, live_one = earlier
    trans_two, shift_two, cov_two, info_two, vec_two, live_two = later
    identity_mat = jnp.eye(trans_one.shape[-1], dtype=jnp.float32)
    live_mat = live_one[..., None, None]
    factor_one = jnp.linalg.cholesky(cov_one + (1.0 - live_mat) * identity_mat)
    inner_mat = identity_mat + product(product(flipped(factor_one), info_two), factor_one)
    inner_factor = jnp.linalg.cholesky(inner_mat)
    solved = lax.linalg.triangular_solve(
        inner_factor, flipped(factor_one), left_side=True, lower=True
    )
    spread_mat = product(trans_two, flipped(solved))
    pushed = product(info_two, trans_one)
    reduced = product(solved, pushed)
    residue = vec_two - mat_vec(info_two, shift_one)
    solved_residue = mat_vec(solved, residue)
    trans_new = product(trans_two, trans_one) - product(spread_mat, reduced)
    shift_new = mat_vec(trans_two, shift_one) + mat_vec(spread_mat, solved_residue) + shift_two
    cov_new = product(spread_mat, flipped(spread_mat)) + cov_two
    info_new = product(flipped(trans_one), pushed) - product(flipped(reduced), reduced) + info_one
    vec_new = (
        mat_vec(flipped(trans_one), residue) - mat_vec(flipped(reduced), solved_residue) + vec_one
    )
    alive_mat = live_mat > 0.5
    alive_vec = live_one[..., None] > 0.5
    return (
        jnp.where(alive_mat, trans_new, trans_two),
        jnp.where(alive_vec, shift_new, shift_two),
        jnp.where(alive_mat, cov_new, cov_two),
        jnp.where(alive_mat, info_new, info_two),
        jnp.where(alive_vec, vec_new, vec_two),
        jnp.maximum(live_one, live_two),
    )


def smooth_join(lower_elem, higher_elem):
    gain_low, offset_low, cov_low = lower_elem
    gain_high, offset_high, cov_high = higher_elem
    return (
        product(gain_low, gain_high),
        mat_vec(gain_low, offset_high) + offset_low,
        product(product(gain_low, cov_high), flipped(gain_low)) + cov_low,
    )


def smooth_scan_join(earlier, later):
    return smooth_join(later, earlier)


def take_last(stacked):
    return stacked[-1]


def take_first(stacked):
    return stacked[0]


def per_device(panel_data, cell_mask, loadings, noise_prec, transition, proc_var, prior_mean):
    n_time = lax.axis_size("tm")
    n_unit = lax.axis_size("unit")
    time_index = lax.axis_index("tm")
    unit_index = lax.axis_index("unit")
    rows_own, total_time = panel_data.shape
    steps = total_time // n_time
    width = transition.shape[0]
    identity_mat = jnp.eye(width, dtype=jnp.float32)
    my_columns = lax.dynamic_slice_in_dim(cell_mask, time_index * steps, steps, 1)
    half_load = lax.dynamic_index_in_dim(
        loadings.reshape(n_time, n_unit, rows_own, width), unit_index, 1, keepdims=False
    ).reshape(n_time * rows_own, width)
    half_prec = lax.dynamic_index_in_dim(
        noise_prec.reshape(n_time, n_unit, rows_own), unit_index, 1, keepdims=False
    ).reshape(n_time * rows_own)
    half_ids = (
        (jnp.arange(n_time, dtype=jnp.int32)[:, None] * n_unit + unit_index) * rows_own
        + jnp.arange(rows_own, dtype=jnp.int32)[None, :]
    ).reshape(-1)
    half_weighted = (half_prec[:, None] * half_load.astype(jnp.float32)).astype(jnp.bfloat16)
    half_mask = jnp.take(my_columns, half_ids // BLOCK, axis=0).astype(jnp.bfloat16)
    regrouped = lax.all_to_all(panel_data, "tm", split_axis=1, concat_axis=0, tiled=True)
    vec_half = jnp.dot((half_mask * regrouped).T, half_weighted, preferred_element_type=jnp.float32)
    group_rows = min(rows_own, BLOCK)
    n_groups = n_time * rows_own // group_rows
    group_gram = jnp.einsum(
        "gnk,gnl->gkl",
        half_weighted.reshape(n_groups, group_rows, width),
        half_load.reshape(n_groups, group_rows, width),
        preferred_element_type=jnp.float32,
    )
    group_block = half_ids.reshape(n_groups, group_rows)[:, 0] // BLOCK
    group_mask = jnp.take(my_columns, group_block, axis=0).astype(jnp.float32)
    info_half = jnp.einsum("gt,gkl->tkl", group_mask, group_gram, precision=HIGHEST)
    info_mat, info_vec = lax.psum((info_half, vec_half), "unit")
    global_step = time_index * steps + jnp.arange(steps, dtype=jnp.int32)
    first_step = (global_step == 0).astype(jnp.float32)
    keep_step = 1.0 - first_step
    last_keep = 1.0 - (global_step == total_time - 1).astype(jnp.float32)
    inv_var = 1.0 / proc_var
    prior_prec = first_step[:, None, None] * identity_mat + keep_step[:, None, None] * jnp.diag(
        inv_var
    )
    eyes = jnp.broadcast_to(identity_mat, info_mat.shape)
    post_cov = chol_apply(jnp.linalg.cholesky(prior_prec + info_mat), eyes)
    shift_vec = jnp.einsum(
        "skl,sl->sk",
        post_cov,
        info_vec + first_step[:, None] * prior_mean[None, :],
        precision=HIGHEST,
    )
    scaled_trans = inv_var[:, None] * transition
    trans_part = keep_step[:, None, None] * jnp.einsum(
        "skl,lm->skm", post_cov, scaled_trans, precision=HIGHEST
    )
    middle = jnp.diag(inv_var)[None] - inv_var[None, :, None] * post_cov * inv_var[None, None, :]
    pressed = jnp.einsum("slm,mn->sln", middle, transition, precision=HIGHEST)
    info_part = keep_step[:, None, None] * jnp.einsum(
        "lk,sln->skn", transition, pressed, precision=HIGHEST
    )
    vec_part = keep_step[:, None] * jnp.einsum(
        "lk,sl->sk", transition, inv_var[None, :] * shift_vec, precision=HIGHEST
    )
    elements = (
        trans_part,
        shift_vec,
        post_cov,
        info_part,
        vec_part,
        jnp.ones((steps,), jnp.float32),
    )
    zero_vec = jnp.zeros((width,), jnp.float32)
    zero_mat = jnp.zeros((width, width), jnp.float32)
    filter_identity = (identity_mat, zero_vec, zero_mat, zero_mat, zero_vec, jnp.float32(0.0))
    local_joined = lax.associative_scan(filter_join, elements)
    filter_total = jax.tree.map(take_last, local_joined)
    before = carried_in(filter_total, "tm", filter_join, filter_identity, False)
    filtered = jax.vmap(filter_join, in_axes=(None, 0))(before, local_joined)
    filt_mean = filtered[1]
    filt_cov = filtered[2]
    moved_cov = jnp.einsum("kl,slm->skm", transition, filt_cov, precision=HIGHEST)
    pred_next = (
        jnp.einsum("skm,nm->skn", moved_cov, transition, precision=HIGHEST)
        + jnp.diag(proc_var)[None]
    )
    gain = (
        jnp.transpose(chol_apply(jnp.linalg.cholesky(pred_next), moved_cov), (0, 2, 1))
        * last_keep[:, None, None]
    )
    moved_mean = jnp.einsum("kl,sl->sk", transition, filt_mean, precision=HIGHEST)
    offset = filt_mean - jnp.einsum("skl,sl->sk", gain, moved_mean, precision=HIGHEST)
    resid_cov = filt_cov - jnp.einsum("skl,slm->skm", gain, moved_cov, precision=HIGHEST)
    smooth_identity = (identity_mat, zero_vec, zero_mat)
    local_suffix = lax.associative_scan(smooth_scan_join, (gain, offset, resid_cov), reverse=True)
    smooth_total = jax.tree.map(take_first, local_suffix)
    after = carried_in(smooth_total, "tm", smooth_scan_join, smooth_identity, True)
    smoothed = jax.vmap(smooth_join, in_axes=(0, None))(local_suffix, after)
    smoothed_mean = smoothed[1]
    smoothed_var = jnp.diagonal(smoothed[2], axis1=1, axis2=2)
    return (smoothed_mean, smoothed_var)


def per_device_any(*arrays):
    fits = arrays[0].shape[1] <= 64 * lax.axis_size("unit") and lax.axis_size("unit") == 2
    return redundant(*arrays) if fits else per_device(*arrays)


def solution(mesh):
    return jax.shard_map(
        per_device_any,
        mesh=mesh,
        in_specs=(P(("grp", "tm", "unit"), None), P("grp", None), P(), P(), P(), P(), P()),
        out_specs=(P(("grp", "tm"), None), P(("grp", "tm"), None)),
        check_vma=False,
    )
```

```python
import functools

import jax
import jax.numpy as jnp
from jax import lax
from jax.experimental import pallas as pl
from jax.experimental.pallas import tpu as pltpu
from jax.sharding import PartitionSpec as P

f32 = jnp.float32
bf16 = jnp.bfloat16
WIDTH = 128
HIGHEST = lax.Precision.HIGHEST
VMEM_LIMIT = 30 << 20
RESIDUAL_MAX = 7e-3
GROUP = 16
JOIN_BOUNDS = ((1.0, 4.0), (1.0, 5.2), (1.0, 5.2), (1.0, 6.0), (1.0, 10.0), (1.0, 13.0))
COV_BOUNDS = ((0.70, 1.37), (0.50, 1.90), (0.31, 2.85), (0.19, 4.50), (0.12, 6.30))


def schedule(bounds, goal=2.5e-3):
    low, high = bounds
    alpha, radius, factors = 2.0 / (low + high), (high - low) / (high + low), []
    while radius > goal:
        square = radius * radius
        factors.append(2.0 / (2.0 - square))
        radius = square / (2.0 - square)
    return alpha, factors


def bounds_at(table, level):
    return table[min(level, len(table) - 1)]


def mm(left, right):
    return lax.dot_general(left, right, (((1,), (0,)), ((), ())), preferred_element_type=f32)


def mm_nt(left, right):
    return lax.dot_general(left, right, (((1,), (1,)), ((), ())), preferred_element_type=f32)


def split(value):
    high = value.astype(bf16)
    return high, (value - high.astype(f32)).astype(bf16)


def lanes(*parts):
    return jnp.concatenate(parts, axis=1)


def rows(*parts):
    return jnp.concatenate(parts, axis=0)


def mm3(left, right):
    lh, ll = split(left)
    rh, rl = split(right)
    return mm(lanes(lh, ll), rows(rh, rh)) + mm(lh, rl)


def mm3_nt(left, right):
    lh, ll = split(left)
    rh, rl = split(right)
    return mm_nt(lanes(lh, ll), lanes(rh, rh)) + mm_nt(lh, rl)


def identity():
    shape = (WIDTH, WIDTH)
    return (lax.broadcasted_iota(jnp.int32, shape, 0) == lax.broadcasted_iota(jnp.int32, shape, 1)).astype(f32)


def squares(value):
    return jnp.sum((value * value).reshape(WIDTH // 8, 8, WIDTH), axis=0)


def fast_inverses(items, eye, beside=iter(())):
    mats = [mat for mat, _, _ in items]
    plans = [schedule(bounds) for _, bounds, _ in items]
    n = range(len(items))
    halves = [split(mat) for mat in mats]
    rest = [eye - plan[0] * mat for plan, mat in zip(plans, mats)]
    guess = [(plan[0] * plan[1][0]) * (eye + r) for plan, r in zip(plans, rest)]
    for step in range(max(len(factors) for _, factors in plans)):
        rest_b = [r.astype(bf16) for r in rest]
        guess_b = [g.astype(bf16) for g in guess]
        for k in n:
            factors = plans[k][1]
            more = step + 1 < len(factors)
            if step >= len(factors):
                continue
            factor = factors[step]
            if step == 0:
                if more:
                    rest[k] = (1.0 - factor) * eye + factor * mm(rest_b[k], rest_b[k])
            elif more:
                out = mm(rest_b[k], lanes(guess_b[k], rest_b[k]))
                guess[k] = factor * (guess[k] + out[:, :WIDTH])
                rest[k] = (1.0 - factor) * eye + factor * out[:, WIDTH:]
            else:
                guess[k] = factor * (guess[k] + mm(rest_b[k], guess_b[k]))
        next(beside, None)
    guess_b = [g.astype(bf16) for g in guess]
    resid = [eye - mm(lanes(h, l), rows(g, g)) for (h, l), g in zip(halves, guess_b)]
    guess = [g.astype(f32) + mm(g, e.astype(bf16)) for g, e in zip(guess_b, resid)]
    next(beside, None)
    sides = [(g, e.astype(bf16)) for g, e in zip(guess_b, resid)]
    again = [k for k in n if items[k][2]]
    fine = {k: eye - mm3(mats[k], guess[k]) for k in again}
    for k in again:
        resid[k] = fine[k]
        guess[k] = guess[k] + mm(guess[k].astype(bf16), fine[k].astype(bf16))
        sides[k] = (guess[k], None)
    worst = squares(resid[0])
    for e in resid[1:]:
        worst = jnp.maximum(worst, squares(e))
    return guess, sides, worst


def safe_inverse(mat, eye):
    size = jnp.max(jnp.sum(jnp.abs(mat), axis=0, keepdims=True), axis=1, keepdims=True)
    product = functools.partial(jnp.dot, precision=HIGHEST, preferred_element_type=f32)

    def unfinished(state):
        step, size, _ = state
        return jnp.logical_and(step < 64, jnp.logical_not(size <= 1e-7))

    def improve(state):
        step, _, guess = state
        resid = eye - product(mat, guess)
        return step + 1, jnp.sum(squares(resid)), guess + product(guess, resid)

    return lax.while_loop(unfinished, improve, (0, f32(jnp.inf), eye / size))[2]


def diagonal(mat, eye):
    return jnp.sum(mat * eye, axis=0, keepdims=True)


def scaled(mat, eye):
    row = 1.0 / diagonal(mat, eye)
    return mat * row, row


def pack(value):
    return lanes(*split(value))


def unpack(value):
    return value[:, :WIDTH].astype(f32) + value[:, WIDTH:].astype(f32)


def path_steps(half, steps, first):
    found = []
    for level in reversed(range(half.bit_length() - 1)):
        stride = 1 << level
        if 2 * stride > steps:
            found.append((level, (first // (2 * stride)) * (2 * stride) + stride - 1))
        else:
            found += [(level, first + (2 * k + 1) * stride - 1) for k in range(steps // (2 * stride))]
    return found


def join_item(level, pair, eye):
    (_, c1, _), (_, _, j2) = pair
    return eye + mm3(c1, j2), bounds_at(JOIN_BOUNDS, level), False


def in_turns(*works):
    works = list(works)
    while works:
        for work in tuple(works):
            if next(work, works) is works:
                works.remove(work)


def joining(level, pairs, inverses, eye, results):
    turned = [jnp.transpose(one[0]) for one, two in pairs]
    if level < 2:
        less = [(eye - p).astype(bf16) for p in inverses]
        us = [two[0] - mm(two[0].astype(bf16), d) for (one, two), d in zip(pairs, less)]
        vs = [one[0] - mm(d, one[0].astype(bf16)) for (one, two), d in zip(pairs, less)]
    else:
        us = [mm3(two[0], p) for (one, two), p in zip(pairs, inverses)]
        vs = [mm3(p, one[0]) for (one, two), p in zip(pairs, inverses)]
    yield
    zs = [mm3(u, one[1]) for u, (one, two) in zip(us, pairs)]
    ys = [mm3(two[2], v) for v, (one, two) in zip(vs, pairs)]
    yield
    ts = [mm3(two[0], v) for v, (one, two) in zip(vs, pairs)]
    few = level < 2
    cs = [
        two[1] + (mm_nt(z.astype(bf16), two[0].astype(bf16)) if few else mm3_nt(z, two[0]))
        for z, (one, two) in zip(zs, pairs)
    ]
    yield
    js = [one[2] + (mm(t.astype(bf16), y.astype(bf16)) if few else mm3(t, y)) for t, y, (one, two) in zip(turned, ys, pairs)]
    results += list(zip(us, vs, ts, zs, ys, cs, js))


def condition_item(level, entry, eye):
    mat, scale = scaled(entry["c"], eye)
    return (mat, bounds_at(COV_BOUNDS, level), level > 2), scale


def conditioning(entries, scales, inverses, results):
    zs, vs = [e["z"] for e in entries], [e["v"] for e in entries]
    kepts = [mm3(e["p"], e["c1"]) for e in entries]
    backs = [mm3(jnp.transpose(inverse) * scale, z) for inverse, scale, z in zip(inverses, scales, zs)]
    yield
    forths = [jnp.transpose(back) for back in backs]
    gains = [v - mm3(forth, e["a"]) for v, forth, e in zip(vs, forths, entries)]
    yield
    conds = [kept - mm3(forth, z) for kept, forth, z in zip(kepts, forths, zs)]
    yield
    results += [
        (
            pack(rows(jnp.transpose(gain), back)),
            cond,
            pack(rows(jnp.transpose(e["p"]), jnp.transpose(kept), -back)),
        )
        for e, gain, back, cond, kept in zip(entries, gains, backs, conds, kepts)
    ]


def level_entry(refs, level, node, c1):
    uz_ref, yv_ref, a_ref, c_ref, _, p_ref = refs
    uz = uz_ref[node]
    return dict(
        z=uz[:WIDTH, WIDTH:].astype(f32) + uz[WIDTH:, WIDTH:].astype(f32),
        v=unpack(yv_ref[node, WIDTH:, :]),
        a=a_ref[node],
        c=c_ref[node],
        p=p_ref[node],
        c1=c1,
    )


LEVEL_ARRAYS = 6


def first_kernel(half, index_ref, mask_hbm, load_hbm, prec_hbm, trans_hbm, var_hbm, prior_hbm,
                 weight_ref, end_ref, mask_out, const_ref, uz_ref, yv_ref, a_ref, c_ref, j_ref, p_ref,
                 gram_ref, acc_ref, mask_ref, mask_vmem, load_ref, prec_ref, base_ref, row_ref, sems):
    unit, n_unit = index_ref[0], index_ref[2]
    copies = [
        pltpu.make_async_copy(source, target, sems.at[k])
        for k, (source, target) in enumerate((
            (load_hbm, load_ref), (prec_hbm, prec_ref), (trans_hbm, base_ref.at[0]), (var_hbm, row_ref.at[0]),
            (prior_hbm, row_ref.at[1]), (mask_hbm, mask_ref), (mask_hbm, mask_vmem),
        ))
    ]
    for copy in copies:
        copy.start()
    for copy in copies:
        copy.wait()
    eye = identity()
    n_blocks = load_ref.shape[0] // WIDTH
    for block in range(n_blocks):
        load = load_ref[block * WIDTH:(block + 1) * WIDTH, :]
        weighted = (jnp.transpose(load.astype(f32)) * prec_ref[block:block + 1, :]).astype(bf16)
        weight_ref[block] = weighted
        gram = mm(weighted, load)
        gram_ref[block] = 0.5 * (gram + jnp.transpose(gram))
    base_ref[1] = eye * row_ref[0]
    base_ref[2] = jnp.transpose(base_ref[0])
    base_ref[3] = jnp.transpose(jnp.broadcast_to(row_ref[0], (WIDTH, WIDTH)))
    const_ref[0] = jnp.broadcast_to(row_ref[1], (WIDTH, WIDTH))
    const_ref[1] = base_ref[1]
    mask_out[...] = mask_vmem[...].astype(f32).astype(bf16)

    def info(step):
        out = mask_ref[0, step].astype(f32) * gram_ref[0]
        for block in range(1, n_blocks):
            out = out + mask_ref[block, step].astype(f32) * gram_ref[block]
        return out

    end_ref[...] = info(n_unit * half - 1)

    outs = (uz_ref, yv_ref, a_ref, c_ref, j_ref, p_ref)

    def leaf_joins(nodes, fast):
        trans, noise, turned, column, row = base_ref[0], base_ref[1], base_ref[2], base_ref[3], row_ref[0]
        step = [unit * half + 2 * node for node in nodes]
        start = jnp.where(step[0] == 0, 1.0, 0.0).astype(f32)
        before = [info(jnp.maximum(at - 1, 0)) for at in step]
        before[0] = before[0] * (1.0 - start)
        after = [info(at) for at in step]
        left = [trans * (1.0 - start)] + [trans] * (len(nodes) - 1)
        rows_of = [row + start * (1.0 - row)] + [row] * (len(nodes) - 1)
        mats = [eye + column * j for j in after]
        mats[0] = eye + (column + start * (1.0 - column)) * after[0]
        inverses = invert([(mat, bounds_at(JOIN_BOUNDS, 0), False) for mat in mats], eye, fast, acc_ref)
        less = [(eye - p).astype(bf16) for p in inverses]
        trans_b, turned_b = trans.astype(bf16), turned.astype(bf16)
        us = [trans - mm(trans_b, d) for d in less]
        vs = [one - mm(d, one.astype(bf16)) for one, d in zip(left, less)]
        zs = [u * r for u, r in zip(us, rows_of)]
        ts = [mm3(trans, v) for v in vs]
        ys = [mm3(j, v) for j, v in zip(after, vs)]
        cs = [noise + mm_nt(z.astype(bf16), trans_b) for z in zs]
        js = [j + mm(turned_b, y.astype(bf16)) for j, y in zip(before, ys)]
        for node, p, u, v, t, z, y, c, j in zip(nodes, inverses, us, vs, ts, zs, ys, cs, js):
            zh, zl = split(z)
            uz_ref[node, :, WIDTH:] = rows(zh, zl)
            yv_ref[node, WIDTH:, :] = pack(v)
            p_ref[node] = p
            a_ref[node] = t
            c_ref[node] = c
            j_ref[node] = j
        uh, ul = split(us[0])
        uz_ref[nodes[0], :, :WIDTH] = rows(uh, ul)
        yv_ref[nodes[0], :WIDTH, :] = pack(ys[0])

    def sweep(fast):
        count = half // 2
        group = min(count, GROUP) if fast else 1

        def some(block, carry):
            leaf_joins([block * group + k for k in range(group)], fast)
            return carry

        lax.fori_loop(0, count // group, some, 0)

    checked(sweep, acc_ref)


def invert(items, eye, fast, acc_ref, apart=False, beside=iter(())):
    if not fast:
        inverses = [safe_inverse(mat, eye) for mat, _, _ in items]
        return (inverses, [(p, None, None) for p in inverses]) if apart else inverses
    inverses, sides, worst = fast_inverses(items, eye, beside)
    acc_ref[...] = jnp.maximum(acc_ref[...], worst)
    return (inverses, [(g, e, mat) for (g, e), (mat, _, _) in zip(sides, items)]) if apart else inverses


def times_inverse(left, side):
    guess, resid, _ = side
    if resid is None:
        return mm3(left, guess)
    out = mm(lanes(*split(left)), rows(guess, guess))
    return out + mm(out.astype(bf16), resid)


def inverse_times(side, right, eye):
    guess, resid, mat = side
    if resid is None:
        return mm3(guess, right)
    resid = eye - mm(lanes(guess, guess), rows(*split(mat)))
    out = mm(lanes(guess, guess), rows(*split(right)))
    return out + mm(resid.astype(bf16), out.astype(bf16))


def checked(sweep, acc_ref, **beside):
    acc_ref[...] = jnp.zeros((8, WIDTH), f32)
    sweep(True, **beside)
    worst = jnp.sum(acc_ref[...])

    @pl.when(jnp.logical_not(worst <= RESIDUAL_MAX))
    def _():
        sweep(False)


def store_joined(outs, nodes, inverses, results):
    uz_ref, yv_ref, a_ref, c_ref, j_ref, p_ref = outs
    for node, p, (u, v, t, z, y, c, j) in zip(nodes, inverses, results):
        uh, ul = split(u)
        zh, zl = split(z)
        uz_ref[node] = rows(lanes(uh, zh), lanes(ul, zl))
        yv_ref[node] = rows(pack(y), pack(v))
        p_ref[node] = p
        a_ref[node] = t
        c_ref[node] = c
        j_ref[node] = j


def entries_of(level, half, steps, first, unit, refs, below):
    found = []
    for at_level, at in path_steps(half, steps, first):
        if at_level != level:
            continue
        node = at // (2 << level)
        if level == 0:
            eye = identity()
            start = jnp.where(unit * half + at == 0, 1.0, 0.0).astype(f32)
            c1 = below + start * (eye - below)
        else:
            c1 = below[2 * node]
        found.append(level_entry(refs, level, node, c1))
    return found


def panel_vectors(half, rows_own, unit, place, panel_in, mask_ref, weight_ref, panel_ref, all_ref, leaf_ref):
    total = panel_ref.shape[1]
    n_blocks = weight_ref.shape[0]
    n_time = panel_in.shape[0] // (2 * rows_own)
    for k in range(2 * n_time):
        core, chip, hop = (1 - unit if k % 2 else unit), place, n_time // 2
        for bit in range(1, n_time.bit_length()):
            if (k >> bit) % 2:
                chip = jnp.bitwise_xor(chip, hop)
            hop = hop // 2
        at = pl.multiple_of((2 * chip + core) * rows_own, rows_own)
        panel_ref[pl.ds(at, rows_own), :] = panel_in[k * rows_own:(k + 1) * rows_own, :]
    turned = jnp.zeros((WIDTH, total), f32)
    for block in range(n_blocks):
        mask = mask_ref[block:block + 1, :]
        turned = turned + mm(weight_ref[block], mask * panel_ref[block * WIDTH:(block + 1) * WIDTH, :])
    late = pltpu.roll(jnp.transpose(turned), 1, 0)
    all_ref[...] = late
    all_ref[0:1, :] = jnp.zeros((1, WIDTH), f32)
    leaf = all_ref[pl.ds(pl.multiple_of(unit * half, half), half), :]
    leaf_ref[...] = leaf
    return late[0:1, :], leaf


def vector_level(level, half, prior, gain_refs, leaf, bs, es):
    uz_ref, yv_ref = gain_refs
    stride = 1 << level
    zero = jnp.zeros((1, WIDTH), f32)
    for node in range(half >> (level + 1)):
        if node and node % 4 == 0:
            yield
        at = (2 * node + 1) * stride - 1
        if level == 0:
            b1, b2 = (prior if node == 0 else zero), zero
            e1, e2 = leaf[at:at + 1, :], leaf[at + 1:at + 2, :]
            if node > 0:
                high, low = split(e2)
                both = rows(high, low)
                out = mm_nt(both, uz_ref[node, :, WIDTH:])
                bs[at] = out[0:1, :WIDTH] + out[1:2, :WIDTH] + out[0:1, WIDTH:]
                out = mm(both, yv_ref[node, WIDTH:, :])
                es[at] = e1 + out[0:1, :WIDTH] + out[1:2, :WIDTH] + out[0:1, WIDTH:]
                continue
        else:
            one, two = at - stride // 2, at + stride // 2
            b1, b2, e1, e2 = bs[one], bs[two], es[one], es[two]
        high, low = split(lanes(b1, e2))
        out = mm_nt(rows(high, low), uz_ref[node])
        bs[at] = b2 + out[0:1, :WIDTH] + out[1:2, :WIDTH] + out[0:1, WIDTH:]
        high, low = split(lanes(-b1, e2))
        out = mm(rows(high, low), yv_ref[node])
        es[at] = e1 + out[0:1, :WIDTH] + out[1:2, :WIDTH] + out[0:1, WIDTH:]


def up_kernel(joins, half, steps, rows_own, index_ref, const_ref, *refs):
    unit, place = index_ref[0], index_ref[1]
    n_levels = half.bit_length() - 1
    low = joins[0]
    held = {}
    refs = list(refs)
    if rows_own:
        panel_in, mask_ref, weight_ref = refs[:3]
        refs = refs[3:]
        gain_refs, refs = refs[:2 * (low - 1)], refs[2 * (low - 1):]
        panel_ref, all_ref = refs[-2:]
        leaf_ref, b_ref, e_ref, message_ref = refs[-7:-3]
        refs = refs[:-7] + refs[-3:-2]
    if low > 1:
        below_ref = refs.pop(0)
    held[low - 1], refs = refs[:LEVEL_ARRAYS], refs[LEVEL_ARRAYS:]
    outs = {}
    for level in joins:
        held[level], refs = refs[:LEVEL_ARRAYS], refs[LEVEL_ARRAYS:]
        outs[level], refs = refs[:3], refs[3:]
    acc_ref, = refs
    eye = identity()

    def children(level, node):
        _, _, a_ref, c_ref, j_ref, _ = held[level - 1]
        return tuple((a_ref[k], c_ref[k], j_ref[k]) for k in (2 * node, 2 * node + 1))

    def condition_inputs(level):
        if level == 0:
            below = const_ref[1]
        elif level == low - 1:
            below = below_ref
        else:
            below = held[level - 1][3]
        return entries_of(level, half, steps, place * steps, unit, held[level], below)

    def store(level, results):
        for slot, result in enumerate(results):
            for ref, value in zip(outs[level], result):
                ref[slot] = value

    def sweep(fast, beside=iter(())):
        for level in joins:
            count = half >> (level + 1)
            under = level - 1
            if fast and count <= GROUP:
                nodes = list(range(count))
                entries = condition_inputs(under)
                pairs = [children(level, node) for node in nodes]
                items = [join_item(level, pair, eye) for pair in pairs]
                extra = [condition_item(under, entry, eye) for entry in entries]
                inverses = invert(items + [item for item, _ in extra], eye, True, acc_ref, beside=beside)
                results, seen = [], []
                in_turns(
                    joining(level, pairs, inverses[:count], eye, results),
                    conditioning(entries, [scale for _, scale in extra], inverses[count:], seen),
                    beside,
                )
                store_joined(held[level], nodes, inverses[:count], results)
                store(level, seen)
                continue
            group = min(count, GROUP) if fast else 1

            def some(block, carry):
                nodes = [block * group + k for k in range(group)]
                pairs = [children(level, node) for node in nodes]
                inverses = invert([join_item(level, pair, eye) for pair in pairs], eye, fast, acc_ref)
                results = []
                in_turns(joining(level, pairs, inverses, eye, results))
                store_joined(held[level], nodes, inverses, results)
                return carry

            lax.fori_loop(0, count // group, some, 0)
            entries = condition_inputs(under)
            extra = [condition_item(under, entry, eye) for entry in entries]
            inverses = invert([item for item, _ in extra], eye, fast, acc_ref)
            seen = []
            in_turns(conditioning(entries, [scale for _, scale in extra], inverses, seen))
            store(level, seen)

    if not rows_own:
        checked(sweep, acc_ref)
        return
    prior = jnp.where(unit == 0, 1.0, 0.0) * const_ref[0, 0:1, :]
    gains = [gain_refs[2 * level:2 * level + 2] for level in range(low - 1)] + [held[low - 1][:2]]
    bs, es, found = {}, {}, []

    def means():
        found.extend(panel_vectors(
            half, rows_own, unit, index_ref[3], panel_in, mask_ref, weight_ref, panel_ref, all_ref, leaf_ref
        ))
        yield
        for level in range(low):
            yield from vector_level(level, half, prior, gains[level], found[1], bs, es)
            yield

    pieces = means()
    checked(sweep, acc_ref, beside=pieces)
    for _ in pieces:
        pass
    end, leaf = found
    for level in range(low, n_levels):
        in_turns(vector_level(level, half, prior, held[level][:2], leaf, bs, es))
    for at in bs:
        b_ref[at:at + 1, :] = bs[at]
        e_ref[at:at + 1, :] = es[at]
    top = half // 2 - 1
    _, _, a_ref, c_ref, j_ref, _ = held[n_levels - 1]
    for k, ref in enumerate((a_ref, c_ref, j_ref)):
        message_ref[k * WIDTH:(k + 1) * WIDTH, :] = ref[0]
    message_ref[3 * WIDTH:, :] = rows(bs[top], es[top], end, jnp.zeros((5, WIDTH), f32))


SMEM = pl.BlockSpec(memory_space=pltpu.SMEM)
VMEM = pl.BlockSpec(memory_space=pltpu.VMEM)


ANY = pl.BlockSpec(memory_space=pl.ANY)


def level_shapes(half, level):
    count = half >> (level + 1)
    mat = (count, WIDTH, WIDTH)
    wide = (count, 2 * WIDTH, 2 * WIDTH)
    return [jax.ShapeDtypeStruct(wide, bf16)] * 2 + [jax.ShapeDtypeStruct(mat, f32)] * 4


def path_shapes(half, steps, level):
    count = len([k for k, _ in path_steps(half, steps, 0) if k == level])
    return [
        jax.ShapeDtypeStruct((count, 2 * WIDTH, 2 * WIDTH), bf16),
        jax.ShapeDtypeStruct((count, WIDTH, WIDTH), f32),
        jax.ShapeDtypeStruct((count, 3 * WIDTH, 2 * WIDTH), bf16),
    ]


def estimate(matrices):
    return pl.CostEstimate(flops=matrices * 600 * WIDTH**3, transcendentals=0, bytes_accessed=1 << 20)


def first_sweep(half, index, cell_mask, loadings, prec_rows, transition, var_row, prior_row):
    mat = (WIDTH, WIDTH)
    n_blocks = loadings.shape[0] // WIDTH
    outs = [
        jax.ShapeDtypeStruct((n_blocks,) + mat, bf16),
        jax.ShapeDtypeStruct(mat, f32),
        jax.ShapeDtypeStruct(cell_mask.shape, bf16),
        jax.ShapeDtypeStruct((2,) + mat, f32),
    ] + level_shapes(half, 0)
    inputs = [
        pltpu.with_memory_space_constraint(array, pltpu.HBM)
        for array in (cell_mask, loadings, prec_rows, transition, var_row, prior_row)
    ]
    return pl.pallas_call(
        functools.partial(first_kernel, half),
        out_shape=outs,
        in_specs=[SMEM] + [ANY] * 6,
        out_specs=[VMEM] * len(outs),
        scratch_shapes=[
            pltpu.VMEM((n_blocks,) + mat, f32),
            pltpu.VMEM((8, WIDTH), f32),
            pltpu.SMEM(cell_mask.shape, jnp.int32),
            pltpu.VMEM(cell_mask.shape, jnp.int32),
            pltpu.VMEM(loadings.shape, bf16),
            pltpu.VMEM(prec_rows.shape, f32),
            pltpu.VMEM((4,) + mat, f32),
            pltpu.VMEM((2, 1, WIDTH), f32),
            pltpu.SemaphoreType.DMA((7,)),
        ],
        compiler_params=pltpu.CompilerParams(vmem_limit_bytes=VMEM_LIMIT),
        cost_estimate=estimate(half // 2),
        name="first_sweep",
    )(index, *inputs)


def up_sweep(joins, half, steps, index, consts, held, rows_own=0, vectors=()):
    low = joins[0]
    operands = ([held[low - 2][3]] if low > 1 else []) + list(held[low - 1])
    outs = []
    for level in joins:
        outs += level_shapes(half, level) + path_shapes(half, steps, level - 1)
    scratch = [pltpu.VMEM((8, WIDTH), f32)]
    if rows_own:
        panel = vectors[0]
        operands = list(vectors) + [array for level in held[:-1] for array in level[:2]] + operands
        row = jax.ShapeDtypeStruct((half, WIDTH), f32)
        outs += [row, row, row, jax.ShapeDtypeStruct((3 * WIDTH + 8, WIDTH), f32)]
        scratch += [pltpu.VMEM((panel.shape[1], WIDTH), f32)]
        scratch = scratch[:1] + [pltpu.VMEM(panel.shape, bf16)] + scratch[1:]
    results = pl.pallas_call(
        functools.partial(up_kernel, joins, half, steps, rows_own),
        out_shape=outs,
        in_specs=[SMEM] + [VMEM] * (1 + len(operands)),
        out_specs=[VMEM] * len(outs),
        scratch_shapes=scratch,
        compiler_params=pltpu.CompilerParams(vmem_limit_bytes=VMEM_LIMIT),
        cost_estimate=estimate(sum(half >> level for level in joins)),
        name="up_sweep_%d" % low,
    )(index, consts, *operands)
    results = list(results)
    step = LEVEL_ARRAYS + 3
    parts = [results[k * step:(k + 1) * step] for k in range(len(joins))]
    return [part[:LEVEL_ARRAYS] for part in parts], [part[LEVEL_ARRAYS:] for part in parts], results[len(joins) * step:]


def down_kernel(steps, index_ref, own_ref, other_ref, end_ref, const_ref, leaf_ref, b_ref, e_ref, below_ref,
                *refs):
    refs = list(refs)
    top_refs, refs = refs[:LEVEL_ARRAYS], refs[LEVEL_ARRAYS:]
    out_ref, acc_ref, top_ref, gt_ref, cond_ref, shift_ref = refs[-6:]
    path_refs = refs[:-6]
    unit, place = index_ref[0], index_ref[1]
    half = leaf_ref.shape[0]
    n_levels = half.bit_length() - 1
    eye = identity()
    flag = jnp.where(unit == 0, 1.0, 0.0).astype(f32)

    def pick(zero, one):
        return flag * zero + (1.0 - flag) * one

    def both(first, count):
        part = slice(first, first + count)
        return own_ref[part, :], other_ref[part, :]

    own, other = both(WIDTH, WIDTH)
    cov0 = pick(own, other)
    trans1, cov1, info1 = [pick(*both(k * WIDTH, WIDTH)[::-1]) for k in range(3)]
    b0 = pick(*both(3 * WIDTH, 1))
    b1, e1 = [pick(*both(3 * WIDTH + k, 1)[::-1]) for k in range(2)]
    e_end = own_ref[3 * WIDTH + 2:3 * WIDTH + 3, :]
    end = end_ref[...]

    first = place * steps

    def roots(fast, beside=iter(())):
        under = n_levels - 1
        entries = entries_of(under, half, steps, first, unit, top_refs, below_ref)
        extra = [condition_item(under, entry, eye) for entry in entries]
        item = (eye + mm3(cov0, info1), bounds_at(JOIN_BOUNDS, n_levels), True)
        ready = mm3_nt(cov0, trans1)
        ready_end, cov1_end = mm3(ready, end), mm3(cov1, end)
        (p, *inverses), sides = invert([item] + [item for item, _ in extra], eye, fast, acc_ref, True, beside)
        u = times_inverse(trans1, sides[0])
        last = eye + cov1_end + mm3(u, ready_end)
        cov = cov1 + mm3(u, ready)
        z = mm3(u, cov0)
        kept = mm3(p, cov0)
        results = []
        in_turns(conditioning(entries, [scale for _, scale in extra], inverses, results), beside)
        for slot, result in enumerate(results):
            for ref, value in zip((gt_ref, cond_ref, shift_ref), result):
                ref[slot] = value
        info_z = mm3(jnp.transpose(z), end)
        _, (side,) = invert([(last, bounds_at(JOIN_BOUNDS, 0), False)], eye, fast, acc_ref, True)
        top_ref[0], top_ref[1] = inverse_times(side, cov, eye), inverse_times(side, z, eye)
        top_ref[2] = kept - mm3(info_z, top_ref[1])
        top_ref[3] = p

    prior = flag * const_ref[0, 0:1, :]
    path = path_steps(half, steps, first)
    levels = [(gt_ref, cond_ref, shift_ref)] + [path_refs[k:k + 3] for k in range(0, len(path_refs), 3)]
    places, seen = [], {}
    for level, _ in path:
        seen[level] = seen.get(level, -1) + 1
        places.append((levels[n_levels - 1 - level], seen[level]))

    def shift(slot):
        level, at = path[slot]
        row_of = lambda ref, k: ref[pl.ds(k, 1), :]
        if level == 0:
            one, two = jnp.where(at == 0, 1.0, 0.0) * prior, row_of(leaf_ref, at + 1)
        else:
            near = (1 << level) // 2
            one, two = row_of(b_ref, at - near), row_of(e_ref, at + near)
        high, low = split(lanes(one, two, row_of(b_ref, at)))
        arrays, own = places[slot]
        out = mm(rows(high, low), arrays[2][own])
        return out[0:1, :WIDTH] + out[1:2, :WIDTH] + out[0:1, WIDTH:]

    shifts = {}

    def shifting():
        for slot, (level, _) in enumerate(path):
            if level < n_levels - 1:
                shifts[slot] = shift(slot)
                yield

    pieces = shifting()
    checked(roots, acc_ref, beside=pieces)
    for _ in pieces:
        pass
    shifts[0] = shift(0)
    cov_top, cov_cross, cov_mid, p = [top_ref[k] for k in range(4)]
    mean_mid = mm3_nt(b0 + mm3(e1, cov0), p)
    b_end = mm3_nt(mean_mid, trans1) + b1
    news = e_end - mm3(b_end, end)
    mean_top = b_end + mm3_nt(news, cov_top)
    mean_mid = mean_mid + mm3(news, cov_cross)
    keep = 1.0 - flag
    joint = rows(
        lanes(keep * cov_mid, keep * jnp.transpose(cov_cross)),
        lanes(keep * cov_cross, pick(cov_mid, cov_top)),
    )
    means = lanes(keep * mean_mid, pick(mean_mid, mean_top))

    def nodes(slots, joints, means, leaf):
        packs = [places[slot][0][0][places[slot][1]] for slot in slots]
        conds = [places[slot][0][1][places[slot][1]] for slot in slots]
        halves = [split(joint) for joint in joints]
        crosses = [
            mm(lanes(jh, jl), rows(g[:, :WIDTH], g[:, :WIDTH])) + mm(jh, g[:, WIDTH:])
            for (jh, jl), g in zip(halves, packs)
        ]
        outs = [mm(rows(*split(mean)), g) for mean, g in zip(means, packs)]
        found = [
            shifts[slot] + out[0:1, :WIDTH] + out[1:2, :WIDTH] + out[0:1, WIDTH:] for slot, out in zip(slots, outs)
        ]
        gains = [unpack(g) for g in packs]
        if leaf:
            owns = [
                diagonal(cond, eye) + jnp.sum(gain * cross, axis=0, keepdims=True)
                for cond, gain, cross in zip(conds, gains, crosses)
            ]
        else:
            owns = [cond + mm3(jnp.transpose(gain), cross) for cond, gain, cross in zip(conds, gains, crosses)]
        return list(zip(found, owns, crosses))

    def left_pair(joint, means, mean, own, cross):
        c = cross[:WIDTH]
        return rows(lanes(joint[:WIDTH, :WIDTH], c), lanes(jnp.transpose(c), own)), lanes(means[:, :WIDTH], mean)

    def right_pair(joint, means, mean, own, cross):
        c = cross[WIDTH:]
        return rows(lanes(own, jnp.transpose(c)), lanes(c, joint[WIDTH:, WIDTH:])), lanes(mean, means[:, WIDTH:])

    slot = 0
    while path[slot][0] >= steps.bit_length() - 1:
        result, = nodes([slot], [joint], [means], False)
        go_right = jnp.where(first > path[slot][1], 1.0, 0.0).astype(f32)
        lj, lm = left_pair(joint, means, *result)
        rj, rm = right_pair(joint, means, *result)
        joint = go_right * rj + (1.0 - go_right) * lj
        means = go_right * rm + (1.0 - go_right) * lm
        slot += 1

    out_ref[steps - 1:steps, :] = means[:, WIDTH:]
    out_ref[2 * steps - 1:2 * steps, :] = diagonal(joint[WIDTH:, WIDTH:], eye)
    todo = [(0, joint, means)]
    count = steps
    while todo:
        stride, later = count // 2, []
        leaf = stride == 1
        results = nodes(
            range(slot, slot + len(todo)), [joint for _, joint, _ in todo], [means for _, _, means in todo], leaf
        )
        slot += len(todo)
        for (low, joint, means), result in zip(todo, results):
            at = low + stride - 1
            out_ref[at:at + 1, :] = result[0]
            out_ref[steps + at:steps + at + 1, :] = result[1] if leaf else diagonal(result[1], eye)
            if not leaf:
                later.append((low,) + left_pair(joint, means, *result))
                later.append((low + stride,) + right_pair(joint, means, *result))
        todo, count = later, stride


def down_sweep(steps, half, *operands):
    return pl.pallas_call(
        functools.partial(down_kernel, steps),
        out_shape=jax.ShapeDtypeStruct((2 * steps, WIDTH), f32),
        in_specs=[SMEM] + [VMEM] * (len(operands) - 1),
        out_specs=VMEM,
        scratch_shapes=[pltpu.VMEM((8, WIDTH), f32), pltpu.VMEM((6, WIDTH, WIDTH), f32)]
        + [pltpu.VMEM(shape.shape, shape.dtype) for shape in path_shapes(half, steps, half.bit_length() - 2)],
        compiler_params=pltpu.CompilerParams(vmem_limit_bytes=VMEM_LIMIT),
        name="down_sweep",
    )(*operands)


def redundant(panel_data, cell_mask, loadings, noise_prec, transition, proc_var, prior_mean):
    n_time = lax.axis_size("tm")
    n_unit = lax.axis_size("unit")
    place, unit = lax.axis_index("tm"), lax.axis_index("unit")
    total = panel_data.shape[1]
    half = total // n_unit
    steps = total // n_time
    per_half = half // steps
    index = jnp.stack([unit, place % per_half, n_unit, place]).astype(jnp.int32)
    swap = [(0, 1), (1, 0)]

    def swapped(value, other):
        return lax.ppermute(value, "tm", [(k, k ^ other) for k in range(n_time)])

    n_levels = half.bit_length() - 1
    hops = [1 << k for k in reversed(range(n_time.bit_length() - 1))]
    weighted, end, mask, consts, *level0 = first_sweep(
        half, index, cell_mask, loadings, noise_prec.reshape(-1, WIDTH), transition,
        proc_var.reshape(1, WIDTH), prior_mean.reshape(1, WIDTH),
    )
    held, paths = [level0], []
    panel = jnp.concatenate([panel_data, lax.ppermute(panel_data, "unit", swap)])
    cuts = [[1], [2], [3], list(range(4, n_levels))]
    for k, joins in enumerate(cuts):
        panel, held[-1] = lax.optimization_barrier((panel, held[-1]))
        last = k + 1 == len(cuts)
        extra = (panel_data.shape[0], (panel, mask, weighted)) if last else ()
        new, path, rest = up_sweep(joins, half, steps, index, consts, held, *extra)
        if not last:
            panel = jnp.concatenate([panel, swapped(panel, hops[k])])
        held += new
        paths += path
    leaves, bs, es, message = rest
    other = lax.ppermute(message, "unit", swap)
    mine = down_sweep(
        steps, half, index, message, other, end, consts, leaves, bs, es, held[-2][3], *held[-1],
        *[array for path in reversed(paths) for array in path],
    )
    theirs = lax.ppermute(mine, "unit", swap)
    out = jnp.where(unit == place // per_half, mine, theirs)
    return out[:steps], out[steps:]


BLOCK = 128


def carried_in(value, axis, join, neutral, backward):
    count, mine = (lax.axis_size(axis), lax.axis_index(axis))
    pieces = jax.tree.map(lambda part: lax.all_gather(part, axis), value)
    if backward:
        pieces = jax.tree.map(lambda part: part[::-1], pieces)
        mine = count - 1 - mine
    running = jax.tree.map(
        lambda part, zero: jnp.full_like(part, 0) + jnp.asarray(zero, part.dtype), value, neutral
    )

    def step(position, running):
        longer = join(running, jax.tree.map(lambda part: part[position], pieces))
        return jax.tree.map(lambda new, old: jnp.where(position < mine, new, old), longer, running)

    return lax.fori_loop(0, count - 1, step, running)


def product(left, right):
    return jnp.matmul(left, right, precision=HIGHEST)


def mat_vec(matrix, vector):
    return jnp.einsum("...kl,...l->...k", matrix, vector, precision=HIGHEST)


def flipped(matrix):
    return jnp.swapaxes(matrix, -1, -2)


def chol_apply(factor, rhs):
    middle = lax.linalg.triangular_solve(factor, rhs, left_side=True, lower=True)
    return lax.linalg.triangular_solve(factor, middle, left_side=True, lower=True, transpose_a=True)


def filter_join(earlier, later):
    trans_one, shift_one, cov_one, info_one, vec_one, live_one = earlier
    trans_two, shift_two, cov_two, info_two, vec_two, live_two = later
    identity_mat = jnp.eye(trans_one.shape[-1], dtype=jnp.float32)
    live_mat = live_one[..., None, None]
    factor_one = jnp.linalg.cholesky(cov_one + (1.0 - live_mat) * identity_mat)
    inner_mat = identity_mat + product(product(flipped(factor_one), info_two), factor_one)
    inner_factor = jnp.linalg.cholesky(inner_mat)
    solved = lax.linalg.triangular_solve(
        inner_factor, flipped(factor_one), left_side=True, lower=True
    )
    spread_mat = product(trans_two, flipped(solved))
    pushed = product(info_two, trans_one)
    reduced = product(solved, pushed)
    residue = vec_two - mat_vec(info_two, shift_one)
    solved_residue = mat_vec(solved, residue)
    trans_new = product(trans_two, trans_one) - product(spread_mat, reduced)
    shift_new = mat_vec(trans_two, shift_one) + mat_vec(spread_mat, solved_residue) + shift_two
    cov_new = product(spread_mat, flipped(spread_mat)) + cov_two
    info_new = product(flipped(trans_one), pushed) - product(flipped(reduced), reduced) + info_one
    vec_new = (
        mat_vec(flipped(trans_one), residue) - mat_vec(flipped(reduced), solved_residue) + vec_one
    )
    alive_mat = live_mat > 0.5
    alive_vec = live_one[..., None] > 0.5
    return (
        jnp.where(alive_mat, trans_new, trans_two),
        jnp.where(alive_vec, shift_new, shift_two),
        jnp.where(alive_mat, cov_new, cov_two),
        jnp.where(alive_mat, info_new, info_two),
        jnp.where(alive_vec, vec_new, vec_two),
        jnp.maximum(live_one, live_two),
    )


def smooth_join(lower_elem, higher_elem):
    gain_low, offset_low, cov_low = lower_elem
    gain_high, offset_high, cov_high = higher_elem
    return (
        product(gain_low, gain_high),
        mat_vec(gain_low, offset_high) + offset_low,
        product(product(gain_low, cov_high), flipped(gain_low)) + cov_low,
    )


def smooth_scan_join(earlier, later):
    return smooth_join(later, earlier)


def take_last(stacked):
    return stacked[-1]


def take_first(stacked):
    return stacked[0]


def per_device(panel_data, cell_mask, loadings, noise_prec, transition, proc_var, prior_mean):
    n_time = lax.axis_size("tm")
    n_unit = lax.axis_size("unit")
    time_index = lax.axis_index("tm")
    unit_index = lax.axis_index("unit")
    rows_own, total_time = panel_data.shape
    steps = total_time // n_time
    width = transition.shape[0]
    identity_mat = jnp.eye(width, dtype=jnp.float32)
    my_columns = lax.dynamic_slice_in_dim(cell_mask, time_index * steps, steps, 1)
    half_load = lax.dynamic_index_in_dim(
        loadings.reshape(n_time, n_unit, rows_own, width), unit_index, 1, keepdims=False
    ).reshape(n_time * rows_own, width)
    half_prec = lax.dynamic_index_in_dim(
        noise_prec.reshape(n_time, n_unit, rows_own), unit_index, 1, keepdims=False
    ).reshape(n_time * rows_own)
    half_ids = (
        (jnp.arange(n_time, dtype=jnp.int32)[:, None] * n_unit + unit_index) * rows_own
        + jnp.arange(rows_own, dtype=jnp.int32)[None, :]
    ).reshape(-1)
    half_weighted = (half_prec[:, None] * half_load.astype(jnp.float32)).astype(jnp.bfloat16)
    half_mask = jnp.take(my_columns, half_ids // BLOCK, axis=0).astype(jnp.bfloat16)
    regrouped = lax.all_to_all(panel_data, "tm", split_axis=1, concat_axis=0, tiled=True)
    vec_half = jnp.dot((half_mask * regrouped).T, half_weighted, preferred_element_type=jnp.float32)
    group_rows = min(rows_own, BLOCK)
    n_groups = n_time * rows_own // group_rows
    group_gram = jnp.einsum(
        "gnk,gnl->gkl",
        half_weighted.reshape(n_groups, group_rows, width),
        half_load.reshape(n_groups, group_rows, width),
        preferred_element_type=jnp.float32,
    )
    group_block = half_ids.reshape(n_groups, group_rows)[:, 0] // BLOCK
    group_mask = jnp.take(my_columns, group_block, axis=0).astype(jnp.float32)
    info_half = jnp.einsum("gt,gkl->tkl", group_mask, group_gram, precision=HIGHEST)
    info_mat, info_vec = lax.psum((info_half, vec_half), "unit")
    global_step = time_index * steps + jnp.arange(steps, dtype=jnp.int32)
    first_step = (global_step == 0).astype(jnp.float32)
    keep_step = 1.0 - first_step
    last_keep = 1.0 - (global_step == total_time - 1).astype(jnp.float32)
    inv_var = 1.0 / proc_var
    prior_prec = first_step[:, None, None] * identity_mat + keep_step[:, None, None] * jnp.diag(
        inv_var
    )
    eyes = jnp.broadcast_to(identity_mat, info_mat.shape)
    post_cov = chol_apply(jnp.linalg.cholesky(prior_prec + info_mat), eyes)
    shift_vec = jnp.einsum(
        "skl,sl->sk",
        post_cov,
        info_vec + first_step[:, None] * prior_mean[None, :],
        precision=HIGHEST,
    )
    scaled_trans = inv_var[:, None] * transition
    trans_part = keep_step[:, None, None] * jnp.einsum(
        "skl,lm->skm", post_cov, scaled_trans, precision=HIGHEST
    )
    middle = jnp.diag(inv_var)[None] - inv_var[None, :, None] * post_cov * inv_var[None, None, :]
    pressed = jnp.einsum("slm,mn->sln", middle, transition, precision=HIGHEST)
    info_part = keep_step[:, None, None] * jnp.einsum(
        "lk,sln->skn", transition, pressed, precision=HIGHEST
    )
    vec_part = keep_step[:, None] * jnp.einsum(
        "lk,sl->sk", transition, inv_var[None, :] * shift_vec, precision=HIGHEST
    )
    elements = (
        trans_part,
        shift_vec,
        post_cov,
        info_part,
        vec_part,
        jnp.ones((steps,), jnp.float32),
    )
    zero_vec = jnp.zeros((width,), jnp.float32)
    zero_mat = jnp.zeros((width, width), jnp.float32)
    filter_identity = (identity_mat, zero_vec, zero_mat, zero_mat, zero_vec, jnp.float32(0.0))
    local_joined = lax.associative_scan(filter_join, elements)
    filter_total = jax.tree.map(take_last, local_joined)
    before = carried_in(filter_total, "tm", filter_join, filter_identity, False)
    filtered = jax.vmap(filter_join, in_axes=(None, 0))(before, local_joined)
    filt_mean = filtered[1]
    filt_cov = filtered[2]
    moved_cov = jnp.einsum("kl,slm->skm", transition, filt_cov, precision=HIGHEST)
    pred_next = (
        jnp.einsum("skm,nm->skn", moved_cov, transition, precision=HIGHEST)
        + jnp.diag(proc_var)[None]
    )
    gain = (
        jnp.transpose(chol_apply(jnp.linalg.cholesky(pred_next), moved_cov), (0, 2, 1))
        * last_keep[:, None, None]
    )
    moved_mean = jnp.einsum("kl,sl->sk", transition, filt_mean, precision=HIGHEST)
    offset = filt_mean - jnp.einsum("skl,sl->sk", gain, moved_mean, precision=HIGHEST)
    resid_cov = filt_cov - jnp.einsum("skl,slm->skm", gain, moved_cov, precision=HIGHEST)
    smooth_identity = (identity_mat, zero_vec, zero_mat)
    local_suffix = lax.associative_scan(smooth_scan_join, (gain, offset, resid_cov), reverse=True)
    smooth_total = jax.tree.map(take_first, local_suffix)
    after = carried_in(smooth_total, "tm", smooth_scan_join, smooth_identity, True)
    smoothed = jax.vmap(smooth_join, in_axes=(0, None))(local_suffix, after)
    smoothed_mean = smoothed[1]
    smoothed_var = jnp.diagonal(smoothed[2], axis1=1, axis2=2)
    return (smoothed_mean, smoothed_var)


def per_device_any(*arrays):
    fits = arrays[0].shape[1] <= 64 * lax.axis_size("unit") and lax.axis_size("unit") == 2
    return redundant(*arrays) if fits else per_device(*arrays)


def solution(mesh):
    return jax.shard_map(
        per_device_any,
        mesh=mesh,
        in_specs=(P(("grp", "tm", "unit"), None), P("grp", None), P(), P(), P(), P(), P()),
        out_specs=(P(("grp", "tm"), None), P(("grp", "tm"), None)),
        check_vma=False,
    )
```

```python
import functools

import jax
import jax.numpy as jnp
from jax import lax
from jax.experimental import pallas as pl
from jax.experimental.pallas import tpu as pltpu
from jax.sharding import PartitionSpec as P

f32 = jnp.float32
bf16 = jnp.bfloat16
WIDTH = 128
HIGHEST = lax.Precision.HIGHEST
VMEM_LIMIT = 30 << 20
RESIDUAL_MAX = 7e-3
GROUP = 16
JOIN_BOUNDS = ((1.0, 4.0), (1.0, 5.2), (1.0, 5.2), (1.0, 6.0), (1.0, 10.0), (1.0, 13.0))
COV_BOUNDS = ((0.70, 1.37), (0.50, 1.90), (0.31, 2.85), (0.19, 4.50), (0.12, 6.30))


def schedule(bounds, goal=2.5e-3):
    low, high = bounds
    alpha, radius, factors = 2.0 / (low + high), (high - low) / (high + low), []
    while radius > goal:
        square = radius * radius
        factors.append(2.0 / (2.0 - square))
        radius = square / (2.0 - square)
    return alpha, factors


def bounds_at(table, level):
    return table[min(level, len(table) - 1)]


def mm(left, right):
    return lax.dot_general(left, right, (((1,), (0,)), ((), ())), preferred_element_type=f32)


def mm_nt(left, right):
    return lax.dot_general(left, right, (((1,), (1,)), ((), ())), preferred_element_type=f32)


def split(value):
    high = value.astype(bf16)
    return high, (value - high.astype(f32)).astype(bf16)


def lanes(*parts):
    return jnp.concatenate(parts, axis=1)


def rows(*parts):
    return jnp.concatenate(parts, axis=0)


def mm3(left, right):
    lh, ll = split(left)
    rh, rl = split(right)
    return mm(lanes(lh, ll), rows(rh, rh)) + mm(lh, rl)


def mm3_nt(left, right):
    lh, ll = split(left)
    rh, rl = split(right)
    return mm_nt(lanes(lh, ll), lanes(rh, rh)) + mm_nt(lh, rl)


def identity():
    shape = (WIDTH, WIDTH)
    return (lax.broadcasted_iota(jnp.int32, shape, 0) == lax.broadcasted_iota(jnp.int32, shape, 1)).astype(f32)


def squares(value):
    return jnp.sum((value * value).reshape(WIDTH // 8, 8, WIDTH), axis=0)


def fast_inverses(items, eye, beside=iter(())):
    mats = [mat for mat, _, _ in items]
    plans = [schedule(bounds) for _, bounds, _ in items]
    n = range(len(items))
    halves = [split(mat) for mat in mats]
    rest = [eye - plan[0] * mat for plan, mat in zip(plans, mats)]
    guess = [(plan[0] * plan[1][0]) * (eye + r) for plan, r in zip(plans, rest)]
    for step in range(max(len(factors) for _, factors in plans)):
        rest_b = [r.astype(bf16) for r in rest]
        guess_b = [g.astype(bf16) for g in guess]
        for k in n:
            factors = plans[k][1]
            more = step + 1 < len(factors)
            if step >= len(factors):
                continue
            factor = factors[step]
            if step == 0:
                if more:
                    rest[k] = (1.0 - factor) * eye + factor * mm(rest_b[k], rest_b[k])
            elif more:
                out = mm(rest_b[k], lanes(guess_b[k], rest_b[k]))
                guess[k] = factor * (guess[k] + out[:, :WIDTH])
                rest[k] = (1.0 - factor) * eye + factor * out[:, WIDTH:]
            else:
                guess[k] = factor * (guess[k] + mm(rest_b[k], guess_b[k]))
        next(beside, None)
    guess_b = [g.astype(bf16) for g in guess]
    resid = [eye - mm(lanes(h, l), rows(g, g)) for (h, l), g in zip(halves, guess_b)]
    guess = [g.astype(f32) + mm(g, e.astype(bf16)) for g, e in zip(guess_b, resid)]
    next(beside, None)
    sides = [(g, e.astype(bf16)) for g, e in zip(guess_b, resid)]
    again = [k for k in n if items[k][2]]
    fine = {k: eye - mm3(mats[k], guess[k]) for k in again}
    for k in again:
        resid[k] = fine[k]
        guess[k] = guess[k] + mm(guess[k].astype(bf16), fine[k].astype(bf16))
        sides[k] = (guess[k], None)
    sizes = [squares(e) for e in resid]
    sizes = [jnp.where(size < 1e6, size, 1e6) for size in sizes]
    worst = sizes[0]
    for size in sizes[1:]:
        worst = jnp.maximum(worst, size)
    return guess, sides, worst


def safe_inverse(mat, eye):
    size = jnp.max(jnp.sum(jnp.abs(mat), axis=0, keepdims=True), axis=1, keepdims=True)
    product = functools.partial(jnp.dot, precision=HIGHEST, preferred_element_type=f32)

    def unfinished(state):
        step, size, _ = state
        return jnp.logical_and(step < 64, jnp.logical_not(size <= 1e-7))

    def improve(state):
        step, _, guess = state
        resid = eye - product(mat, guess)
        return step + 1, jnp.sum(squares(resid)), guess + product(guess, resid)

    return lax.while_loop(unfinished, improve, (0, f32(jnp.inf), eye / size))[2]


def diagonal(mat, eye):
    return jnp.sum(mat * eye, axis=0, keepdims=True)


def scaled(mat, eye):
    row = 1.0 / diagonal(mat, eye)
    return mat * row, row


def pack(value):
    return lanes(*split(value))


def unpack(value):
    return value[:, :WIDTH].astype(f32) + value[:, WIDTH:].astype(f32)


def path_steps(half, steps, first):
    found = []
    for level in reversed(range(half.bit_length() - 1)):
        stride = 1 << level
        if 2 * stride > steps:
            found.append((level, (first // (2 * stride)) * (2 * stride) + stride - 1))
        else:
            found += [(level, first + (2 * k + 1) * stride - 1) for k in range(steps // (2 * stride))]
    return found


def join_item(level, pair, eye):
    (_, c1, _), (_, _, j2) = pair
    return eye + mm3(c1, j2), bounds_at(JOIN_BOUNDS, level), False


def in_turns(*works):
    works = list(works)
    while works:
        for work in tuple(works):
            if next(work, works) is works:
                works.remove(work)


def joining(level, pairs, inverses, eye, results):
    turned = [jnp.transpose(one[0]) for one, two in pairs]
    if level < 2:
        less = [(eye - p).astype(bf16) for p in inverses]
        us = [two[0] - mm(two[0].astype(bf16), d) for (one, two), d in zip(pairs, less)]
        vs = [one[0] - mm(d, one[0].astype(bf16)) for (one, two), d in zip(pairs, less)]
    else:
        us = [mm3(two[0], p) for (one, two), p in zip(pairs, inverses)]
        vs = [mm3(p, one[0]) for (one, two), p in zip(pairs, inverses)]
    yield
    zs = [mm3(u, one[1]) for u, (one, two) in zip(us, pairs)]
    ys = [mm3(two[2], v) for v, (one, two) in zip(vs, pairs)]
    yield
    ts = [mm3(two[0], v) for v, (one, two) in zip(vs, pairs)]
    few = level < 2
    cs = [
        two[1] + (mm_nt(z.astype(bf16), two[0].astype(bf16)) if few else mm3_nt(z, two[0]))
        for z, (one, two) in zip(zs, pairs)
    ]
    yield
    js = [one[2] + (mm(t.astype(bf16), y.astype(bf16)) if few else mm3(t, y)) for t, y, (one, two) in zip(turned, ys, pairs)]
    results += list(zip(us, vs, ts, zs, ys, cs, js))


def condition_item(level, entry, eye):
    mat, scale = scaled(entry["c"], eye)
    return (mat, bounds_at(COV_BOUNDS, level), level > 2), scale


def conditioning(entries, scales, inverses, results):
    zs, vs = [e["z"] for e in entries], [e["v"] for e in entries]
    kepts = [mm3(e["p"], e["c1"]) for e in entries]
    backs = [mm3(jnp.transpose(inverse) * scale, z) for inverse, scale, z in zip(inverses, scales, zs)]
    yield
    forths = [jnp.transpose(back) for back in backs]
    gains = [v - mm3(forth, e["a"]) for v, forth, e in zip(vs, forths, entries)]
    yield
    conds = [kept - mm3(forth, z) for kept, forth, z in zip(kepts, forths, zs)]
    yield
    results += [
        (
            pack(rows(jnp.transpose(gain), back)),
            cond,
            pack(rows(jnp.transpose(e["p"]), jnp.transpose(kept), -back)),
        )
        for e, gain, back, cond, kept in zip(entries, gains, backs, conds, kepts)
    ]


def level_entry(refs, level, node, c1):
    uz_ref, yv_ref, a_ref, c_ref, _, p_ref = refs
    uz = uz_ref[node]
    return dict(
        z=uz[:WIDTH, WIDTH:].astype(f32) + uz[WIDTH:, WIDTH:].astype(f32),
        v=unpack(yv_ref[node, WIDTH:, :]),
        a=a_ref[node],
        c=c_ref[node],
        p=p_ref[node],
        c1=c1,
    )


LEVEL_ARRAYS = 6


def first_kernel(half, index_ref, mask_hbm, load_hbm, prec_hbm, trans_hbm, var_hbm, prior_hbm,
                 weight_ref, end_ref, mask_out, const_ref, uz_ref, yv_ref, a_ref, c_ref, j_ref, p_ref,
                 gram_ref, acc_ref, mask_ref, mask_vmem, load_ref, prec_ref, base_ref, row_ref, sems):
    unit, n_unit = index_ref[0], index_ref[2]
    copies = [
        pltpu.make_async_copy(source, target, sems.at[k])
        for k, (source, target) in enumerate((
            (load_hbm, load_ref), (prec_hbm, prec_ref), (trans_hbm, base_ref.at[0]), (var_hbm, row_ref.at[0]),
            (prior_hbm, row_ref.at[1]), (mask_hbm, mask_ref), (mask_hbm, mask_vmem),
        ))
    ]
    for copy in copies:
        copy.start()
    for copy in copies:
        copy.wait()
    eye = identity()
    n_blocks = load_ref.shape[0] // WIDTH
    for block in range(n_blocks):
        load = load_ref[block * WIDTH:(block + 1) * WIDTH, :]
        weighted = (jnp.transpose(load.astype(f32)) * prec_ref[block:block + 1, :]).astype(bf16)
        weight_ref[block] = weighted
        gram = mm(weighted, load)
        gram_ref[block] = 0.5 * (gram + jnp.transpose(gram))
    base_ref[1] = eye * row_ref[0]
    base_ref[2] = jnp.transpose(base_ref[0])
    base_ref[3] = jnp.transpose(jnp.broadcast_to(row_ref[0], (WIDTH, WIDTH)))
    const_ref[0] = jnp.broadcast_to(row_ref[1], (WIDTH, WIDTH))
    const_ref[1] = base_ref[1]
    mask_out[...] = mask_vmem[...].astype(f32).astype(bf16)

    def info(step):
        out = mask_ref[0, step].astype(f32) * gram_ref[0]
        for block in range(1, n_blocks):
            out = out + mask_ref[block, step].astype(f32) * gram_ref[block]
        return out

    end_ref[...] = info(n_unit * half - 1)

    outs = (uz_ref, yv_ref, a_ref, c_ref, j_ref, p_ref)

    def leaf_joins(nodes, fast):
        trans, noise, turned, column, row = base_ref[0], base_ref[1], base_ref[2], base_ref[3], row_ref[0]
        step = [unit * half + 2 * node for node in nodes]
        start = jnp.where(step[0] == 0, 1.0, 0.0).astype(f32)
        before = [info(jnp.maximum(at - 1, 0)) for at in step]
        before[0] = before[0] * (1.0 - start)
        after = [info(at) for at in step]
        left = [trans * (1.0 - start)] + [trans] * (len(nodes) - 1)
        rows_of = [row + start * (1.0 - row)] + [row] * (len(nodes) - 1)
        mats = [eye + column * j for j in after]
        mats[0] = eye + (column + start * (1.0 - column)) * after[0]
        inverses = invert([(mat, bounds_at(JOIN_BOUNDS, 0), False) for mat in mats], eye, fast, acc_ref)
        less = [(eye - p).astype(bf16) for p in inverses]
        trans_b, turned_b = trans.astype(bf16), turned.astype(bf16)
        us = [trans - mm(trans_b, d) for d in less]
        vs = [one - mm(d, one.astype(bf16)) for one, d in zip(left, less)]
        zs = [u * r for u, r in zip(us, rows_of)]
        ts = [mm3(trans, v) for v in vs]
        ys = [mm3(j, v) for j, v in zip(after, vs)]
        cs = [noise + mm_nt(z.astype(bf16), trans_b) for z in zs]
        js = [j + mm(turned_b, y.astype(bf16)) for j, y in zip(before, ys)]
        for node, p, u, v, t, z, y, c, j in zip(nodes, inverses, us, vs, ts, zs, ys, cs, js):
            zh, zl = split(z)
            uz_ref[node, :, WIDTH:] = rows(zh, zl)
            yv_ref[node, WIDTH:, :] = pack(v)
            p_ref[node] = p
            a_ref[node] = t
            c_ref[node] = c
            j_ref[node] = j
        uh, ul = split(us[0])
        uz_ref[nodes[0], :, :WIDTH] = rows(uh, ul)
        yv_ref[nodes[0], :WIDTH, :] = pack(ys[0])

    def sweep(fast):
        count = half // 2
        group = min(count, GROUP) if fast else 1

        def some(block, carry):
            leaf_joins([block * group + k for k in range(group)], fast)
            return carry

        lax.fori_loop(0, count // group, some, 0)

    checked(sweep, acc_ref)


def invert(items, eye, fast, acc_ref, apart=False, beside=iter(())):
    if not fast:
        inverses = [safe_inverse(mat, eye) for mat, _, _ in items]
        return (inverses, [(p, None, None) for p in inverses]) if apart else inverses
    inverses, sides, worst = fast_inverses(items, eye, beside)
    acc_ref[...] = jnp.maximum(acc_ref[...], worst)
    return (inverses, [(g, e, mat) for (g, e), (mat, _, _) in zip(sides, items)]) if apart else inverses


def times_inverse(left, side):
    guess, resid, _ = side
    if resid is None:
        return mm3(left, guess)
    out = mm(lanes(*split(left)), rows(guess, guess))
    return out + mm(out.astype(bf16), resid)


def inverse_times(side, right, eye):
    guess, resid, mat = side
    if resid is None:
        return mm3(guess, right)
    resid = eye - mm(lanes(guess, guess), rows(*split(mat)))
    out = mm(lanes(guess, guess), rows(*split(right)))
    return out + mm(resid.astype(bf16), out.astype(bf16))


def checked(sweep, acc_ref, **beside):
    acc_ref[...] = jnp.zeros((8, WIDTH), f32)
    sweep(True, **beside)
    worst = jnp.sum(acc_ref[...])

    @pl.when(jnp.logical_not(worst <= RESIDUAL_MAX))
    def _():
        sweep(False)


def store_joined(outs, nodes, inverses, results):
    uz_ref, yv_ref, a_ref, c_ref, j_ref, p_ref = outs
    for node, p, (u, v, t, z, y, c, j) in zip(nodes, inverses, results):
        uh, ul = split(u)
        zh, zl = split(z)
        uz_ref[node] = rows(lanes(uh, zh), lanes(ul, zl))
        yv_ref[node] = rows(pack(y), pack(v))
        p_ref[node] = p
        a_ref[node] = t
        c_ref[node] = c
        j_ref[node] = j


def entries_of(level, half, steps, first, unit, refs, below):
    found = []
    for at_level, at in path_steps(half, steps, first):
        if at_level != level:
            continue
        node = at // (2 << level)
        if level == 0:
            eye = identity()
            start = jnp.where(unit * half + at == 0, 1.0, 0.0).astype(f32)
            c1 = below + start * (eye - below)
        else:
            c1 = below[2 * node]
        found.append(level_entry(refs, level, node, c1))
    return found


def panel_vectors(half, rows_own, unit, place, panel_in, mask_ref, weight_ref, panel_ref, all_ref, leaf_ref):
    total = panel_ref.shape[1]
    n_blocks = weight_ref.shape[0]
    n_time = panel_in.shape[0] // (2 * rows_own)
    for k in range(2 * n_time):
        core, chip, hop = (1 - unit if k % 2 else unit), place, n_time // 2
        for bit in range(1, n_time.bit_length()):
            if (k >> bit) % 2:
                chip = jnp.bitwise_xor(chip, hop)
            hop = hop // 2
        at = pl.multiple_of((2 * chip + core) * rows_own, rows_own)
        panel_ref[pl.ds(at, rows_own), :] = panel_in[k * rows_own:(k + 1) * rows_own, :]
    turned = jnp.zeros((WIDTH, total), f32)
    for block in range(n_blocks):
        mask = mask_ref[block:block + 1, :]
        turned = turned + mm(weight_ref[block], mask * panel_ref[block * WIDTH:(block + 1) * WIDTH, :])
    late = pltpu.roll(jnp.transpose(turned), 1, 0)
    all_ref[...] = late
    all_ref[0:1, :] = jnp.zeros((1, WIDTH), f32)
    leaf = all_ref[pl.ds(pl.multiple_of(unit * half, half), half), :]
    leaf_ref[...] = leaf
    return late[0:1, :], leaf


def vector_level(level, half, prior, gain_refs, leaf, bs, es):
    uz_ref, yv_ref = gain_refs
    stride = 1 << level
    zero = jnp.zeros((1, WIDTH), f32)
    for node in range(half >> (level + 1)):
        if node and node % 4 == 0:
            yield
        at = (2 * node + 1) * stride - 1
        if level == 0:
            b1, b2 = (prior if node == 0 else zero), zero
            e1, e2 = leaf[at:at + 1, :], leaf[at + 1:at + 2, :]
            if node > 0:
                high, low = split(e2)
                both = rows(high, low)
                out = mm_nt(both, uz_ref[node, :, WIDTH:])
                bs[at] = out[0:1, :WIDTH] + out[1:2, :WIDTH] + out[0:1, WIDTH:]
                out = mm(both, yv_ref[node, WIDTH:, :])
                es[at] = e1 + out[0:1, :WIDTH] + out[1:2, :WIDTH] + out[0:1, WIDTH:]
                continue
        else:
            one, two = at - stride // 2, at + stride // 2
            b1, b2, e1, e2 = bs[one], bs[two], es[one], es[two]
        high, low = split(lanes(b1, e2))
        out = mm_nt(rows(high, low), uz_ref[node])
        bs[at] = b2 + out[0:1, :WIDTH] + out[1:2, :WIDTH] + out[0:1, WIDTH:]
        high, low = split(lanes(-b1, e2))
        out = mm(rows(high, low), yv_ref[node])
        es[at] = e1 + out[0:1, :WIDTH] + out[1:2, :WIDTH] + out[0:1, WIDTH:]


def up_kernel(joins, half, steps, rows_own, index_ref, const_ref, *refs):
    unit, place = index_ref[0], index_ref[1]
    n_levels = half.bit_length() - 1
    low = joins[0]
    held = {}
    refs = list(refs)
    if rows_own:
        panel_in, mask_ref, weight_ref = refs[:3]
        refs = refs[3:]
        gain_refs, refs = refs[:2 * (low - 1)], refs[2 * (low - 1):]
        panel_ref, all_ref = refs[-2:]
        leaf_ref, b_ref, e_ref, message_ref = refs[-7:-3]
        refs = refs[:-7] + refs[-3:-2]
    if low > 1:
        below_ref = refs.pop(0)
    held[low - 1], refs = refs[:LEVEL_ARRAYS], refs[LEVEL_ARRAYS:]
    outs = {}
    for level in joins:
        held[level], refs = refs[:LEVEL_ARRAYS], refs[LEVEL_ARRAYS:]
        outs[level], refs = refs[:3], refs[3:]
    acc_ref, = refs
    eye = identity()

    def children(level, node):
        _, _, a_ref, c_ref, j_ref, _ = held[level - 1]
        return tuple((a_ref[k], c_ref[k], j_ref[k]) for k in (2 * node, 2 * node + 1))

    def condition_inputs(level):
        if level == 0:
            below = const_ref[1]
        elif level == low - 1:
            below = below_ref
        else:
            below = held[level - 1][3]
        return entries_of(level, half, steps, place * steps, unit, held[level], below)

    def store(level, results):
        for slot, result in enumerate(results):
            for ref, value in zip(outs[level], result):
                ref[slot] = value

    def sweep(fast, beside=iter(())):
        for level in joins:
            count = half >> (level + 1)
            under = level - 1
            if fast and count <= GROUP:
                nodes = list(range(count))
                entries = condition_inputs(under)
                pairs = [children(level, node) for node in nodes]
                items = [join_item(level, pair, eye) for pair in pairs]
                extra = [condition_item(under, entry, eye) for entry in entries]
                inverses = invert(items + [item for item, _ in extra], eye, True, acc_ref, beside=beside)
                results, seen = [], []
                in_turns(
                    joining(level, pairs, inverses[:count], eye, results),
                    conditioning(entries, [scale for _, scale in extra], inverses[count:], seen),
                    beside,
                )
                store_joined(held[level], nodes, inverses[:count], results)
                store(level, seen)
                continue
            group = min(count, GROUP) if fast else 1

            def some(block, carry):
                nodes = [block * group + k for k in range(group)]
                pairs = [children(level, node) for node in nodes]
                inverses = invert([join_item(level, pair, eye) for pair in pairs], eye, fast, acc_ref)
                results = []
                in_turns(joining(level, pairs, inverses, eye, results))
                store_joined(held[level], nodes, inverses, results)
                return carry

            lax.fori_loop(0, count // group, some, 0)
            entries = condition_inputs(under)
            extra = [condition_item(under, entry, eye) for entry in entries]
            inverses = invert([item for item, _ in extra], eye, fast, acc_ref)
            seen = []
            in_turns(conditioning(entries, [scale for _, scale in extra], inverses, seen))
            store(level, seen)

    if not rows_own:
        checked(sweep, acc_ref)
        return
    prior = jnp.where(unit == 0, 1.0, 0.0) * const_ref[0, 0:1, :]
    gains = [gain_refs[2 * level:2 * level + 2] for level in range(low - 1)] + [held[low - 1][:2]]
    bs, es, found = {}, {}, []

    def means():
        found.extend(panel_vectors(
            half, rows_own, unit, index_ref[3], panel_in, mask_ref, weight_ref, panel_ref, all_ref, leaf_ref
        ))
        yield
        for level in range(low):
            yield from vector_level(level, half, prior, gains[level], found[1], bs, es)
            yield

    pieces = means()
    checked(sweep, acc_ref, beside=pieces)
    for _ in pieces:
        pass
    end, leaf = found
    for level in range(low, n_levels):
        in_turns(vector_level(level, half, prior, held[level][:2], leaf, bs, es))
    for at in bs:
        b_ref[at:at + 1, :] = bs[at]
        e_ref[at:at + 1, :] = es[at]
    top = half // 2 - 1
    _, _, a_ref, c_ref, j_ref, _ = held[n_levels - 1]
    for k, ref in enumerate((a_ref, c_ref, j_ref)):
        message_ref[k * WIDTH:(k + 1) * WIDTH, :] = ref[0]
    message_ref[3 * WIDTH:, :] = rows(bs[top], es[top], end, jnp.zeros((5, WIDTH), f32))


SMEM = pl.BlockSpec(memory_space=pltpu.SMEM)
VMEM = pl.BlockSpec(memory_space=pltpu.VMEM)


ANY = pl.BlockSpec(memory_space=pl.ANY)


def level_shapes(half, level):
    count = half >> (level + 1)
    mat = (count, WIDTH, WIDTH)
    wide = (count, 2 * WIDTH, 2 * WIDTH)
    return [jax.ShapeDtypeStruct(wide, bf16)] * 2 + [jax.ShapeDtypeStruct(mat, f32)] * 4


def path_shapes(half, steps, level):
    count = len([k for k, _ in path_steps(half, steps, 0) if k == level])
    return [
        jax.ShapeDtypeStruct((count, 2 * WIDTH, 2 * WIDTH), bf16),
        jax.ShapeDtypeStruct((count, WIDTH, WIDTH), f32),
        jax.ShapeDtypeStruct((count, 3 * WIDTH, 2 * WIDTH), bf16),
    ]


def estimate(matrices):
    return pl.CostEstimate(flops=matrices * 600 * WIDTH**3, transcendentals=0, bytes_accessed=1 << 20)


def first_sweep(half, index, cell_mask, loadings, prec_rows, transition, var_row, prior_row):
    mat = (WIDTH, WIDTH)
    n_blocks = loadings.shape[0] // WIDTH
    outs = [
        jax.ShapeDtypeStruct((n_blocks,) + mat, bf16),
        jax.ShapeDtypeStruct(mat, f32),
        jax.ShapeDtypeStruct(cell_mask.shape, bf16),
        jax.ShapeDtypeStruct((2,) + mat, f32),
    ] + level_shapes(half, 0)
    inputs = [
        pltpu.with_memory_space_constraint(array, pltpu.HBM)
        for array in (cell_mask, loadings, prec_rows, transition, var_row, prior_row)
    ]
    return pl.pallas_call(
        functools.partial(first_kernel, half),
        out_shape=outs,
        in_specs=[SMEM] + [ANY] * 6,
        out_specs=[VMEM] * len(outs),
        scratch_shapes=[
            pltpu.VMEM((n_blocks,) + mat, f32),
            pltpu.VMEM((8, WIDTH), f32),
            pltpu.SMEM(cell_mask.shape, jnp.int32),
            pltpu.VMEM(cell_mask.shape, jnp.int32),
            pltpu.VMEM(loadings.shape, bf16),
            pltpu.VMEM(prec_rows.shape, f32),
            pltpu.VMEM((4,) + mat, f32),
            pltpu.VMEM((2, 1, WIDTH), f32),
            pltpu.SemaphoreType.DMA((7,)),
        ],
        compiler_params=pltpu.CompilerParams(vmem_limit_bytes=VMEM_LIMIT),
        cost_estimate=estimate(half // 2),
        name="first_sweep",
    )(index, *inputs)


def up_sweep(joins, half, steps, index, consts, held, rows_own=0, vectors=()):
    low = joins[0]
    operands = ([held[low - 2][3]] if low > 1 else []) + list(held[low - 1])
    outs = []
    for level in joins:
        outs += level_shapes(half, level) + path_shapes(half, steps, level - 1)
    scratch = [pltpu.VMEM((8, WIDTH), f32)]
    if rows_own:
        panel = vectors[0]
        operands = list(vectors) + [array for level in held[:-1] for array in level[:2]] + operands
        row = jax.ShapeDtypeStruct((half, WIDTH), f32)
        outs += [row, row, row, jax.ShapeDtypeStruct((3 * WIDTH + 8, WIDTH), f32)]
        scratch += [pltpu.VMEM((panel.shape[1], WIDTH), f32)]
        scratch = scratch[:1] + [pltpu.VMEM(panel.shape, bf16)] + scratch[1:]
    results = pl.pallas_call(
        functools.partial(up_kernel, joins, half, steps, rows_own),
        out_shape=outs,
        in_specs=[SMEM] + [VMEM] * (1 + len(operands)),
        out_specs=[VMEM] * len(outs),
        scratch_shapes=scratch,
        compiler_params=pltpu.CompilerParams(vmem_limit_bytes=VMEM_LIMIT),
        cost_estimate=estimate(sum(half >> level for level in joins)),
        name="up_sweep_%d" % low,
    )(index, consts, *operands)
    results = list(results)
    step = LEVEL_ARRAYS + 3
    parts = [results[k * step:(k + 1) * step] for k in range(len(joins))]
    return [part[:LEVEL_ARRAYS] for part in parts], [part[LEVEL_ARRAYS:] for part in parts], results[len(joins) * step:]


def down_kernel(steps, index_ref, own_ref, other_ref, end_ref, const_ref, leaf_ref, b_ref, e_ref, below_ref,
                *refs):
    refs = list(refs)
    top_refs, refs = refs[:LEVEL_ARRAYS], refs[LEVEL_ARRAYS:]
    out_ref, acc_ref, top_ref, gt_ref, cond_ref, shift_ref = refs[-6:]
    path_refs = refs[:-6]
    unit, place = index_ref[0], index_ref[1]
    half = leaf_ref.shape[0]
    n_levels = half.bit_length() - 1
    eye = identity()
    flag = jnp.where(unit == 0, 1.0, 0.0).astype(f32)

    def pick(zero, one):
        return flag * zero + (1.0 - flag) * one

    def both(first, count):
        part = slice(first, first + count)
        return own_ref[part, :], other_ref[part, :]

    own, other = both(WIDTH, WIDTH)
    cov0 = pick(own, other)
    trans1, cov1, info1 = [pick(*both(k * WIDTH, WIDTH)[::-1]) for k in range(3)]
    b0 = pick(*both(3 * WIDTH, 1))
    b1, e1 = [pick(*both(3 * WIDTH + k, 1)[::-1]) for k in range(2)]
    e_end = own_ref[3 * WIDTH + 2:3 * WIDTH + 3, :]
    end = end_ref[...]

    first = place * steps

    def roots(fast, beside=iter(())):
        under = n_levels - 1
        entries = entries_of(under, half, steps, first, unit, top_refs, below_ref)
        extra = [condition_item(under, entry, eye) for entry in entries]
        item = (eye + mm3(cov0, info1), bounds_at(JOIN_BOUNDS, n_levels), True)
        ready = mm3_nt(cov0, trans1)
        ready_end, cov1_end = mm3(ready, end), mm3(cov1, end)
        (p, *inverses), sides = invert([item] + [item for item, _ in extra], eye, fast, acc_ref, True, beside)
        u = times_inverse(trans1, sides[0])
        last = eye + cov1_end + mm3(u, ready_end)
        cov = cov1 + mm3(u, ready)
        z = mm3(u, cov0)
        kept = mm3(p, cov0)
        results = []
        work = conditioning(entries, [scale for _, scale in extra], inverses, results)
        info_z = mm3(jnp.transpose(z), end)
        _, (side,) = invert([(last, bounds_at(JOIN_BOUNDS, 0), False)], eye, fast, acc_ref, True, work)
        for _ in work:
            pass
        for slot, result in enumerate(results):
            for ref, value in zip((gt_ref, cond_ref, shift_ref), result):
                ref[slot] = value
        top_ref[0], top_ref[1] = inverse_times(side, cov, eye), inverse_times(side, z, eye)
        top_ref[2] = kept - mm3(info_z, top_ref[1])
        top_ref[3] = p

    prior = flag * const_ref[0, 0:1, :]
    path = path_steps(half, steps, first)
    levels = [(gt_ref, cond_ref, shift_ref)] + [path_refs[k:k + 3] for k in range(0, len(path_refs), 3)]
    places, seen = [], {}
    for level, _ in path:
        seen[level] = seen.get(level, -1) + 1
        places.append((levels[n_levels - 1 - level], seen[level]))

    def shift(slot):
        level, at = path[slot]
        row_of = lambda ref, k: ref[pl.ds(k, 1), :]
        if level == 0:
            one, two = jnp.where(at == 0, 1.0, 0.0) * prior, row_of(leaf_ref, at + 1)
        else:
            near = (1 << level) // 2
            one, two = row_of(b_ref, at - near), row_of(e_ref, at + near)
        high, low = split(lanes(one, two, row_of(b_ref, at)))
        arrays, own = places[slot]
        out = mm(rows(high, low), arrays[2][own])
        return out[0:1, :WIDTH] + out[1:2, :WIDTH] + out[0:1, WIDTH:]

    shifts = {}

    def shifting():
        for slot, (level, _) in enumerate(path):
            if level < n_levels - 1:
                shifts[slot] = shift(slot)
                yield

    pieces = shifting()
    checked(roots, acc_ref, beside=pieces)
    for _ in pieces:
        pass
    shifts[0] = shift(0)
    cov_top, cov_cross, cov_mid, p = [top_ref[k] for k in range(4)]
    mean_mid = mm3_nt(b0 + mm3(e1, cov0), p)
    b_end = mm3_nt(mean_mid, trans1) + b1
    news = e_end - mm3(b_end, end)
    mean_top = b_end + mm3_nt(news, cov_top)
    mean_mid = mean_mid + mm3(news, cov_cross)
    keep = 1.0 - flag
    joint = rows(
        lanes(keep * cov_mid, keep * jnp.transpose(cov_cross)),
        lanes(keep * cov_cross, pick(cov_mid, cov_top)),
    )
    means = lanes(keep * mean_mid, pick(mean_mid, mean_top))

    def nodes(slots, joints, means, leaf):
        packs = [places[slot][0][0][places[slot][1]] for slot in slots]
        conds = [places[slot][0][1][places[slot][1]] for slot in slots]
        halves = [split(joint) for joint in joints]
        crosses = [
            mm(lanes(jh, jl), rows(g[:, :WIDTH], g[:, :WIDTH])) + mm(jh, g[:, WIDTH:])
            for (jh, jl), g in zip(halves, packs)
        ]
        outs = [mm(rows(*split(mean)), g) for mean, g in zip(means, packs)]
        found = [
            shifts[slot] + out[0:1, :WIDTH] + out[1:2, :WIDTH] + out[0:1, WIDTH:] for slot, out in zip(slots, outs)
        ]
        gains = [unpack(g) for g in packs]
        if leaf:
            owns = [
                diagonal(cond, eye) + jnp.sum(gain * cross, axis=0, keepdims=True)
                for cond, gain, cross in zip(conds, gains, crosses)
            ]
        else:
            owns = [cond + mm3(jnp.transpose(gain), cross) for cond, gain, cross in zip(conds, gains, crosses)]
        return list(zip(found, owns, crosses))

    def left_pair(joint, means, mean, own, cross):
        c = cross[:WIDTH]
        return rows(lanes(joint[:WIDTH, :WIDTH], c), lanes(jnp.transpose(c), own)), lanes(means[:, :WIDTH], mean)

    def right_pair(joint, means, mean, own, cross):
        c = cross[WIDTH:]
        return rows(lanes(own, jnp.transpose(c)), lanes(c, joint[WIDTH:, WIDTH:])), lanes(mean, means[:, WIDTH:])

    slot = 0
    while path[slot][0] >= steps.bit_length() - 1:
        result, = nodes([slot], [joint], [means], False)
        go_right = jnp.where(first > path[slot][1], 1.0, 0.0).astype(f32)
        lj, lm = left_pair(joint, means, *result)
        rj, rm = right_pair(joint, means, *result)
        joint = go_right * rj + (1.0 - go_right) * lj
        means = go_right * rm + (1.0 - go_right) * lm
        slot += 1

    out_ref[steps - 1:steps, :] = means[:, WIDTH:]
    out_ref[2 * steps - 1:2 * steps, :] = diagonal(joint[WIDTH:, WIDTH:], eye)
    todo = [(0, joint, means)]
    count = steps
    while todo:
        stride, later = count // 2, []
        leaf = stride == 1
        results = nodes(
            range(slot, slot + len(todo)), [joint for _, joint, _ in todo], [means for _, _, means in todo], leaf
        )
        slot += len(todo)
        for (low, joint, means), result in zip(todo, results):
            at = low + stride - 1
            out_ref[at:at + 1, :] = result[0]
            out_ref[steps + at:steps + at + 1, :] = result[1] if leaf else diagonal(result[1], eye)
            if not leaf:
                later.append((low,) + left_pair(joint, means, *result))
                later.append((low + stride,) + right_pair(joint, means, *result))
        todo, count = later, stride


def down_sweep(steps, half, *operands):
    return pl.pallas_call(
        functools.partial(down_kernel, steps),
        out_shape=jax.ShapeDtypeStruct((2 * steps, WIDTH), f32),
        in_specs=[SMEM] + [VMEM] * (len(operands) - 1),
        out_specs=VMEM,
        scratch_shapes=[pltpu.VMEM((8, WIDTH), f32), pltpu.VMEM((6, WIDTH, WIDTH), f32)]
        + [pltpu.VMEM(shape.shape, shape.dtype) for shape in path_shapes(half, steps, half.bit_length() - 2)],
        compiler_params=pltpu.CompilerParams(vmem_limit_bytes=VMEM_LIMIT),
        name="down_sweep",
    )(*operands)


def redundant(panel_data, cell_mask, loadings, noise_prec, transition, proc_var, prior_mean):
    n_time = lax.axis_size("tm")
    n_unit = lax.axis_size("unit")
    place, unit = lax.axis_index("tm"), lax.axis_index("unit")
    total = panel_data.shape[1]
    half = total // n_unit
    steps = total // n_time
    per_half = half // steps
    index = jnp.stack([unit, place % per_half, n_unit, place]).astype(jnp.int32)
    swap = [(0, 1), (1, 0)]

    def swapped(value, other):
        return lax.ppermute(value, "tm", [(k, k ^ other) for k in range(n_time)])

    n_levels = half.bit_length() - 1
    hops = [1 << k for k in reversed(range(n_time.bit_length() - 1))]
    weighted, end, mask, consts, *level0 = first_sweep(
        half, index, cell_mask, loadings, noise_prec.reshape(-1, WIDTH), transition,
        proc_var.reshape(1, WIDTH), prior_mean.reshape(1, WIDTH),
    )
    held, paths = [level0], []
    panel = jnp.concatenate([panel_data, lax.ppermute(panel_data, "unit", swap)])
    cuts = [[1], [2], [3], list(range(4, n_levels))]
    for k, joins in enumerate(cuts):
        panel, held[-1] = lax.optimization_barrier((panel, held[-1]))
        last = k + 1 == len(cuts)
        extra = (panel_data.shape[0], (panel, mask, weighted)) if last else ()
        new, path, rest = up_sweep(joins, half, steps, index, consts, held, *extra)
        if not last:
            panel = jnp.concatenate([panel, swapped(panel, hops[k])])
        held += new
        paths += path
    leaves, bs, es, message = rest
    other = lax.ppermute(message, "unit", swap)
    mine = down_sweep(
        steps, half, index, message, other, end, consts, leaves, bs, es, held[-2][3], *held[-1],
        *[array for path in reversed(paths) for array in path],
    )
    theirs = lax.ppermute(mine, "unit", swap)
    out = jnp.where(unit == place // per_half, mine, theirs)
    return out[:steps], out[steps:]


BLOCK = 128


def carried_in(value, axis, join, neutral, backward):
    count, mine = (lax.axis_size(axis), lax.axis_index(axis))
    pieces = jax.tree.map(lambda part: lax.all_gather(part, axis), value)
    if backward:
        pieces = jax.tree.map(lambda part: part[::-1], pieces)
        mine = count - 1 - mine
    running = jax.tree.map(
        lambda part, zero: jnp.full_like(part, 0) + jnp.asarray(zero, part.dtype), value, neutral
    )

    def step(position, running):
        longer = join(running, jax.tree.map(lambda part: part[position], pieces))
        return jax.tree.map(lambda new, old: jnp.where(position < mine, new, old), longer, running)

    return lax.fori_loop(0, count - 1, step, running)


def product(left, right):
    return jnp.matmul(left, right, precision=HIGHEST)


def mat_vec(matrix, vector):
    return jnp.einsum("...kl,...l->...k", matrix, vector, precision=HIGHEST)


def flipped(matrix):
    return jnp.swapaxes(matrix, -1, -2)


def chol_apply(factor, rhs):
    middle = lax.linalg.triangular_solve(factor, rhs, left_side=True, lower=True)
    return lax.linalg.triangular_solve(factor, middle, left_side=True, lower=True, transpose_a=True)


def filter_join(earlier, later):
    trans_one, shift_one, cov_one, info_one, vec_one, live_one = earlier
    trans_two, shift_two, cov_two, info_two, vec_two, live_two = later
    identity_mat = jnp.eye(trans_one.shape[-1], dtype=jnp.float32)
    live_mat = live_one[..., None, None]
    factor_one = jnp.linalg.cholesky(cov_one + (1.0 - live_mat) * identity_mat)
    inner_mat = identity_mat + product(product(flipped(factor_one), info_two), factor_one)
    inner_factor = jnp.linalg.cholesky(inner_mat)
    solved = lax.linalg.triangular_solve(
        inner_factor, flipped(factor_one), left_side=True, lower=True
    )
    spread_mat = product(trans_two, flipped(solved))
    pushed = product(info_two, trans_one)
    reduced = product(solved, pushed)
    residue = vec_two - mat_vec(info_two, shift_one)
    solved_residue = mat_vec(solved, residue)
    trans_new = product(trans_two, trans_one) - product(spread_mat, reduced)
    shift_new = mat_vec(trans_two, shift_one) + mat_vec(spread_mat, solved_residue) + shift_two
    cov_new = product(spread_mat, flipped(spread_mat)) + cov_two
    info_new = product(flipped(trans_one), pushed) - product(flipped(reduced), reduced) + info_one
    vec_new = (
        mat_vec(flipped(trans_one), residue) - mat_vec(flipped(reduced), solved_residue) + vec_one
    )
    alive_mat = live_mat > 0.5
    alive_vec = live_one[..., None] > 0.5
    return (
        jnp.where(alive_mat, trans_new, trans_two),
        jnp.where(alive_vec, shift_new, shift_two),
        jnp.where(alive_mat, cov_new, cov_two),
        jnp.where(alive_mat, info_new, info_two),
        jnp.where(alive_vec, vec_new, vec_two),
        jnp.maximum(live_one, live_two),
    )


def smooth_join(lower_elem, higher_elem):
    gain_low, offset_low, cov_low = lower_elem
    gain_high, offset_high, cov_high = higher_elem
    return (
        product(gain_low, gain_high),
        mat_vec(gain_low, offset_high) + offset_low,
        product(product(gain_low, cov_high), flipped(gain_low)) + cov_low,
    )


def smooth_scan_join(earlier, later):
    return smooth_join(later, earlier)


def take_last(stacked):
    return stacked[-1]


def take_first(stacked):
    return stacked[0]


def per_device(panel_data, cell_mask, loadings, noise_prec, transition, proc_var, prior_mean):
    n_time = lax.axis_size("tm")
    n_unit = lax.axis_size("unit")
    time_index = lax.axis_index("tm")
    unit_index = lax.axis_index("unit")
    rows_own, total_time = panel_data.shape
    steps = total_time // n_time
    width = transition.shape[0]
    identity_mat = jnp.eye(width, dtype=jnp.float32)
    my_columns = lax.dynamic_slice_in_dim(cell_mask, time_index * steps, steps, 1)
    half_load = lax.dynamic_index_in_dim(
        loadings.reshape(n_time, n_unit, rows_own, width), unit_index, 1, keepdims=False
    ).reshape(n_time * rows_own, width)
    half_prec = lax.dynamic_index_in_dim(
        noise_prec.reshape(n_time, n_unit, rows_own), unit_index, 1, keepdims=False
    ).reshape(n_time * rows_own)
    half_ids = (
        (jnp.arange(n_time, dtype=jnp.int32)[:, None] * n_unit + unit_index) * rows_own
        + jnp.arange(rows_own, dtype=jnp.int32)[None, :]
    ).reshape(-1)
    half_weighted = (half_prec[:, None] * half_load.astype(jnp.float32)).astype(jnp.bfloat16)
    half_mask = jnp.take(my_columns, half_ids // BLOCK, axis=0).astype(jnp.bfloat16)
    regrouped = lax.all_to_all(panel_data, "tm", split_axis=1, concat_axis=0, tiled=True)
    vec_half = jnp.dot((half_mask * regrouped).T, half_weighted, preferred_element_type=jnp.float32)
    group_rows = min(rows_own, BLOCK)
    n_groups = n_time * rows_own // group_rows
    group_gram = jnp.einsum(
        "gnk,gnl->gkl",
        half_weighted.reshape(n_groups, group_rows, width),
        half_load.reshape(n_groups, group_rows, width),
        preferred_element_type=jnp.float32,
    )
    group_block = half_ids.reshape(n_groups, group_rows)[:, 0] // BLOCK
    group_mask = jnp.take(my_columns, group_block, axis=0).astype(jnp.float32)
    info_half = jnp.einsum("gt,gkl->tkl", group_mask, group_gram, precision=HIGHEST)
    info_mat, info_vec = lax.psum((info_half, vec_half), "unit")
    global_step = time_index * steps + jnp.arange(steps, dtype=jnp.int32)
    first_step = (global_step == 0).astype(jnp.float32)
    keep_step = 1.0 - first_step
    last_keep = 1.0 - (global_step == total_time - 1).astype(jnp.float32)
    inv_var = 1.0 / proc_var
    prior_prec = first_step[:, None, None] * identity_mat + keep_step[:, None, None] * jnp.diag(
        inv_var
    )
    eyes = jnp.broadcast_to(identity_mat, info_mat.shape)
    post_cov = chol_apply(jnp.linalg.cholesky(prior_prec + info_mat), eyes)
    shift_vec = jnp.einsum(
        "skl,sl->sk",
        post_cov,
        info_vec + first_step[:, None] * prior_mean[None, :],
        precision=HIGHEST,
    )
    scaled_trans = inv_var[:, None] * transition
    trans_part = keep_step[:, None, None] * jnp.einsum(
        "skl,lm->skm", post_cov, scaled_trans, precision=HIGHEST
    )
    middle = jnp.diag(inv_var)[None] - inv_var[None, :, None] * post_cov * inv_var[None, None, :]
    pressed = jnp.einsum("slm,mn->sln", middle, transition, precision=HIGHEST)
    info_part = keep_step[:, None, None] * jnp.einsum(
        "lk,sln->skn", transition, pressed, precision=HIGHEST
    )
    vec_part = keep_step[:, None] * jnp.einsum(
        "lk,sl->sk", transition, inv_var[None, :] * shift_vec, precision=HIGHEST
    )
    elements = (
        trans_part,
        shift_vec,
        post_cov,
        info_part,
        vec_part,
        jnp.ones((steps,), jnp.float32),
    )
    zero_vec = jnp.zeros((width,), jnp.float32)
    zero_mat = jnp.zeros((width, width), jnp.float32)
    filter_identity = (identity_mat, zero_vec, zero_mat, zero_mat, zero_vec, jnp.float32(0.0))
    local_joined = lax.associative_scan(filter_join, elements)
    filter_total = jax.tree.map(take_last, local_joined)
    before = carried_in(filter_total, "tm", filter_join, filter_identity, False)
    filtered = jax.vmap(filter_join, in_axes=(None, 0))(before, local_joined)
    filt_mean = filtered[1]
    filt_cov = filtered[2]
    moved_cov = jnp.einsum("kl,slm->skm", transition, filt_cov, precision=HIGHEST)
    pred_next = (
        jnp.einsum("skm,nm->skn", moved_cov, transition, precision=HIGHEST)
        + jnp.diag(proc_var)[None]
    )
    gain = (
        jnp.transpose(chol_apply(jnp.linalg.cholesky(pred_next), moved_cov), (0, 2, 1))
        * last_keep[:, None, None]
    )
    moved_mean = jnp.einsum("kl,sl->sk", transition, filt_mean, precision=HIGHEST)
    offset = filt_mean - jnp.einsum("skl,sl->sk", gain, moved_mean, precision=HIGHEST)
    resid_cov = filt_cov - jnp.einsum("skl,slm->skm", gain, moved_cov, precision=HIGHEST)
    smooth_identity = (identity_mat, zero_vec, zero_mat)
    local_suffix = lax.associative_scan(smooth_scan_join, (gain, offset, resid_cov), reverse=True)
    smooth_total = jax.tree.map(take_first, local_suffix)
    after = carried_in(smooth_total, "tm", smooth_scan_join, smooth_identity, True)
    smoothed = jax.vmap(smooth_join, in_axes=(0, None))(local_suffix, after)
    smoothed_mean = smoothed[1]
    smoothed_var = jnp.diagonal(smoothed[2], axis1=1, axis2=2)
    return (smoothed_mean, smoothed_var)


def per_device_any(*arrays):
    half = arrays[0].shape[1] // 2
    fits = lax.axis_size("unit") == 2 and half in (32, 64) and arrays[4].shape[0] == WIDTH
    return redundant(*arrays) if fits else per_device(*arrays)


def solution(mesh):
    return jax.shard_map(
        per_device_any,
        mesh=mesh,
        in_specs=(P(("grp", "tm", "unit"), None), P("grp", None), P(), P(), P(), P(), P()),
        out_specs=(P(("grp", "tm"), None), P(("grp", "tm"), None)),
        check_vma=False,
    )
```

```python
import functools

import jax
import jax.numpy as jnp
from jax import lax
from jax.experimental import pallas as pl
from jax.experimental.pallas import tpu as pltpu
from jax.sharding import PartitionSpec as P

f32 = jnp.float32
bf16 = jnp.bfloat16
WIDTH = 128
HIGHEST = lax.Precision.HIGHEST
VMEM_LIMIT = 30 << 20
RESIDUAL_MAX = 7e-3
GROUP = 16
JOIN_BOUNDS = ((1.0, 4.0), (1.0, 5.2), (1.0, 5.2), (1.0, 6.0), (1.0, 10.0), (1.0, 13.0))
COV_BOUNDS = ((0.70, 1.37), (0.50, 1.90), (0.31, 2.85), (0.19, 4.50), (0.12, 6.30))


def schedule(bounds, goal=2.5e-3):
    low, high = bounds
    alpha, radius, factors = 2.0 / (low + high), (high - low) / (high + low), []
    while radius > goal:
        square = radius * radius
        factors.append(2.0 / (2.0 - square))
        radius = square / (2.0 - square)
    return alpha, factors


def bounds_at(table, level):
    return table[min(level, len(table) - 1)]


def mm(left, right):
    return lax.dot_general(left, right, (((1,), (0,)), ((), ())), preferred_element_type=f32)


def mm_nt(left, right):
    return lax.dot_general(left, right, (((1,), (1,)), ((), ())), preferred_element_type=f32)


def split(value):
    high = value.astype(bf16)
    return high, (value - high.astype(f32)).astype(bf16)


def lanes(*parts):
    return jnp.concatenate(parts, axis=1)


def rows(*parts):
    return jnp.concatenate(parts, axis=0)


def mm3(left, right):
    lh, ll = split(left)
    rh, rl = split(right)
    return mm(lanes(lh, ll), rows(rh, rh)) + mm(lh, rl)


def mm3_nt(left, right):
    lh, ll = split(left)
    rh, rl = split(right)
    return mm_nt(lanes(lh, ll), lanes(rh, rh)) + mm_nt(lh, rl)


def identity():
    shape = (WIDTH, WIDTH)
    return (lax.broadcasted_iota(jnp.int32, shape, 0) == lax.broadcasted_iota(jnp.int32, shape, 1)).astype(f32)


def squares(value):
    return jnp.sum((value * value).reshape(WIDTH // 8, 8, WIDTH), axis=0)


def fast_inverses(items, eye, beside=iter(())):
    mats = [mat for mat, _, _ in items]
    plans = [schedule(bounds) for _, bounds, _ in items]
    n = range(len(items))
    halves = [split(mat) for mat in mats]
    rest = [eye - plan[0] * mat for plan, mat in zip(plans, mats)]
    guess = [(plan[0] * plan[1][0]) * (eye + r) for plan, r in zip(plans, rest)]
    for step in range(max(len(factors) for _, factors in plans)):
        rest_b = [r.astype(bf16) for r in rest]
        guess_b = [g.astype(bf16) for g in guess]
        for k in n:
            factors = plans[k][1]
            more = step + 1 < len(factors)
            if step >= len(factors):
                continue
            factor = factors[step]
            if step == 0:
                if more:
                    rest[k] = (1.0 - factor) * eye + factor * mm(rest_b[k], rest_b[k])
            elif more:
                out = mm(rest_b[k], lanes(guess_b[k], rest_b[k]))
                guess[k] = factor * (guess[k] + out[:, :WIDTH])
                rest[k] = (1.0 - factor) * eye + factor * out[:, WIDTH:]
            else:
                guess[k] = factor * (guess[k] + mm(rest_b[k], guess_b[k]))
        next(beside, None)
    guess_b = [g.astype(bf16) for g in guess]
    resid = [eye - mm(lanes(h, l), rows(g, g)) for (h, l), g in zip(halves, guess_b)]
    guess = [g.astype(f32) + mm(g, e.astype(bf16)) for g, e in zip(guess_b, resid)]
    next(beside, None)
    sides = [(g, e.astype(bf16)) for g, e in zip(guess_b, resid)]
    again = [k for k in n if items[k][2]]
    fine = {k: eye - mm3(mats[k], guess[k]) for k in again}
    for k in again:
        resid[k] = fine[k]
        guess[k] = guess[k] + mm(guess[k].astype(bf16), fine[k].astype(bf16))
        sides[k] = (guess[k], None)
    sizes = [jnp.sum(squares(e), keepdims=True) for e in resid]
    sizes = [jnp.where(size < 1e6, size, 1e6) for size in sizes]
    worst = sizes[0]
    for size in sizes[1:]:
        worst = jnp.maximum(worst, size)
    return guess, sides, worst


def safe_inverse(mat, eye):
    size = jnp.max(jnp.sum(jnp.abs(mat), axis=0, keepdims=True), axis=1, keepdims=True)
    product = functools.partial(jnp.dot, precision=HIGHEST, preferred_element_type=f32)

    def unfinished(state):
        step, size, _ = state
        return jnp.logical_and(step < 64, jnp.logical_not(size <= 1e-7))

    def improve(state):
        step, _, guess = state
        resid = eye - product(mat, guess)
        return step + 1, jnp.sum(squares(resid)), guess + product(guess, resid)

    return lax.while_loop(unfinished, improve, (0, f32(jnp.inf), eye / size))[2]


def diagonal(mat, eye):
    return jnp.sum(mat * eye, axis=0, keepdims=True)


def scaled(mat, eye):
    row = 1.0 / diagonal(mat, eye)
    return mat * row, row


def pack(value):
    return lanes(*split(value))


def unpack(value):
    return value[:, :WIDTH].astype(f32) + value[:, WIDTH:].astype(f32)


def path_steps(half, steps, first):
    found = []
    for level in reversed(range(half.bit_length() - 1)):
        stride = 1 << level
        if 2 * stride > steps:
            found.append((level, (first // (2 * stride)) * (2 * stride) + stride - 1))
        else:
            found += [(level, first + (2 * k + 1) * stride - 1) for k in range(steps // (2 * stride))]
    return found


def join_item(level, pair, eye):
    (_, c1, _), (_, _, j2) = pair
    return eye + mm3(c1, j2), bounds_at(JOIN_BOUNDS, level), False


def in_turns(*works):
    works = list(works)
    while works:
        for work in tuple(works):
            if next(work, works) is works:
                works.remove(work)


def joining(level, pairs, inverses, eye, results):
    turned = [jnp.transpose(one[0]) for one, two in pairs]
    if level < 2:
        less = [(eye - p).astype(bf16) for p in inverses]
        us = [two[0] - mm(two[0].astype(bf16), d) for (one, two), d in zip(pairs, less)]
        vs = [one[0] - mm(d, one[0].astype(bf16)) for (one, two), d in zip(pairs, less)]
    else:
        us = [mm3(two[0], p) for (one, two), p in zip(pairs, inverses)]
        vs = [mm3(p, one[0]) for (one, two), p in zip(pairs, inverses)]
    yield
    zs = [mm3(u, one[1]) for u, (one, two) in zip(us, pairs)]
    ys = [mm3(two[2], v) for v, (one, two) in zip(vs, pairs)]
    yield
    ts = [mm3(two[0], v) for v, (one, two) in zip(vs, pairs)]
    few = level < 2
    cs = [
        two[1] + (mm_nt(z.astype(bf16), two[0].astype(bf16)) if few else mm3_nt(z, two[0]))
        for z, (one, two) in zip(zs, pairs)
    ]
    yield
    js = [one[2] + (mm(t.astype(bf16), y.astype(bf16)) if few else mm3(t, y)) for t, y, (one, two) in zip(turned, ys, pairs)]
    results += list(zip(us, vs, ts, zs, ys, cs, js))


def condition_item(level, entry, eye):
    mat, scale = scaled(entry["c"], eye)
    return (mat, bounds_at(COV_BOUNDS, level), level > 3), scale


def conditioning(entries, scales, inverses, results):
    zs, vs = [e["z"] for e in entries], [e["v"] for e in entries]
    kepts = [mm3(e["p"], e["c1"]) for e in entries]
    backs = [mm3(jnp.transpose(inverse) * scale, z) for inverse, scale, z in zip(inverses, scales, zs)]
    yield
    forths = [jnp.transpose(back) for back in backs]
    gains = [v - mm3(forth, e["a"]) for v, forth, e in zip(vs, forths, entries)]
    yield
    conds = [kept - mm3(forth, z) for kept, forth, z in zip(kepts, forths, zs)]
    yield
    results += [
        (
            pack(rows(jnp.transpose(gain), back)),
            cond,
            pack(rows(jnp.transpose(e["p"]), jnp.transpose(kept), -back)),
        )
        for e, gain, back, cond, kept in zip(entries, gains, backs, conds, kepts)
    ]


def level_entry(refs, level, node, c1):
    uz_ref, yv_ref, a_ref, c_ref, _, p_ref = refs
    uz = uz_ref[node]
    return dict(
        z=uz[:WIDTH, WIDTH:].astype(f32) + uz[WIDTH:, WIDTH:].astype(f32),
        v=unpack(yv_ref[node, WIDTH:, :]),
        a=a_ref[node],
        c=c_ref[node],
        p=p_ref[node],
        c1=c1,
    )


LEVEL_ARRAYS = 6


def first_kernel(half, index_ref, mask_hbm, load_hbm, prec_hbm, trans_hbm, var_hbm, prior_hbm,
                 weight_ref, end_ref, mask_out, const_ref, uz_ref, yv_ref, a_ref, c_ref, j_ref, p_ref,
                 gram_ref, acc_ref, mask_ref, mask_vmem, load_ref, prec_ref, base_ref, row_ref, sems):
    unit, n_unit = index_ref[0], index_ref[2]
    copies = [
        pltpu.make_async_copy(source, target, sems.at[k])
        for k, (source, target) in enumerate((
            (load_hbm, load_ref), (prec_hbm, prec_ref), (trans_hbm, base_ref.at[0]), (var_hbm, row_ref.at[0]),
            (prior_hbm, row_ref.at[1]), (mask_hbm, mask_ref), (mask_hbm, mask_vmem),
        ))
    ]
    for copy in copies:
        copy.start()
    for copy in copies:
        copy.wait()
    eye = identity()
    n_blocks = load_ref.shape[0] // WIDTH
    for block in range(n_blocks):
        load = load_ref[block * WIDTH:(block + 1) * WIDTH, :]
        weighted = (jnp.transpose(load.astype(f32)) * prec_ref[block:block + 1, :]).astype(bf16)
        weight_ref[block] = weighted
        gram = mm(weighted, load)
        gram_ref[block] = 0.5 * (gram + jnp.transpose(gram))
    base_ref[1] = eye * row_ref[0]
    base_ref[2] = jnp.transpose(base_ref[0])
    base_ref[3] = jnp.transpose(jnp.broadcast_to(row_ref[0], (WIDTH, WIDTH)))
    const_ref[0] = jnp.broadcast_to(row_ref[1], (WIDTH, WIDTH))
    const_ref[1] = base_ref[1]
    mask_out[...] = mask_vmem[...].astype(f32).astype(bf16)

    def info(step):
        out = mask_ref[0, step].astype(f32) * gram_ref[0]
        for block in range(1, n_blocks):
            out = out + mask_ref[block, step].astype(f32) * gram_ref[block]
        return out

    end_ref[...] = info(n_unit * half - 1)

    outs = (uz_ref, yv_ref, a_ref, c_ref, j_ref, p_ref)

    def leaf_joins(nodes, fast):
        trans, noise, turned, column, row = base_ref[0], base_ref[1], base_ref[2], base_ref[3], row_ref[0]
        step = [unit * half + 2 * node for node in nodes]
        start = jnp.where(step[0] == 0, 1.0, 0.0).astype(f32)
        before = [info(jnp.maximum(at - 1, 0)) for at in step]
        before[0] = before[0] * (1.0 - start)
        after = [info(at) for at in step]
        left = [trans * (1.0 - start)] + [trans] * (len(nodes) - 1)
        rows_of = [row + start * (1.0 - row)] + [row] * (len(nodes) - 1)
        mats = [eye + column * j for j in after]
        mats[0] = eye + (column + start * (1.0 - column)) * after[0]
        inverses = invert([(mat, bounds_at(JOIN_BOUNDS, 0), False) for mat in mats], eye, fast, acc_ref)
        less = [(eye - p).astype(bf16) for p in inverses]
        trans_b, turned_b = trans.astype(bf16), turned.astype(bf16)
        us = [trans - mm(trans_b, d) for d in less]
        vs = [one - mm(d, one.astype(bf16)) for one, d in zip(left, less)]
        zs = [u * r for u, r in zip(us, rows_of)]
        ts = [mm3(trans, v) for v in vs]
        ys = [mm3(j, v) for j, v in zip(after, vs)]
        cs = [noise + mm_nt(z.astype(bf16), trans_b) for z in zs]
        js = [j + mm(turned_b, y.astype(bf16)) for j, y in zip(before, ys)]
        for node, p, u, v, t, z, y, c, j in zip(nodes, inverses, us, vs, ts, zs, ys, cs, js):
            zh, zl = split(z)
            uz_ref[node, :, WIDTH:] = rows(zh, zl)
            yv_ref[node, WIDTH:, :] = pack(v)
            p_ref[node] = p
            a_ref[node] = t
            c_ref[node] = c
            j_ref[node] = j
        uh, ul = split(us[0])
        uz_ref[nodes[0], :, :WIDTH] = rows(uh, ul)
        yv_ref[nodes[0], :WIDTH, :] = pack(ys[0])

    def sweep(fast):
        count = half // 2
        group = min(count, GROUP) if fast else 1

        def some(block, carry):
            leaf_joins([block * group + k for k in range(group)], fast)
            return carry

        lax.fori_loop(0, count // group, some, 0)

    checked(sweep, acc_ref)


def invert(items, eye, fast, acc_ref, apart=False, beside=iter(())):
    if not fast:
        inverses = [safe_inverse(mat, eye) for mat, _, _ in items]
        return (inverses, [(p, None, None) for p in inverses]) if apart else inverses
    inverses, sides, worst = fast_inverses(items, eye, beside)
    acc_ref[...] = jnp.maximum(acc_ref[...], worst)
    return (inverses, [(g, e, mat) for (g, e), (mat, _, _) in zip(sides, items)]) if apart else inverses


def times_inverse(left, side):
    guess, resid, _ = side
    if resid is None:
        return mm3(left, guess)
    out = mm(lanes(*split(left)), rows(guess, guess))
    return out + mm(out.astype(bf16), resid)


def inverse_times(side, right, eye):
    guess, resid, mat = side
    if resid is None:
        return mm3(guess, right)
    resid = eye - mm(lanes(guess, guess), rows(*split(mat)))
    out = mm(lanes(guess, guess), rows(*split(right)))
    return out + mm(resid.astype(bf16), out.astype(bf16))


def checked(sweep, acc_ref, **beside):
    acc_ref[...] = jnp.zeros((8, WIDTH), f32)
    sweep(True, **beside)
    worst = jnp.max(acc_ref[...])

    @pl.when(jnp.logical_not(worst <= RESIDUAL_MAX))
    def _():
        sweep(False)


def store_joined(outs, nodes, inverses, results):
    uz_ref, yv_ref, a_ref, c_ref, j_ref, p_ref = outs
    for node, p, (u, v, t, z, y, c, j) in zip(nodes, inverses, results):
        uh, ul = split(u)
        zh, zl = split(z)
        uz_ref[node] = rows(lanes(uh, zh), lanes(ul, zl))
        yv_ref[node] = rows(pack(y), pack(v))
        p_ref[node] = p
        a_ref[node] = t
        c_ref[node] = c
        j_ref[node] = j


def entries_of(level, half, steps, first, unit, refs, below):
    found = []
    for at_level, at in path_steps(half, steps, first):
        if at_level != level:
            continue
        node = at // (2 << level)
        if level == 0:
            eye = identity()
            start = jnp.where(unit * half + at == 0, 1.0, 0.0).astype(f32)
            c1 = below + start * (eye - below)
        else:
            c1 = below[2 * node]
        found.append(level_entry(refs, level, node, c1))
    return found


def panel_vectors(half, rows_own, unit, place, panel_in, mask_ref, weight_ref, panel_ref, all_ref, leaf_ref):
    total = panel_ref.shape[1]
    n_blocks = weight_ref.shape[0]
    n_time = panel_in.shape[0] // (2 * rows_own)
    for k in range(2 * n_time):
        core, chip, hop = (1 - unit if k % 2 else unit), place, n_time // 2
        for bit in range(1, n_time.bit_length()):
            if (k >> bit) % 2:
                chip = jnp.bitwise_xor(chip, hop)
            hop = hop // 2
        at = pl.multiple_of((2 * chip + core) * rows_own, rows_own)
        panel_ref[pl.ds(at, rows_own), :] = panel_in[k * rows_own:(k + 1) * rows_own, :]
    turned = jnp.zeros((WIDTH, total), f32)
    for block in range(n_blocks):
        mask = mask_ref[block:block + 1, :]
        turned = turned + mm(weight_ref[block], mask * panel_ref[block * WIDTH:(block + 1) * WIDTH, :])
    late = pltpu.roll(jnp.transpose(turned), 1, 0)
    all_ref[...] = late
    all_ref[0:1, :] = jnp.zeros((1, WIDTH), f32)
    leaf = all_ref[pl.ds(pl.multiple_of(unit * half, half), half), :]
    leaf_ref[...] = leaf
    return late[0:1, :], leaf


def vector_level(level, half, prior, gain_refs, leaf, bs, es):
    uz_ref, yv_ref = gain_refs
    stride = 1 << level
    zero = jnp.zeros((1, WIDTH), f32)
    for node in range(half >> (level + 1)):
        if node and node % 4 == 0:
            yield
        at = (2 * node + 1) * stride - 1
        if level == 0:
            b1, b2 = (prior if node == 0 else zero), zero
            e1, e2 = leaf[at:at + 1, :], leaf[at + 1:at + 2, :]
            if node > 0:
                high, low = split(e2)
                both = rows(high, low)
                out = mm_nt(both, uz_ref[node, :, WIDTH:])
                bs[at] = out[0:1, :WIDTH] + out[1:2, :WIDTH] + out[0:1, WIDTH:]
                out = mm(both, yv_ref[node, WIDTH:, :])
                es[at] = e1 + out[0:1, :WIDTH] + out[1:2, :WIDTH] + out[0:1, WIDTH:]
                continue
        else:
            one, two = at - stride // 2, at + stride // 2
            b1, b2, e1, e2 = bs[one], bs[two], es[one], es[two]
        high, low = split(lanes(b1, e2))
        out = mm_nt(rows(high, low), uz_ref[node])
        bs[at] = b2 + out[0:1, :WIDTH] + out[1:2, :WIDTH] + out[0:1, WIDTH:]
        high, low = split(lanes(-b1, e2))
        out = mm(rows(high, low), yv_ref[node])
        es[at] = e1 + out[0:1, :WIDTH] + out[1:2, :WIDTH] + out[0:1, WIDTH:]


def up_kernel(joins, half, steps, rows_own, index_ref, const_ref, *refs):
    unit, place = index_ref[0], index_ref[1]
    n_levels = half.bit_length() - 1
    low = joins[0]
    held = {}
    refs = list(refs)
    if rows_own:
        panel_in, mask_ref, weight_ref = refs[:3]
        refs = refs[3:]
        gain_refs, refs = refs[:2 * (low - 1)], refs[2 * (low - 1):]
        panel_ref, all_ref = refs[-2:]
        leaf_ref, b_ref, e_ref, message_ref = refs[-7:-3]
        refs = refs[:-7] + refs[-3:-2]
    if low > 1:
        below_ref = refs.pop(0)
    held[low - 1], refs = refs[:LEVEL_ARRAYS], refs[LEVEL_ARRAYS:]
    outs = {}
    for level in joins:
        held[level], refs = refs[:LEVEL_ARRAYS], refs[LEVEL_ARRAYS:]
        outs[level], refs = refs[:3], refs[3:]
    acc_ref, = refs
    eye = identity()

    def children(level, node):
        _, _, a_ref, c_ref, j_ref, _ = held[level - 1]
        return tuple((a_ref[k], c_ref[k], j_ref[k]) for k in (2 * node, 2 * node + 1))

    def condition_inputs(level):
        if level == 0:
            below = const_ref[1]
        elif level == low - 1:
            below = below_ref
        else:
            below = held[level - 1][3]
        return entries_of(level, half, steps, place * steps, unit, held[level], below)

    def store(level, results):
        for slot, result in enumerate(results):
            for ref, value in zip(outs[level], result):
                ref[slot] = value

    def sweep(fast, beside=iter(())):
        for level in joins:
            count = half >> (level + 1)
            under = level - 1
            if fast and count <= GROUP:
                nodes = list(range(count))
                entries = condition_inputs(under)
                pairs = [children(level, node) for node in nodes]
                items = [join_item(level, pair, eye) for pair in pairs]
                extra = [condition_item(under, entry, eye) for entry in entries]
                inverses = invert(items + [item for item, _ in extra], eye, True, acc_ref, beside=beside)
                results, seen = [], []
                in_turns(
                    joining(level, pairs, inverses[:count], eye, results),
                    conditioning(entries, [scale for _, scale in extra], inverses[count:], seen),
                    beside,
                )
                store_joined(held[level], nodes, inverses[:count], results)
                store(level, seen)
                continue
            group = min(count, GROUP) if fast else 1

            def some(block, carry):
                nodes = [block * group + k for k in range(group)]
                pairs = [children(level, node) for node in nodes]
                inverses = invert([join_item(level, pair, eye) for pair in pairs], eye, fast, acc_ref)
                results = []
                in_turns(joining(level, pairs, inverses, eye, results))
                store_joined(held[level], nodes, inverses, results)
                return carry

            lax.fori_loop(0, count // group, some, 0)
            entries = condition_inputs(under)
            extra = [condition_item(under, entry, eye) for entry in entries]
            inverses = invert([item for item, _ in extra], eye, fast, acc_ref)
            seen = []
            in_turns(conditioning(entries, [scale for _, scale in extra], inverses, seen))
            store(level, seen)

    if not rows_own:
        checked(sweep, acc_ref)
        return
    prior = jnp.where(unit == 0, 1.0, 0.0) * const_ref[0, 0:1, :]
    gains = [gain_refs[2 * level:2 * level + 2] for level in range(low - 1)] + [held[low - 1][:2]]
    bs, es, found = {}, {}, []

    def means():
        found.extend(panel_vectors(
            half, rows_own, unit, index_ref[3], panel_in, mask_ref, weight_ref, panel_ref, all_ref, leaf_ref
        ))
        yield
        for level in range(low):
            yield from vector_level(level, half, prior, gains[level], found[1], bs, es)
            yield

    pieces = means()
    checked(sweep, acc_ref, beside=pieces)
    for _ in pieces:
        pass
    end, leaf = found
    for level in range(low, n_levels):
        in_turns(vector_level(level, half, prior, held[level][:2], leaf, bs, es))
    for at in bs:
        b_ref[at:at + 1, :] = bs[at]
        e_ref[at:at + 1, :] = es[at]
    top = half // 2 - 1
    _, _, a_ref, c_ref, j_ref, _ = held[n_levels - 1]
    for k, ref in enumerate((a_ref, c_ref, j_ref)):
        message_ref[k * WIDTH:(k + 1) * WIDTH, :] = ref[0]
    message_ref[3 * WIDTH:, :] = rows(bs[top], es[top], end, jnp.zeros((5, WIDTH), f32))


SMEM = pl.BlockSpec(memory_space=pltpu.SMEM)
VMEM = pl.BlockSpec(memory_space=pltpu.VMEM)


ANY = pl.BlockSpec(memory_space=pl.ANY)


def level_shapes(half, level):
    count = half >> (level + 1)
    mat = (count, WIDTH, WIDTH)
    wide = (count, 2 * WIDTH, 2 * WIDTH)
    return [jax.ShapeDtypeStruct(wide, bf16)] * 2 + [jax.ShapeDtypeStruct(mat, f32)] * 4


def path_shapes(half, steps, level):
    count = len([k for k, _ in path_steps(half, steps, 0) if k == level])
    return [
        jax.ShapeDtypeStruct((count, 2 * WIDTH, 2 * WIDTH), bf16),
        jax.ShapeDtypeStruct((count, WIDTH, WIDTH), f32),
        jax.ShapeDtypeStruct((count, 3 * WIDTH, 2 * WIDTH), bf16),
    ]


def estimate(matrices):
    return pl.CostEstimate(flops=matrices * 600 * WIDTH**3, transcendentals=0, bytes_accessed=1 << 20)


def first_sweep(half, index, cell_mask, loadings, prec_rows, transition, var_row, prior_row):
    mat = (WIDTH, WIDTH)
    n_blocks = loadings.shape[0] // WIDTH
    outs = [
        jax.ShapeDtypeStruct((n_blocks,) + mat, bf16),
        jax.ShapeDtypeStruct(mat, f32),
        jax.ShapeDtypeStruct(cell_mask.shape, bf16),
        jax.ShapeDtypeStruct((2,) + mat, f32),
    ] + level_shapes(half, 0)
    inputs = [
        pltpu.with_memory_space_constraint(array, pltpu.HBM)
        for array in (cell_mask, loadings, prec_rows, transition, var_row, prior_row)
    ]
    return pl.pallas_call(
        functools.partial(first_kernel, half),
        out_shape=outs,
        in_specs=[SMEM] + [ANY] * 6,
        out_specs=[VMEM] * len(outs),
        scratch_shapes=[
            pltpu.VMEM((n_blocks,) + mat, f32),
            pltpu.VMEM((8, WIDTH), f32),
            pltpu.SMEM(cell_mask.shape, jnp.int32),
            pltpu.VMEM(cell_mask.shape, jnp.int32),
            pltpu.VMEM(loadings.shape, bf16),
            pltpu.VMEM(prec_rows.shape, f32),
            pltpu.VMEM((4,) + mat, f32),
            pltpu.VMEM((2, 1, WIDTH), f32),
            pltpu.SemaphoreType.DMA((7,)),
        ],
        compiler_params=pltpu.CompilerParams(vmem_limit_bytes=VMEM_LIMIT),
        cost_estimate=estimate(half // 2),
        name="first_sweep",
    )(index, *inputs)


def up_sweep(joins, half, steps, index, consts, held, rows_own=0, vectors=()):
    low = joins[0]
    operands = ([held[low - 2][3]] if low > 1 else []) + list(held[low - 1])
    outs = []
    for level in joins:
        outs += level_shapes(half, level) + path_shapes(half, steps, level - 1)
    scratch = [pltpu.VMEM((8, WIDTH), f32)]
    if rows_own:
        panel = vectors[0]
        operands = list(vectors) + [array for level in held[:-1] for array in level[:2]] + operands
        row = jax.ShapeDtypeStruct((half, WIDTH), f32)
        outs += [row, row, row, jax.ShapeDtypeStruct((3 * WIDTH + 8, WIDTH), f32)]
        scratch += [pltpu.VMEM((panel.shape[1], WIDTH), f32)]
        scratch = scratch[:1] + [pltpu.VMEM(panel.shape, bf16)] + scratch[1:]
    results = pl.pallas_call(
        functools.partial(up_kernel, joins, half, steps, rows_own),
        out_shape=outs,
        in_specs=[SMEM] + [VMEM] * (1 + len(operands)),
        out_specs=[VMEM] * len(outs),
        scratch_shapes=scratch,
        compiler_params=pltpu.CompilerParams(vmem_limit_bytes=VMEM_LIMIT),
        cost_estimate=estimate(sum(half >> level for level in joins)),
        name="up_sweep_%d" % low,
    )(index, consts, *operands)
    results = list(results)
    step = LEVEL_ARRAYS + 3
    parts = [results[k * step:(k + 1) * step] for k in range(len(joins))]
    return [part[:LEVEL_ARRAYS] for part in parts], [part[LEVEL_ARRAYS:] for part in parts], results[len(joins) * step:]


def down_kernel(steps, index_ref, own_ref, other_ref, end_ref, const_ref, leaf_ref, b_ref, e_ref, below_ref,
                *refs):
    refs = list(refs)
    top_refs, refs = refs[:LEVEL_ARRAYS], refs[LEVEL_ARRAYS:]
    out_ref, acc_ref, top_ref, gt_ref, cond_ref, shift_ref = refs[-6:]
    path_refs = refs[:-6]
    unit, place = index_ref[0], index_ref[1]
    half = leaf_ref.shape[0]
    n_levels = half.bit_length() - 1
    eye = identity()
    flag = jnp.where(unit == 0, 1.0, 0.0).astype(f32)

    def pick(zero, one):
        return flag * zero + (1.0 - flag) * one

    def both(first, count):
        part = slice(first, first + count)
        return own_ref[part, :], other_ref[part, :]

    own, other = both(WIDTH, WIDTH)
    cov0 = pick(own, other)
    trans1, cov1, info1 = [pick(*both(k * WIDTH, WIDTH)[::-1]) for k in range(3)]
    b0 = pick(*both(3 * WIDTH, 1))
    b1, e1 = [pick(*both(3 * WIDTH + k, 1)[::-1]) for k in range(2)]
    e_end = own_ref[3 * WIDTH + 2:3 * WIDTH + 3, :]
    end = end_ref[...]

    first = place * steps

    def roots(fast, beside=iter(())):
        under = n_levels - 1
        entries = entries_of(under, half, steps, first, unit, top_refs, below_ref)
        extra = [condition_item(under, entry, eye) for entry in entries]
        item = (eye + mm3(cov0, info1), bounds_at(JOIN_BOUNDS, n_levels), True)
        ready = mm3_nt(cov0, trans1)
        ready_end, cov1_end = mm3(ready, end), mm3(cov1, end)
        (p, *inverses), sides = invert([item] + [item for item, _ in extra], eye, fast, acc_ref, True, beside)
        u = times_inverse(trans1, sides[0])
        last = eye + cov1_end + mm3(u, ready_end)
        cov = cov1 + mm3(u, ready)
        z = mm3(u, cov0)
        kept = mm3(p, cov0)
        results = []
        work = conditioning(entries, [scale for _, scale in extra], inverses, results)
        info_z = mm3(jnp.transpose(z), end)
        _, (side,) = invert([(last, bounds_at(JOIN_BOUNDS, 0), False)], eye, fast, acc_ref, True, work)
        for _ in work:
            pass
        for slot, result in enumerate(results):
            for ref, value in zip((gt_ref, cond_ref, shift_ref), result):
                ref[slot] = value
        top_ref[0], top_ref[1] = inverse_times(side, cov, eye), inverse_times(side, z, eye)
        top_ref[2] = kept - mm3(info_z, top_ref[1])
        top_ref[3] = p

    prior = flag * const_ref[0, 0:1, :]
    path = path_steps(half, steps, first)
    levels = [(gt_ref, cond_ref, shift_ref)] + [path_refs[k:k + 3] for k in range(0, len(path_refs), 3)]
    places, seen = [], {}
    for level, _ in path:
        seen[level] = seen.get(level, -1) + 1
        places.append((levels[n_levels - 1 - level], seen[level]))

    def shift(slot):
        level, at = path[slot]
        row_of = lambda ref, k: ref[pl.ds(k, 1), :]
        if level == 0:
            one, two = jnp.where(at == 0, 1.0, 0.0) * prior, row_of(leaf_ref, at + 1)
        else:
            near = (1 << level) // 2
            one, two = row_of(b_ref, at - near), row_of(e_ref, at + near)
        high, low = split(lanes(one, two, row_of(b_ref, at)))
        arrays, own = places[slot]
        out = mm(rows(high, low), arrays[2][own])
        return out[0:1, :WIDTH] + out[1:2, :WIDTH] + out[0:1, WIDTH:]

    shifts = {}

    def shifting():
        for slot, (level, _) in enumerate(path):
            if level < n_levels - 1:
                shifts[slot] = shift(slot)
                yield

    pieces = shifting()
    checked(roots, acc_ref, beside=pieces)
    for _ in pieces:
        pass
    shifts[0] = shift(0)
    cov_top, cov_cross, cov_mid, p = [top_ref[k] for k in range(4)]
    mean_mid = mm3_nt(b0 + mm3(e1, cov0), p)
    b_end = mm3_nt(mean_mid, trans1) + b1
    news = e_end - mm3(b_end, end)
    mean_top = b_end + mm3_nt(news, cov_top)
    mean_mid = mean_mid + mm3(news, cov_cross)
    keep = 1.0 - flag
    joint = rows(
        lanes(keep * cov_mid, keep * jnp.transpose(cov_cross)),
        lanes(keep * cov_cross, pick(cov_mid, cov_top)),
    )
    means = lanes(keep * mean_mid, pick(mean_mid, mean_top))

    def nodes(slots, joints, means, leaf):
        packs = [places[slot][0][0][places[slot][1]] for slot in slots]
        conds = [places[slot][0][1][places[slot][1]] for slot in slots]
        halves = [split(joint) for joint in joints]
        crosses = [
            mm(lanes(jh, jl), rows(g[:, :WIDTH], g[:, :WIDTH])) + mm(jh, g[:, WIDTH:])
            for (jh, jl), g in zip(halves, packs)
        ]
        outs = [mm(rows(*split(mean)), g) for mean, g in zip(means, packs)]
        found = [
            shifts[slot] + out[0:1, :WIDTH] + out[1:2, :WIDTH] + out[0:1, WIDTH:] for slot, out in zip(slots, outs)
        ]
        gains = [unpack(g) for g in packs]
        if leaf:
            owns = [
                diagonal(cond, eye) + jnp.sum(gain * cross, axis=0, keepdims=True)
                for cond, gain, cross in zip(conds, gains, crosses)
            ]
        else:
            owns = [cond + mm3(jnp.transpose(gain), cross) for cond, gain, cross in zip(conds, gains, crosses)]
        return list(zip(found, owns, crosses))

    def left_pair(joint, means, mean, own, cross):
        c = cross[:WIDTH]
        return rows(lanes(joint[:WIDTH, :WIDTH], c), lanes(jnp.transpose(c), own)), lanes(means[:, :WIDTH], mean)

    def right_pair(joint, means, mean, own, cross):
        c = cross[WIDTH:]
        return rows(lanes(own, jnp.transpose(c)), lanes(c, joint[WIDTH:, WIDTH:])), lanes(mean, means[:, WIDTH:])

    slot = 0
    while path[slot][0] >= steps.bit_length() - 1:
        result, = nodes([slot], [joint], [means], False)
        go_right = jnp.where(first > path[slot][1], 1.0, 0.0).astype(f32)
        lj, lm = left_pair(joint, means, *result)
        rj, rm = right_pair(joint, means, *result)
        joint = go_right * rj + (1.0 - go_right) * lj
        means = go_right * rm + (1.0 - go_right) * lm
        slot += 1

    out_ref[steps - 1:steps, :] = means[:, WIDTH:]
    out_ref[2 * steps - 1:2 * steps, :] = diagonal(joint[WIDTH:, WIDTH:], eye)
    todo = [(0, joint, means)]
    count = steps
    while todo:
        stride, later = count // 2, []
        leaf = stride == 1
        results = nodes(
            range(slot, slot + len(todo)), [joint for _, joint, _ in todo], [means for _, _, means in todo], leaf
        )
        slot += len(todo)
        for (low, joint, means), result in zip(todo, results):
            at = low + stride - 1
            out_ref[at:at + 1, :] = result[0]
            out_ref[steps + at:steps + at + 1, :] = result[1] if leaf else diagonal(result[1], eye)
            if not leaf:
                later.append((low,) + left_pair(joint, means, *result))
                later.append((low + stride,) + right_pair(joint, means, *result))
        todo, count = later, stride


def down_sweep(steps, half, *operands):
    return pl.pallas_call(
        functools.partial(down_kernel, steps),
        out_shape=jax.ShapeDtypeStruct((2 * steps, WIDTH), f32),
        in_specs=[SMEM] + [VMEM] * (len(operands) - 1),
        out_specs=VMEM,
        scratch_shapes=[pltpu.VMEM((8, WIDTH), f32), pltpu.VMEM((6, WIDTH, WIDTH), f32)]
        + [pltpu.VMEM(shape.shape, shape.dtype) for shape in path_shapes(half, steps, half.bit_length() - 2)],
        compiler_params=pltpu.CompilerParams(vmem_limit_bytes=VMEM_LIMIT),
        name="down_sweep",
    )(*operands)


def redundant(panel_data, cell_mask, loadings, noise_prec, transition, proc_var, prior_mean):
    n_time = lax.axis_size("tm")
    n_unit = lax.axis_size("unit")
    place, unit = lax.axis_index("tm"), lax.axis_index("unit")
    total = panel_data.shape[1]
    half = total // n_unit
    steps = total // n_time
    per_half = half // steps
    index = jnp.stack([unit, place % per_half, n_unit, place]).astype(jnp.int32)
    swap = [(0, 1), (1, 0)]

    def swapped(value, other):
        return lax.ppermute(value, "tm", [(k, k ^ other) for k in range(n_time)])

    n_levels = half.bit_length() - 1
    hops = [1 << k for k in reversed(range(n_time.bit_length() - 1))]
    weighted, end, mask, consts, *level0 = first_sweep(
        half, index, cell_mask, loadings, noise_prec.reshape(-1, WIDTH), transition,
        proc_var.reshape(1, WIDTH), prior_mean.reshape(1, WIDTH),
    )
    held, paths = [level0], []
    panel = jnp.concatenate([panel_data, lax.ppermute(panel_data, "unit", swap)])
    cuts = [[1], [2], [3], list(range(4, n_levels))]
    for k, joins in enumerate(cuts):
        panel, held[-1] = lax.optimization_barrier((panel, held[-1]))
        last = k + 1 == len(cuts)
        extra = (panel_data.shape[0], (panel, mask, weighted)) if last else ()
        new, path, rest = up_sweep(joins, half, steps, index, consts, held, *extra)
        if not last:
            panel = jnp.concatenate([panel, swapped(panel, hops[k])])
        held += new
        paths += path
    leaves, bs, es, message = rest
    other = lax.ppermute(message, "unit", swap)
    mine = down_sweep(
        steps, half, index, message, other, end, consts, leaves, bs, es, held[-2][3], *held[-1],
        *[array for path in reversed(paths) for array in path],
    )
    theirs = lax.ppermute(mine, "unit", swap)
    out = jnp.where(unit == place // per_half, mine, theirs)
    return out[:steps], out[steps:]


BLOCK = 128


def carried_in(value, axis, join, neutral, backward):
    count, mine = (lax.axis_size(axis), lax.axis_index(axis))
    pieces = jax.tree.map(lambda part: lax.all_gather(part, axis), value)
    if backward:
        pieces = jax.tree.map(lambda part: part[::-1], pieces)
        mine = count - 1 - mine
    running = jax.tree.map(
        lambda part, zero: jnp.full_like(part, 0) + jnp.asarray(zero, part.dtype), value, neutral
    )

    def step(position, running):
        longer = join(running, jax.tree.map(lambda part: part[position], pieces))
        return jax.tree.map(lambda new, old: jnp.where(position < mine, new, old), longer, running)

    return lax.fori_loop(0, count - 1, step, running)


def product(left, right):
    return jnp.matmul(left, right, precision=HIGHEST)


def mat_vec(matrix, vector):
    return jnp.einsum("...kl,...l->...k", matrix, vector, precision=HIGHEST)


def flipped(matrix):
    return jnp.swapaxes(matrix, -1, -2)


def chol_apply(factor, rhs):
    middle = lax.linalg.triangular_solve(factor, rhs, left_side=True, lower=True)
    return lax.linalg.triangular_solve(factor, middle, left_side=True, lower=True, transpose_a=True)


def filter_join(earlier, later):
    trans_one, shift_one, cov_one, info_one, vec_one, live_one = earlier
    trans_two, shift_two, cov_two, info_two, vec_two, live_two = later
    identity_mat = jnp.eye(trans_one.shape[-1], dtype=jnp.float32)
    live_mat = live_one[..., None, None]
    factor_one = jnp.linalg.cholesky(cov_one + (1.0 - live_mat) * identity_mat)
    inner_mat = identity_mat + product(product(flipped(factor_one), info_two), factor_one)
    inner_factor = jnp.linalg.cholesky(inner_mat)
    solved = lax.linalg.triangular_solve(
        inner_factor, flipped(factor_one), left_side=True, lower=True
    )
    spread_mat = product(trans_two, flipped(solved))
    pushed = product(info_two, trans_one)
    reduced = product(solved, pushed)
    residue = vec_two - mat_vec(info_two, shift_one)
    solved_residue = mat_vec(solved, residue)
    trans_new = product(trans_two, trans_one) - product(spread_mat, reduced)
    shift_new = mat_vec(trans_two, shift_one) + mat_vec(spread_mat, solved_residue) + shift_two
    cov_new = product(spread_mat, flipped(spread_mat)) + cov_two
    info_new = product(flipped(trans_one), pushed) - product(flipped(reduced), reduced) + info_one
    vec_new = (
        mat_vec(flipped(trans_one), residue) - mat_vec(flipped(reduced), solved_residue) + vec_one
    )
    alive_mat = live_mat > 0.5
    alive_vec = live_one[..., None] > 0.5
    return (
        jnp.where(alive_mat, trans_new, trans_two),
        jnp.where(alive_vec, shift_new, shift_two),
        jnp.where(alive_mat, cov_new, cov_two),
        jnp.where(alive_mat, info_new, info_two),
        jnp.where(alive_vec, vec_new, vec_two),
        jnp.maximum(live_one, live_two),
    )


def smooth_join(lower_elem, higher_elem):
    gain_low, offset_low, cov_low = lower_elem
    gain_high, offset_high, cov_high = higher_elem
    return (
        product(gain_low, gain_high),
        mat_vec(gain_low, offset_high) + offset_low,
        product(product(gain_low, cov_high), flipped(gain_low)) + cov_low,
    )


def smooth_scan_join(earlier, later):
    return smooth_join(later, earlier)


def take_last(stacked):
    return stacked[-1]


def take_first(stacked):
    return stacked[0]


def per_device(panel_data, cell_mask, loadings, noise_prec, transition, proc_var, prior_mean):
    n_time = lax.axis_size("tm")
    n_unit = lax.axis_size("unit")
    time_index = lax.axis_index("tm")
    unit_index = lax.axis_index("unit")
    rows_own, total_time = panel_data.shape
    steps = total_time // n_time
    width = transition.shape[0]
    identity_mat = jnp.eye(width, dtype=jnp.float32)
    my_columns = lax.dynamic_slice_in_dim(cell_mask, time_index * steps, steps, 1)
    half_load = lax.dynamic_index_in_dim(
        loadings.reshape(n_time, n_unit, rows_own, width), unit_index, 1, keepdims=False
    ).reshape(n_time * rows_own, width)
    half_prec = lax.dynamic_index_in_dim(
        noise_prec.reshape(n_time, n_unit, rows_own), unit_index, 1, keepdims=False
    ).reshape(n_time * rows_own)
    half_ids = (
        (jnp.arange(n_time, dtype=jnp.int32)[:, None] * n_unit + unit_index) * rows_own
        + jnp.arange(rows_own, dtype=jnp.int32)[None, :]
    ).reshape(-1)
    half_weighted = (half_prec[:, None] * half_load.astype(jnp.float32)).astype(jnp.bfloat16)
    half_mask = jnp.take(my_columns, half_ids // BLOCK, axis=0).astype(jnp.bfloat16)
    regrouped = lax.all_to_all(panel_data, "tm", split_axis=1, concat_axis=0, tiled=True)
    vec_half = jnp.dot((half_mask * regrouped).T, half_weighted, preferred_element_type=jnp.float32)
    group_rows = min(rows_own, BLOCK)
    n_groups = n_time * rows_own // group_rows
    group_gram = jnp.einsum(
        "gnk,gnl->gkl",
        half_weighted.reshape(n_groups, group_rows, width),
        half_load.reshape(n_groups, group_rows, width),
        preferred_element_type=jnp.float32,
    )
    group_block = half_ids.reshape(n_groups, group_rows)[:, 0] // BLOCK
    group_mask = jnp.take(my_columns, group_block, axis=0).astype(jnp.float32)
    info_half = jnp.einsum("gt,gkl->tkl", group_mask, group_gram, precision=HIGHEST)
    info_mat, info_vec = lax.psum((info_half, vec_half), "unit")
    global_step = time_index * steps + jnp.arange(steps, dtype=jnp.int32)
    first_step = (global_step == 0).astype(jnp.float32)
    keep_step = 1.0 - first_step
    last_keep = 1.0 - (global_step == total_time - 1).astype(jnp.float32)
    inv_var = 1.0 / proc_var
    prior_prec = first_step[:, None, None] * identity_mat + keep_step[:, None, None] * jnp.diag(
        inv_var
    )
    eyes = jnp.broadcast_to(identity_mat, info_mat.shape)
    post_cov = chol_apply(jnp.linalg.cholesky(prior_prec + info_mat), eyes)
    shift_vec = jnp.einsum(
        "skl,sl->sk",
        post_cov,
        info_vec + first_step[:, None] * prior_mean[None, :],
        precision=HIGHEST,
    )
    scaled_trans = inv_var[:, None] * transition
    trans_part = keep_step[:, None, None] * jnp.einsum(
        "skl,lm->skm", post_cov, scaled_trans, precision=HIGHEST
    )
    middle = jnp.diag(inv_var)[None] - inv_var[None, :, None] * post_cov * inv_var[None, None, :]
    pressed = jnp.einsum("slm,mn->sln", middle, transition, precision=HIGHEST)
    info_part = keep_step[:, None, None] * jnp.einsum(
        "lk,sln->skn", transition, pressed, precision=HIGHEST
    )
    vec_part = keep_step[:, None] * jnp.einsum(
        "lk,sl->sk", transition, inv_var[None, :] * shift_vec, precision=HIGHEST
    )
    elements = (
        trans_part,
        shift_vec,
        post_cov,
        info_part,
        vec_part,
        jnp.ones((steps,), jnp.float32),
    )
    zero_vec = jnp.zeros((width,), jnp.float32)
    zero_mat = jnp.zeros((width, width), jnp.float32)
    filter_identity = (identity_mat, zero_vec, zero_mat, zero_mat, zero_vec, jnp.float32(0.0))
    local_joined = lax.associative_scan(filter_join, elements)
    filter_total = jax.tree.map(take_last, local_joined)
    before = carried_in(filter_total, "tm", filter_join, filter_identity, False)
    filtered = jax.vmap(filter_join, in_axes=(None, 0))(before, local_joined)
    filt_mean = filtered[1]
    filt_cov = filtered[2]
    moved_cov = jnp.einsum("kl,slm->skm", transition, filt_cov, precision=HIGHEST)
    pred_next = (
        jnp.einsum("skm,nm->skn", moved_cov, transition, precision=HIGHEST)
        + jnp.diag(proc_var)[None]
    )
    gain = (
        jnp.transpose(chol_apply(jnp.linalg.cholesky(pred_next), moved_cov), (0, 2, 1))
        * last_keep[:, None, None]
    )
    moved_mean = jnp.einsum("kl,sl->sk", transition, filt_mean, precision=HIGHEST)
    offset = filt_mean - jnp.einsum("skl,sl->sk", gain, moved_mean, precision=HIGHEST)
    resid_cov = filt_cov - jnp.einsum("skl,slm->skm", gain, moved_cov, precision=HIGHEST)
    smooth_identity = (identity_mat, zero_vec, zero_mat)
    local_suffix = lax.associative_scan(smooth_scan_join, (gain, offset, resid_cov), reverse=True)
    smooth_total = jax.tree.map(take_first, local_suffix)
    after = carried_in(smooth_total, "tm", smooth_scan_join, smooth_identity, True)
    smoothed = jax.vmap(smooth_join, in_axes=(0, None))(local_suffix, after)
    smoothed_mean = smoothed[1]
    smoothed_var = jnp.diagonal(smoothed[2], axis1=1, axis2=2)
    return (smoothed_mean, smoothed_var)


def per_device_any(*arrays):
    half = arrays[0].shape[1] // 2
    fits = lax.axis_size("unit") == 2 and half in (32, 64) and arrays[4].shape[0] == WIDTH
    return redundant(*arrays) if fits else per_device(*arrays)


def solution(mesh):
    return jax.shard_map(
        per_device_any,
        mesh=mesh,
        in_specs=(P(("grp", "tm", "unit"), None), P("grp", None), P(), P(), P(), P(), P()),
        out_specs=(P(("grp", "tm"), None), P(("grp", "tm"), None)),
        check_vma=False,
    )
```
